128 devices in a mesh: ctx: 64 (over z, x, y), wsh: 2 (over core).
Axes of the slice: x: 4, y: 4, z: 4, core: 2. Of those that a mesh axis runs over, the one named last changes fastest.
Arguments:
- block_input: bfloat16 [2, 8192, 640], P('wsh', 'ctx'), may hold values from -6 to 6
- cotangent: float32 [2, 8192, 640], P('wsh', 'ctx'), may hold values from -6 to 6
- pair_blocks: int32 [64, 2], replicated, may hold values from 0 to 127, as said below
- w_query: bfloat16 [640, 1024], P(None, 'wsh'), may hold values from -0.25 to 0.25
- w_key: bfloat16 [640, 256], P(None, 'wsh'), may hold values from -0.25 to 0.25
- w_value: bfloat16 [640, 256], P(None, 'wsh'), may hold values from -0.25 to 0.25
- w_out: bfloat16 [1024, 640], P('wsh'), may hold values from -0.1875 to 0.1875
- w_gate: bfloat16 [640, 2048], P(None, 'wsh'), may hold values from -0.25 to 0.25
- w_up: bfloat16 [640, 2048], P(None, 'wsh'), may hold values from -0.25 to 0.25
- w_down: bfloat16 [2048, 640], P('wsh'), may hold values from -0.125 to 0.125
- attn_pre_gain: bfloat16 [640], P('wsh'), may hold values from -0.3984375 to 0.59765625
- query_gain: bfloat16 [256], P('wsh'), may hold values from -0.3984375 to 0.59765625
- key_gain: bfloat16 [256], P('wsh'), may hold values from -0.3984375 to 0.59765625
- attn_post_gain: bfloat16 [640], P('wsh'), may hold values from -0.3984375 to 0.59765625
- ffw_pre_gain: bfloat16 [640], P('wsh'), may hold values from -0.3984375 to 0.59765625
- ffw_post_gain: bfloat16 [640], P('wsh'), may hold values from -0.3984375 to 0.59765625
Outputs:
- block_output: float32 [2, 8192, 640], P('wsh', 'ctx')
- input_grad: float32 [2, 8192, 640], P('wsh', 'ctx')
- w_query_grad: float32 [640, 1024], P(None, 'wsh')
- w_key_grad: float32 [640, 256], P(None, 'wsh')
- w_value_grad: float32 [640, 256], P(None, 'wsh')
- w_out_grad: float32 [1024, 640], P('wsh')
- w_gate_grad: float32 [640, 2048], P(None, 'wsh')
- w_up_grad: float32 [640, 2048], P(None, 'wsh')
- w_down_grad: float32 [2048, 640], P('wsh')
- attn_pre_gain_grad: float32 [640], P('wsh')
- query_gain_grad: float32 [256], P('wsh')
- key_gain_grad: float32 [256], P('wsh')
- attn_post_gain_grad: float32 [640], P('wsh')
- ffw_pre_gain_grad: float32 [640], P('wsh')
- ffw_post_gain_grad: float32 [640], P('wsh')
The draws below stay inside these ranges and needn't reach their ends.
Inputs may be any that keep to these rules, and one draw needn't show every extreme that they name: `pair_blocks`: row r holds a block b and its mirror 2 * 64 - 1 - b, in the order in which index r of ctx stores them; over all rows every one of the 128 blocks appears exactly once.
All inputs are finite; a program needn't handle non-finite values.
Results may differ from the reference program's by a relative error of at most 0.018.
Values may be sent and summed in bfloat16 or wider, within the bound.
No kernel may reach another device: no remote copies, remote signals or barrier semaphores. Data moves between devices by JAX's collectives and lax.ppermute only.
A program may use at most 192 MiB of HBM per device.

```python
import jax
import jax.numpy as jnp
from jax import lax

D = 640
HEADS = 4
HDIM = 256
FF = 2048
TOK_DEV = 128
RANKS = 64
SEQ = 8192
SEQS = 2
N_WSH = 2


def draw_pair_blocks(key, part):
    first = jax.random.permutation(jax.random.fold_in(key, 11), RANKS).astype(jnp.int32)
    flipped = jax.random.randint(jax.random.fold_in(key, 12), (RANKS,), 0, 2).astype(jnp.int32)
    mirror = 2 * RANKS - 1 - first
    lower = jnp.where(flipped == 1, mirror, first)
    upper = jnp.where(flipped == 1, first, mirror)
    return jnp.stack([lower, upper], axis=1).astype(jnp.int32)


def block_scale(key, dims, split, smallest, largest):
    loudness = 1.0
    for dim, shards_of in split:
        steps = jax.random.uniform(jax.random.fold_in(jax.random.fold_in(key, 6), dim), (shards_of,), jnp.float32, smallest / len(split), largest / len(split))
        loudness = loudness * jnp.repeat(jnp.exp(steps), dims[dim] // shards_of).reshape((-1,) + (1,) * (len(dims) - 1 - dim))
    return loudness


def noise(own_key, shape, scale, reach, pieces=(), kind=jnp.bfloat16):
    factor_of = block_scale(own_key, shape, pieces, -0.22, 0.18) if pieces else 1.0
    entries = jax.random.normal(own_key, shape, jnp.float32) * scale * factor_of
    return jnp.minimum(jnp.maximum(entries, -reach), reach).astype(kind)


def setup_inputs(seed: int = 0) -> dict:
    key_of = jax.random.split(jax.random.key(seed), 17)
    return {
        "block_input": noise(key_of[0], (SEQS, SEQ, D), 1.0, 6.0, ((0, 2), (1, 64))),
        "cotangent": noise(key_of[1], (SEQS, SEQ, D), 1.0, 6.0, ((0, 2), (1, 64)), jnp.float32),
        "pair_blocks": draw_pair_blocks(jax.random.fold_in(key_of[16], 71), 0),
        "w_query": noise(key_of[3], (D, HEADS * HDIM), D ** -0.5, 0.25, ((1, 2),)),
        "w_key": noise(key_of[4], (D, HDIM), D ** -0.5, 0.25, ((1, 2),)),
        "w_value": noise(key_of[5], (D, HDIM), D ** -0.5, 0.25, ((1, 2),)),
        "w_out": noise(key_of[6], (HEADS * HDIM, D), (HEADS * HDIM) ** -0.5, 0.1875, ((0, 2),)),
        "w_gate": noise(key_of[7], (D, FF), D ** -0.5, 0.25, ((1, 2),)),
        "w_up": noise(key_of[8], (D, FF), D ** -0.5, 0.25, ((1, 2),)),
        "w_down": noise(key_of[9], (FF, D), FF ** -0.5, 0.125, ((0, 2),)),
        "attn_pre_gain": jnp.clip(-0.3984375 + 0.99609375 * jax.random.uniform(key_of[10], (D,), jnp.float32) ** block_scale(key_of[10], (D,), ((0, 2),), -0.2, 0.2), -0.3984375, 0.59765625).astype(jnp.bfloat16),
        "query_gain": jnp.clip(-0.3984375 + 0.99609375 * jax.random.uniform(key_of[11], (HDIM,), jnp.float32) ** block_scale(key_of[11], (HDIM,), ((0, 2),), -0.2, 0.2), -0.3984375, 0.59765625).astype(jnp.bfloat16),
        "key_gain": jnp.clip(-0.3984375 + 0.99609375 * jax.random.uniform(key_of[12], (HDIM,), jnp.float32) ** block_scale(key_of[12], (HDIM,), ((0, 2),), -0.2, 0.2), -0.3984375, 0.59765625).astype(jnp.bfloat16),
        "attn_post_gain": jnp.clip(-0.3984375 + 0.99609375 * jax.random.uniform(key_of[13], (D,), jnp.float32) ** block_scale(key_of[13], (D,), ((0, 2),), -0.2, 0.2), -0.3984375, 0.59765625).astype(jnp.bfloat16),
        "ffw_pre_gain": jnp.clip(-0.3984375 + 0.99609375 * jax.random.uniform(key_of[14], (D,), jnp.float32) ** block_scale(key_of[14], (D,), ((0, 2),), -0.2, 0.2), -0.3984375, 0.59765625).astype(jnp.bfloat16),
        "ffw_post_gain": jnp.clip(-0.3984375 + 0.99609375 * jax.random.uniform(key_of[15], (D,), jnp.float32) ** block_scale(key_of[15], (D,), ((0, 2),), -0.2, 0.2), -0.3984375, 0.59765625).astype(jnp.bfloat16),
    }


epsilon = 1e-06
theta_base = 1000000.0

def rounded(values):
    return lax.optimization_barrier(values.astype(jnp.bfloat16)).astype(jnp.float32)

def rms_forward(values, gain_w):
    factor = lax.rsqrt(lax.optimization_barrier(jnp.mean(values * values, axis=-1, keepdims=True)) + epsilon)
    return (values * factor * (1.0 + gain_w), factor)

def rms_backward(values, factor, gain_w, grad_out):
    weighted = grad_out * (1.0 + gain_w)
    inner = lax.optimization_barrier(jnp.mean(weighted * values, axis=-1, keepdims=True))
    grad_in = factor * (weighted - values * factor * factor * inner)
    grad_gain = lax.optimization_barrier(jnp.sum((grad_out * values * factor).reshape(-1, values.shape[-1]), axis=0))
    return (grad_in, grad_gain)

def rotary_tables(positions, width):
    half_width = width // 2
    frequency = theta_base ** (-jnp.arange(half_width, dtype=jnp.float32) * 2.0 / width)
    angles = positions.astype(jnp.float32)[:, None] * frequency[None, :]
    return (jnp.cos(angles)[:, None, :], jnp.sin(angles)[:, None, :])

def rotate(values, cos_tab, sin_tab):
    half_width = values.shape[-1] // 2
    first_half = values[..., :half_width]
    second_half = values[..., half_width:]
    return jnp.concatenate([first_half * cos_tab - second_half * sin_tab, second_half * cos_tab + first_half * sin_tab], axis=-1)

def rotate_back(grads, cos_tab, sin_tab):
    half_width = grads.shape[-1] // 2
    first_half = grads[..., :half_width]
    second_half = grads[..., half_width:]
    return jnp.concatenate([first_half * cos_tab + second_half * sin_tab, second_half * cos_tab - first_half * sin_tab], axis=-1)

def block_positions(block_ids, half_rows):
    offsets = jnp.arange(half_rows, dtype=jnp.int32)
    return (block_ids[:, None] * half_rows + offsets[None, :]).reshape(-1)

def masked_scores(query_block, key_f, pos_block, positions):
    scores = jnp.einsum('qhd,kd->hqk', query_block.astype(jnp.float32), key_f) * HDIM ** (-0.5)
    return jnp.where(positions[None, None, :] <= pos_block[None, :, None], scores, -1e+30)

def attention_forward(query_rot, key_rot, value_bf, positions, block_rows):
    count_blocks = query_rot.shape[0] // block_rows
    key_f = key_rot.astype(jnp.float32)
    value_f = value_bf.astype(jnp.float32)

    def step(carry, item):
        query_block, pos_block = item
        scores = masked_scores(query_block, key_f, pos_block, positions)
        top_score = lax.optimization_barrier(jnp.max(scores, axis=-1, keepdims=True))
        shifted = jnp.exp(scores - top_score)
        totals = lax.optimization_barrier(jnp.sum(shifted, axis=-1, keepdims=True))
        probs = shifted / totals
        log_total = top_score[..., 0] + jnp.log(totals[..., 0])
        attn_block = jnp.einsum('hqk,kd->qhd', rounded(probs), value_f)
        return (carry, (attn_block.astype(jnp.bfloat16), log_total))
    items = (query_rot.reshape(count_blocks, block_rows, HEADS, HDIM), positions.reshape(count_blocks, block_rows))
    _, (attn_blocks, log_blocks) = lax.scan(step, jnp.zeros((), jnp.float32), items)
    return (attn_blocks.reshape(-1, HEADS * HDIM), log_blocks)

def attention_backward(query_rot, key_rot, value_bf, positions, grad_attn, attn_out, log_blocks, block_rows):
    count_blocks = query_rot.shape[0] // block_rows
    key_f = key_rot.astype(jnp.float32)
    value_f = value_bf.astype(jnp.float32)
    grad_heads = grad_attn.reshape(-1, HEADS, HDIM)
    delta = lax.optimization_barrier(jnp.sum(grad_heads.astype(jnp.float32) * attn_out.reshape(-1, HEADS, HDIM).astype(jnp.float32), axis=-1))
    delta_blocks = delta.reshape(count_blocks, block_rows, HEADS).transpose(0, 2, 1)

    def step(carry, item):
        grad_key, grad_value = carry
        query_block, pos_block, grad_block, log_block, delta_block = item
        scores = masked_scores(query_block, key_f, pos_block, positions)
        probs_again = jnp.exp(scores - log_block[:, :, None])
        grad_f = grad_block.astype(jnp.float32)
        grad_probs = jnp.einsum('qhd,kd->hqk', grad_f, value_f)
        grad_scores = rounded(probs_again * (grad_probs - delta_block[:, :, None]))
        grad_query = jnp.einsum('hqk,kd->qhd', grad_scores, key_f) * HDIM ** (-0.5)
        grad_key = grad_key + jnp.einsum('hqk,qhd->kd', grad_scores, query_block.astype(jnp.float32)) * HDIM ** (-0.5)
        grad_value = grad_value + jnp.einsum('hqk,qhd->kd', rounded(probs_again), grad_f)
        return ((grad_key, grad_value), grad_query)
    zeros_kv = jnp.zeros((query_rot.shape[0], HDIM), jnp.float32)
    items = (query_rot.reshape(count_blocks, block_rows, HEADS, HDIM), positions.reshape(count_blocks, block_rows), grad_heads.reshape(count_blocks, block_rows, HEADS, HDIM), log_blocks, delta_blocks)
    (grad_key, grad_value), grad_query = lax.scan(step, (zeros_kv, zeros_kv), items)
    return (grad_query.reshape(-1, HEADS, HDIM), grad_key, grad_value)

def dot_f32(left, right):
    return jnp.dot(left, right, preferred_element_type=jnp.float32)

def reference(block_input, cotangent, pair_blocks, w_query, w_key, w_value, w_out, w_gate, w_up, w_down, attn_pre_gain, query_gain, key_gain, attn_post_gain, ffw_pre_gain, ffw_post_gain):
    half_rows = TOK_DEV // 2
    positions = block_positions(pair_blocks.reshape(-1), half_rows)
    cos_tab, sin_tab = rotary_tables(positions, HDIM)
    block_rows = min(512, SEQ)
    gain_one = attn_pre_gain.astype(jnp.float32)
    gain_query = query_gain.astype(jnp.float32)
    gain_key = key_gain.astype(jnp.float32)
    gain_two = attn_post_gain.astype(jnp.float32)
    gain_three = ffw_pre_gain.astype(jnp.float32)
    gain_four = ffw_post_gain.astype(jnp.float32)
    grad_sums = None
    outputs = []
    input_grads = []
    for seq_index in range(N_WSH):
        resid_in = block_input[seq_index].astype(jnp.float32)
        grad_top = cotangent[seq_index]
        normed_one, factor_one = rms_forward(resid_in, gain_one)
        attn_in = normed_one.astype(jnp.bfloat16)
        query_raw = dot_f32(attn_in, w_query).reshape(SEQ, HEADS, HDIM)
        key_raw = dot_f32(attn_in, w_key)[:, None, :]
        value_bf = dot_f32(attn_in, w_value).astype(jnp.bfloat16)
        query_normed, query_factor = rms_forward(query_raw, gain_query)
        key_normed, key_factor = rms_forward(key_raw, gain_key)
        query_rot = rotate(query_normed, cos_tab, sin_tab).astype(jnp.bfloat16)
        key_rot = rotate(key_normed, cos_tab, sin_tab)[:, 0, :].astype(jnp.bfloat16)
        attn_out, log_blocks = attention_forward(query_rot, key_rot, value_bf, positions, block_rows)
        attn_proj = dot_f32(attn_out, w_out)
        normed_two, factor_two = rms_forward(attn_proj, gain_two)
        mid = resid_in + normed_two
        normed_three, factor_three = rms_forward(mid, gain_three)
        ffw_in = normed_three.astype(jnp.bfloat16)
        gate = dot_f32(ffw_in, w_gate)
        up_val = dot_f32(ffw_in, w_up)
        activated, gelu_back = jax.vjp(lambda inner: jax.nn.gelu(inner, approximate=True), gate)
        hidden = (activated * up_val).astype(jnp.bfloat16)
        ffw_proj = dot_f32(hidden, w_down)
        normed_four, factor_four = rms_forward(ffw_proj, gain_four)
        outputs.append(mid + normed_four)
        grad_ffw, grad_gain_four = rms_backward(ffw_proj, factor_four, gain_four, grad_top)
        grad_ffw_bf = grad_ffw.astype(jnp.bfloat16)
        grad_w_down = dot_f32(hidden.T, grad_ffw_bf)
        grad_hidden = dot_f32(grad_ffw_bf, w_down.T)
        grad_gate = gelu_back(grad_hidden * up_val)[0].astype(jnp.bfloat16)
        grad_up = (grad_hidden * activated).astype(jnp.bfloat16)
        grad_w_gate = dot_f32(ffw_in.T, grad_gate)
        grad_w_up = dot_f32(ffw_in.T, grad_up)
        grad_ffw_in = dot_f32(grad_gate, w_gate.T) + dot_f32(grad_up, w_up.T)
        grad_mid_part, grad_gain_three = rms_backward(mid, factor_three, gain_three, grad_ffw_in)
        grad_mid = grad_top + grad_mid_part
        grad_proj, grad_gain_two = rms_backward(attn_proj, factor_two, gain_two, grad_mid)
        grad_proj_bf = grad_proj.astype(jnp.bfloat16)
        grad_w_out = dot_f32(attn_out.T, grad_proj_bf)
        grad_attn = dot_f32(grad_proj_bf, w_out.T).astype(jnp.bfloat16)
        grad_query, grad_key, grad_value = attention_backward(query_rot, key_rot, value_bf, positions, grad_attn, attn_out, log_blocks, block_rows)
        grad_query_raw, grad_gain_query = rms_backward(query_raw, query_factor, gain_query, rotate_back(grad_query, cos_tab, sin_tab))
        grad_key_raw, grad_gain_key = rms_backward(key_raw, key_factor, gain_key, rotate_back(grad_key[:, None, :], cos_tab, sin_tab))
        grad_query_bf = grad_query_raw.reshape(SEQ, HEADS * HDIM).astype(jnp.bfloat16)
        grad_key_bf = grad_key_raw[:, 0, :].astype(jnp.bfloat16)
        grad_value_bf = grad_value.astype(jnp.bfloat16)
        grad_w_query = dot_f32(attn_in.T, grad_query_bf)
        grad_w_key = dot_f32(attn_in.T, grad_key_bf)
        grad_w_value = dot_f32(attn_in.T, grad_value_bf)
        grad_attn_in = dot_f32(grad_query_bf, w_query.T) + dot_f32(grad_key_bf, w_key.T) + dot_f32(grad_value_bf, w_value.T)
        grad_in_part, grad_gain_one = rms_backward(resid_in, factor_one, gain_one, grad_attn_in)
        input_grads.append(grad_mid + grad_in_part)
        current = (grad_w_query, grad_w_key, grad_w_value, grad_w_out, grad_w_gate, grad_w_up, grad_w_down, grad_gain_one, grad_gain_query, grad_gain_key, grad_gain_two, grad_gain_three, grad_gain_four)
        if grad_sums is None:
            grad_sums = current
        else:
            grad_sums = tuple((total + extra for total, extra in zip(grad_sums, current)))
    return (jnp.stack(outputs), jnp.stack(input_grads), grad_sums[0], grad_sums[1], grad_sums[2], grad_sums[3], grad_sums[4], grad_sums[5], grad_sums[6], grad_sums[7], grad_sums[8], grad_sums[9], grad_sums[10], grad_sums[11], grad_sums[12])
```

```python
import jax
import jax.numpy as jnp
from jax import lax
from jax.sharding import Mesh
from jax.sharding import PartitionSpec as P

HEADS = 4
HDIM = 256
CTX = ("z", "x", "y")

epsilon = 1e-06
theta_base = 1000000.0
bf16 = jnp.bfloat16
f32 = jnp.float32


def rms_forward(values, gain_w):
    factor = lax.rsqrt(jnp.mean(values * values, axis=-1, keepdims=True) + epsilon)
    return (values * factor * (1.0 + gain_w), factor)


def rms_backward(values, factor, gain_w, grad_out):
    weighted = grad_out * (1.0 + gain_w)
    inner = jnp.mean(weighted * values, axis=-1, keepdims=True)
    grad_in = factor * (weighted - values * factor * factor * inner)
    grad_gain = jnp.sum((grad_out * values * factor).reshape(-1, values.shape[-1]), axis=0)
    return (grad_in, grad_gain)


def rotary_tables(positions, width):
    half_width = width // 2
    frequency = theta_base ** (-jnp.arange(half_width, dtype=f32) * 2.0 / width)
    angles = positions.astype(f32)[:, None] * frequency[None, :]
    return (jnp.cos(angles), jnp.sin(angles))


def rotate(values, cos_tab, sin_tab):
    half = values.shape[-1] // 2
    a, b = values[..., :half], values[..., half:]
    return jnp.concatenate([a * cos_tab - b * sin_tab, b * cos_tab + a * sin_tab], axis=-1)


def rotate_back(grads, cos_tab, sin_tab):
    half = grads.shape[-1] // 2
    a, b = grads[..., :half], grads[..., half:]
    return jnp.concatenate([a * cos_tab + b * sin_tab, b * cos_tab - a * sin_tab], axis=-1)


def block_positions(block_ids, half_rows):
    offsets = jnp.arange(half_rows, dtype=jnp.int32)
    return (block_ids[:, None] * half_rows + offsets[None, :]).reshape(-1)


def dot_f32(left, right):
    return jnp.dot(left, right, preferred_element_type=f32)


def dot_nt(left, right):
    return lax.dot_general(left, right, (((1,), (1,)), ((), ())), preferred_element_type=f32)


def dot_tn(left, right):
    return lax.dot_general(left, right, (((0,), (0,)), ((), ())), preferred_element_type=f32)


def swap(values):
    return lax.ppermute(values, "wsh", [(0, 1), (1, 0)])


def attention_forward(query, keys, vals, query_pos, key_pos):
    scores = dot_nt(query, keys) * HDIM ** (-0.5)
    scores = jnp.where(key_pos[None, :] <= query_pos[:, None], scores, -1e30)
    top = jnp.max(scores, axis=-1, keepdims=True)
    shifted = jnp.exp(scores - top)
    totals = jnp.sum(shifted, axis=-1, keepdims=True)
    probs = (shifted / totals).astype(bf16)
    return dot_f32(probs, vals).astype(bf16), top + jnp.log(totals)


def attention_backward(query, keys, vals, query_pos, key_pos, grads, log_total, delta):
    scores = dot_nt(query, keys) * HDIM ** (-0.5)
    scores = jnp.where(key_pos[None, :] <= query_pos[:, None], scores, -1e30)
    probs = jnp.exp(scores - log_total)
    grad_probs = dot_nt(grads, vals)
    grad_scores = (probs * (grad_probs - delta)).astype(bf16)
    grad_query = dot_f32(grad_scores, keys) * HDIM ** (-0.5)
    grad_key = dot_tn(grad_scores, query) * HDIM ** (-0.5)
    grad_value = dot_tn(probs.astype(bf16), grads)
    return grad_query, jnp.concatenate([grad_key.astype(bf16), grad_value.astype(bf16)], axis=1)


def gather_ctx(block):
    return lax.all_gather(block, CTX, axis=0, tiled=True)


def scatter_sum(parts):
    got = lax.all_to_all(parts.reshape(64, 128, -1), CTX, split_axis=0, concat_axis=0, tiled=True)
    return jnp.sum(got.astype(f32), axis=0)


def small_sum(values):
    rows = values.shape[0] // 64
    got = lax.all_to_all(values.reshape(64, rows, -1), CTX, split_axis=0, concat_axis=0, tiled=True)
    mine = jnp.sum(got.astype(f32), axis=0).astype(values.dtype)
    wide = jnp.broadcast_to(mine[None], (64,) + mine.shape)
    out = lax.all_to_all(wide, CTX, split_axis=0, concat_axis=0, tiled=True)
    return out.reshape(values.shape)


def per_device(
    block_input,
    cotangent,
    pair_blocks,
    w_query,
    w_key,
    w_value,
    w_out,
    w_gate,
    w_up,
    w_down,
    attn_pre_gain,
    query_gain,
    key_gain,
    attn_post_gain,
    ffw_pre_gain,
    ffw_post_gain,
):
    rows = block_input.shape[1]
    rank = lax.axis_index(CTX)
    first = lax.axis_index("wsh") == 0

    def ordered(own, other, axis):
        return jnp.where(
            first,
            jnp.concatenate([own, other], axis=axis),
            jnp.concatenate([other, own], axis=axis),
        )

    resid_in = block_input[0].astype(f32)
    grad_top = cotangent[0]
    query_pos = block_positions(lax.dynamic_slice_in_dim(pair_blocks, rank, 1, 0)[0], rows // 2)
    key_pos = block_positions(pair_blocks.reshape(-1), rows // 2)
    cos_tab, sin_tab = rotary_tables(query_pos, HDIM)

    gains_own = jnp.concatenate(
        [attn_pre_gain, attn_post_gain, ffw_pre_gain, ffw_post_gain, query_gain, key_gain]
    )[None]
    gains_other = swap(gains_own)
    kv_own = jnp.concatenate([w_key, w_value], axis=1)
    kv_other = swap(kv_own)

    def gain(start, width):
        return ordered(
            gains_own[0, start : start + width], gains_other[0, start : start + width], 0
        ).astype(f32)[None]

    gain_one, gain_two, gain_three, gain_four = (gain(320 * i, 320) for i in range(4))
    gain_query, gain_key = gain(1280, 128), gain(1408, 128)
    key_w = ordered(kv_own[:, :128], kv_other[:, :128], 1)
    value_w = ordered(kv_own[:, 128:], kv_other[:, 128:], 1)

    normed_one, factor_one = rms_forward(resid_in, gain_one)
    attn_in = normed_one.astype(bf16)
    key_raw = dot_f32(attn_in, key_w)
    value_bf = dot_f32(attn_in, value_w).astype(bf16)
    key_normed, key_factor = rms_forward(key_raw, gain_key)
    key_rot = rotate(key_normed, cos_tab, sin_tab).astype(bf16)
    kv_all = gather_ctx(jnp.concatenate([key_rot, value_bf], axis=1))
    key_all, value_all = kv_all[:, :HDIM], kv_all[:, HDIM:]

    query_w = (w_query, swap(w_query))
    out_w = (w_out, swap(w_out))
    gate_w = (w_gate, swap(w_gate))
    up_w = (w_up, swap(w_up))
    down_w = (w_down, swap(w_down))

    def heads_first(pair):
        return jnp.concatenate(
            [half[:, HDIM * h : HDIM * (h + 1)] for half in pair for h in range(2)], axis=0
        )

    def heads_last(stacked):
        return tuple(
            jnp.concatenate([stacked[rows * h : rows * (h + 1)] for h in (2 * p, 2 * p + 1)], axis=1)
            for p in range(2)
        )

    cos4, sin4 = jnp.tile(cos_tab, (HEADS, 1)), jnp.tile(sin_tab, (HEADS, 1))
    query_raw = heads_first(tuple(dot_f32(attn_in, half) for half in query_w))
    query_normed, query_factor = rms_forward(query_raw, gain_query)
    query_rot = rotate(query_normed, cos4, sin4).astype(bf16)
    pos4 = jnp.tile(query_pos, HEADS)
    attn_heads, log_total = attention_forward(query_rot, key_all, value_all, pos4, key_pos)
    attn_out = heads_last(attn_heads)
    attn_proj = dot_f32(attn_out[0], out_w[0]) + dot_f32(attn_out[1], out_w[1])
    normed_two, factor_two = rms_forward(attn_proj, gain_two)
    mid = resid_in + normed_two
    normed_three, factor_three = rms_forward(mid, gain_three)
    ffw_in = normed_three.astype(bf16)

    gate = [dot_f32(ffw_in, half) for half in gate_w]
    up_val = [dot_f32(ffw_in, half) for half in up_w]
    acts = [jax.vjp(lambda inner: jax.nn.gelu(inner, approximate=True), g) for g in gate]
    hidden = [(act[0] * up).astype(bf16) for act, up in zip(acts, up_val)]
    ffw_proj = dot_f32(hidden[0], down_w[0]) + dot_f32(hidden[1], down_w[1])
    normed_four, factor_four = rms_forward(ffw_proj, gain_four)
    block_output = mid + normed_four

    grad_ffw, grad_gain_four = rms_backward(ffw_proj, factor_four, gain_four, grad_top)
    grad_ffw_bf = grad_ffw.astype(bf16)
    grad_hidden = [dot_nt(grad_ffw_bf, half) for half in down_w]
    grad_gate = [
        act[1](gh * up)[0].astype(bf16) for act, gh, up in zip(acts, grad_hidden, up_val)
    ]
    grad_up = [(gh * act[0]).astype(bf16) for act, gh in zip(acts, grad_hidden)]
    grad_ffw_in = (
        dot_nt(grad_gate[0], gate_w[0])
        + dot_nt(grad_gate[1], gate_w[1])
        + dot_nt(grad_up[0], up_w[0])
        + dot_nt(grad_up[1], up_w[1])
    )
    grad_mid_part, grad_gain_three = rms_backward(mid, factor_three, gain_three, grad_ffw_in)
    grad_mid = grad_top + grad_mid_part
    grad_proj, grad_gain_two = rms_backward(attn_proj, factor_two, gain_two, grad_mid)
    grad_proj_bf = grad_proj.astype(bf16)
    grad_attn = tuple(dot_nt(grad_proj_bf, half).astype(bf16) for half in out_w)
    grad_heads = heads_first(grad_attn)

    def both(own, other):
        return jnp.concatenate([own, swap(other)], axis=0)

    ffw_in2 = both(ffw_in, ffw_in)
    grad_w_down = dot_tn(both(hidden[0], hidden[1]), both(grad_ffw_bf, grad_ffw_bf))
    grad_w_gate = dot_tn(ffw_in2, both(grad_gate[0], grad_gate[1]))
    grad_w_up = dot_tn(ffw_in2, both(grad_up[0], grad_up[1]))
    grad_w_out = dot_tn(both(attn_out[0], attn_out[1]), both(grad_proj_bf, grad_proj_bf))
    attn_in2 = both(attn_in, attn_in)

    delta = jnp.sum(grad_heads.astype(f32) * attn_heads.astype(f32), axis=-1, keepdims=True)
    grad_query, kv_terms = attention_backward(
        query_rot, key_all, value_all, pos4, key_pos, grad_heads, log_total, delta
    )
    grad_query_raw, grad_gain_query = rms_backward(
        query_raw, query_factor, gain_query, rotate_back(grad_query, cos4, sin4)
    )
    grad_query_bf = heads_last(grad_query_raw.astype(bf16))
    grad_w_query = dot_tn(attn_in2, both(grad_query_bf[0], grad_query_bf[1]))
    big = tuple(
        g.astype(bf16) for g in (grad_w_query, grad_w_out, grad_w_gate, grad_w_up, grad_w_down)
    )
    sum_query, sum_out, sum_gate, sum_up, sum_down = (
        g.astype(f32) for g in lax.psum(big, CTX)
    )

    kv_mine = scatter_sum(kv_terms)
    grad_key_raw, grad_gain_key = rms_backward(
        key_raw, key_factor, gain_key, rotate_back(kv_mine[:, :HDIM], cos_tab, sin_tab)
    )
    grad_key_bf = grad_key_raw.astype(bf16)
    grad_value_bf = kv_mine[:, HDIM:].astype(bf16)

    def mine_other(full):
        a, b = full[:, :128], full[:, 128:]
        return jnp.where(first, a, b), jnp.where(first, b, a)

    key_m, key_o = mine_other(grad_key_bf)
    val_m, val_o = mine_other(grad_value_bf)
    grad_kv2 = both(
        jnp.concatenate([key_m, val_m], axis=1), jnp.concatenate([key_o, val_o], axis=1)
    )
    grad_w_kv = dot_tn(grad_kv2, attn_in2)

    grad_attn_in = (
        dot_nt(grad_query_bf[0], query_w[0])
        + dot_nt(grad_query_bf[1], query_w[1])
        + dot_nt(grad_key_bf, key_w)
        + dot_nt(grad_value_bf, value_w)
    )
    grad_in_part, grad_gain_one = rms_backward(resid_in, factor_one, gain_one, grad_attn_in)
    input_grad = grad_mid + grad_in_part

    gain_grads = (
        grad_gain_one,
        grad_gain_two,
        grad_gain_three,
        grad_gain_four,
        grad_gain_query,
        grad_gain_key,
    )
    g_own = jnp.concatenate([jnp.where(first, g[: g.size // 2], g[g.size // 2 :]) for g in gain_grads])
    g_other = jnp.concatenate([jnp.where(first, g[g.size // 2 :], g[: g.size // 2]) for g in gain_grads])
    g_sum = g_own + swap(g_other[None])[0]
    g_block = jnp.concatenate([g_sum, jnp.zeros((1024,), f32)]).reshape(64, 40).astype(bf16)
    late = jnp.concatenate([grad_w_kv.astype(bf16).reshape(64, 2560), g_block], axis=1)
    late = small_sum(late).astype(f32)
    sum_kv = late[:, :2560].reshape(256, 640)
    sum_gains = late[:, 2560:].reshape(-1)
    return (
        block_output[None],
        input_grad[None],
        sum_query,
        sum_kv[:128].T,
        sum_kv[128:].T,
        sum_out,
        sum_gate,
        sum_up,
        sum_down,
        sum_gains[:320],
        sum_gains[1280:1408],
        sum_gains[1408:1536],
        sum_gains[320:640],
        sum_gains[640:960],
        sum_gains[960:1280],
    )


def solution(mesh):
    grid = Mesh(mesh.devices.reshape(4, 4, 4, 2), ("z", "x", "y", "wsh"))
    tokens = P("wsh", CTX, None)
    cols, rows, vec = P(None, "wsh"), P("wsh", None), P("wsh")
    return jax.shard_map(
        per_device,
        mesh=grid,
        in_specs=(tokens, tokens, P(), cols, cols, cols, rows, cols, cols, rows) + (vec,) * 6,
        out_specs=(tokens, tokens, cols, cols, cols, rows, cols, cols, rows) + (vec,) * 6,
        check_vma=False,
    )
```

```python
import functools

import jax
import jax.numpy as jnp
from jax import lax
from jax.experimental import pallas as pl
from jax.experimental.pallas import tpu as pltpu
from jax.sharding import Mesh
from jax.sharding import PartitionSpec as P

HEADS = 4
HDIM = 256
CTX = ("z", "x", "y")
LOG2E = 1.4426950408889634

epsilon = 1e-06
theta_base = 1000000.0
bf16 = jnp.bfloat16
f32 = jnp.float32


def rms_forward(values, gain_w):
    factor = lax.rsqrt(jnp.mean(values * values, axis=-1, keepdims=True) + epsilon)
    return (values * factor * (1.0 + gain_w), factor)


def rms_backward(values, factor, gain_w, grad_out):
    weighted = grad_out * (1.0 + gain_w)
    inner = jnp.mean(weighted * values, axis=-1, keepdims=True)
    grad_in = factor * (weighted - values * factor * factor * inner)
    grad_gain = jnp.sum((grad_out * values * factor).reshape(-1, values.shape[-1]), axis=0)
    return (grad_in, grad_gain)


def rotary_tables(positions, width):
    half_width = width // 2
    frequency = theta_base ** (-jnp.arange(half_width, dtype=f32) * 2.0 / width)
    angles = positions.astype(f32)[:, None] * frequency[None, :]
    return (jnp.cos(angles), jnp.sin(angles))


def rotate(values, cos_tab, sin_tab):
    half = values.shape[-1] // 2
    a, b = values[..., :half], values[..., half:]
    return jnp.concatenate([a * cos_tab - b * sin_tab, b * cos_tab + a * sin_tab], axis=-1)


def rotate_back(grads, cos_tab, sin_tab):
    half = grads.shape[-1] // 2
    a, b = grads[..., :half], grads[..., half:]
    return jnp.concatenate([a * cos_tab + b * sin_tab, b * cos_tab - a * sin_tab], axis=-1)


def block_positions(block_ids, half_rows):
    offsets = jnp.arange(half_rows, dtype=jnp.int32)
    return (block_ids[:, None] * half_rows + offsets[None, :]).reshape(-1)


def dot_f32(left, right):
    return jnp.dot(left, right, preferred_element_type=f32)


def dot_nt(left, right):
    return lax.dot_general(left, right, (((1,), (1,)), ((), ())), preferred_element_type=f32)


def dot_tn(left, right):
    return lax.dot_general(left, right, (((0,), (0,)), ((), ())), preferred_element_type=f32)


def swap(values):
    return lax.ppermute(values, "wsh", [(0, 1), (1, 0)])


def load_tile(table, tile, a_ref, b_ref, kv_tile):
    for i in range(4):
        slot = table[4 * tile + i]

        @pl.when(slot < 16)
        def _():
            kv_tile[64 * i : 64 * i + 64, :] = a_ref[pl.ds(pl.multiple_of(slot * 64, 64), 64), :]

        @pl.when(slot >= 16)
        def _():
            start = pl.multiple_of((slot - 16) * 64, 64)
            kv_tile[64 * i : 64 * i + 64, :] = b_ref[pl.ds(start, 64), :]


def key_places(table, tile, shape, dim):
    place = lax.broadcasted_iota(jnp.int32, shape, dim)
    base = jnp.full(shape, table[32 + 4 * tile + 3], jnp.int32)
    for i in (2, 1, 0):
        base = jnp.where(place < 64 * (i + 1), table[32 + 4 * tile + i], base)
    return base * 64 + place % 64


def forward_kernel(first, table, q_ref, a_ref, b_ref, *rest):
    if first:
        acc_ref, tot_ref, kv_tile = rest
        acc_ref[...] = jnp.zeros_like(acc_ref)
        tot_ref[...] = jnp.zeros_like(tot_ref)
    else:
        acc_in, tot_in, acc_ref, tot_ref, kv_tile = rest
        acc_ref[...] = acc_in[...]
        tot_ref[...] = tot_in[...]
    most = jnp.maximum(table[66], table[67])

    def step(tile, carry):
        load_tile(table, tile, a_ref, b_ref, kv_tile)
        places = key_places(table, tile, (1, 256), 1)
        for half in range(2):

            @pl.when(4 * tile < table[66 + half])
            def _():
                rows = slice(256 * half, 256 * half + 256)
                mine = lax.broadcasted_iota(jnp.int32, (256, 1), 0) % 64 + table[64 + half] * 64
                scores = dot_nt(q_ref[rows, :], kv_tile[:, :HDIM])
                probs = jnp.where(places <= mine, jnp.exp2(scores * LOG2E), 0.0)
                tot_ref[rows, :] += probs[:, :128] + probs[:, 128:]
                acc_ref[rows, :] += dot_f32(probs.astype(bf16), kv_tile[:, HDIM:])

        return carry

    lax.fori_loop(0, (most + 3) // 4, step, 0)


def backward_kernel(first, table, q_ref, g_ref, stat_ref, a_ref, b_ref, *rest):
    if first:
        dq_ref, da_ref, db_ref, kv_tile, dkv_tile = rest
        dq_ref[...] = jnp.zeros_like(dq_ref)
    else:
        dq_in, dq_ref, da_ref, db_ref, kv_tile, dkv_tile = rest
        dq_ref[...] = dq_in[...]
    da_ref[...] = jnp.zeros_like(da_ref)
    db_ref[...] = jnp.zeros_like(db_ref)
    most = jnp.maximum(table[66], table[67])

    def step(tile, carry):
        load_tile(table, tile, a_ref, b_ref, kv_tile)
        dkv_tile[...] = jnp.zeros_like(dkv_tile)
        places = key_places(table, tile, (256, 1), 0)
        for half in range(2):

            @pl.when(4 * tile < table[66 + half])
            def _():
                rows = slice(256 * half, 256 * half + 256)
                mine = lax.broadcasted_iota(jnp.int32, (1, 256), 1) % 64 + table[64 + half] * 64
                query, grads = q_ref[rows, :], g_ref[rows, :]
                keys, vals = kv_tile[:, :HDIM], kv_tile[:, HDIM:]
                scores = dot_nt(keys, query) * LOG2E - stat_ref[0:1, rows]
                probs = jnp.where(places <= mine, jnp.exp2(scores), 0.0)
                grad_scores = (probs * (dot_nt(vals, grads) - stat_ref[1:2, rows])).astype(bf16)
                dkv_tile[:, :HDIM] += dot_f32(grad_scores, query)
                dkv_tile[:, HDIM:] += dot_f32(probs.astype(bf16), grads)
                dq_ref[rows, :] += dot_tn(grad_scores, keys)

        for i in range(4):
            slot = table[4 * tile + i]
            block = dkv_tile[64 * i : 64 * i + 64, :].astype(bf16)

            @pl.when(slot < 16)
            def _():
                da_ref[pl.ds(pl.multiple_of(slot * 64, 64), 64), :] = block

            @pl.when(slot >= 16)
            def _():
                db_ref[pl.ds(pl.multiple_of((slot - 16) * 64, 64), 64), :] = block

        return carry

    lax.fori_loop(0, (most + 3) // 4, step, 0)


def specs(count):
    return [pl.BlockSpec(memory_space=pltpu.SMEM)] + [
        pl.BlockSpec(memory_space=pltpu.VMEM) for _ in range(count)
    ]


def forward_piece(table, query, a, b, state):
    return pl.pallas_call(
        functools.partial(forward_kernel, state is None),
        out_shape=(
            jax.ShapeDtypeStruct((512, HDIM), f32),
            jax.ShapeDtypeStruct((512, 128), f32),
        ),
        in_specs=specs(3 if state is None else 5),
        out_specs=tuple(specs(2)[1:]),
        scratch_shapes=[pltpu.VMEM((256, 512), bf16)],
        input_output_aliases={} if state is None else {4: 0, 5: 1},
        name="attn_fwd",
    )(table, query, a, b, *(state or ()))


def backward_piece(table, query, grads, stats, a, b, grad_query):
    return pl.pallas_call(
        functools.partial(backward_kernel, grad_query is None),
        out_shape=(
            jax.ShapeDtypeStruct((512, HDIM), f32),
            jax.ShapeDtypeStruct((1024, 512), bf16),
            jax.ShapeDtypeStruct((1024, 512), bf16),
        ),
        in_specs=specs(5 if grad_query is None else 6),
        out_specs=tuple(specs(3)[1:]),
        scratch_shapes=[pltpu.VMEM((256, 512), bf16), pltpu.VMEM((256, 512), f32)],
        input_output_aliases={} if grad_query is None else {6: 0},
        name="attn_bwd",
    )(table, query, grads, stats, a, b, *(() if grad_query is None else (grad_query,)))


def shift(values, axis, sign):
    perm = [
        (2 * a + w, 2 * ((a + (sign if w == 0 else -sign)) % 4) + w)
        for a in range(4)
        for w in range(2)
    ]
    return lax.ppermute(values, (axis, "wsh"), perm)


def ring_gather(block, axis):
    out = [block]
    for _ in range(3):
        out.append(shift(out[-1], axis, 1))
    return out


def ring_sum(parts, axis):
    moving = parts[3]
    for d in (2, 1, 0):
        moving = shift(moving, axis, -1).astype(f32) + parts[d].astype(f32)
        if d:
            moving = moving.astype(bf16)
    return moving


def gather_ctx(block):
    near = ring_gather(block, "z")
    a = ring_gather(jnp.concatenate([x[:64] for x in near]), "x")
    b = ring_gather(jnp.concatenate([x[64:] for x in near]), "y")
    a = ring_gather(jnp.concatenate(a), "y")
    b = ring_gather(jnp.concatenate(b), "x")
    return list(zip(a, b))


def scatter_sum(pieces):
    a = ring_sum([p[0] for p in pieces], "y").astype(bf16)
    b = ring_sum([p[1] for p in pieces], "x").astype(bf16)
    a = ring_sum([a[256 * d : 256 * d + 256] for d in range(4)], "x").astype(bf16)
    b = ring_sum([b[256 * d : 256 * d + 256] for d in range(4)], "y").astype(bf16)
    both = [
        jnp.concatenate([a[64 * d : 64 * d + 64], b[64 * d : 64 * d + 64]]) for d in range(4)
    ]
    return ring_sum(both, "z")


def piece_tables(pair_blocks, mine, sign):
    z, x, y = (lax.axis_index(name) for name in CTX)
    i = jnp.arange(128, dtype=jnp.int32)
    piece, inside = i // 32, i % 32
    color, outer, inner = inside // 16, (inside % 16) // 4, inside % 4
    at_z = (z - sign * inner) % 4
    at_x = (x - sign * jnp.where(color == 0, outer, piece)) % 4
    at_y = (y - sign * jnp.where(color == 0, piece, outer)) % 4
    source = 2 * (at_z * 16 + at_x * 4 + at_y) + color
    flat = pair_blocks.reshape(1, 128)
    hit = source[:, None] == jnp.arange(128, dtype=jnp.int32)[None]
    ids = jnp.sum(jnp.where(hit, flat, 0), axis=1).reshape(4, 32)
    rank = jnp.sum((ids[:, None, :] < ids[:, :, None]).astype(jnp.int32), axis=2)
    at = rank[:, None, :] == jnp.arange(32, dtype=jnp.int32)[None, :, None]
    slots = jnp.sum(jnp.where(at, jnp.arange(32, dtype=jnp.int32)[None, None], 0), axis=2)
    sorted_ids = jnp.sum(jnp.where(at, ids[:, None, :], 0), axis=2)
    seen = jnp.sum((ids[:, None, :] <= mine[None, :, None]).astype(jnp.int32), axis=2)
    own = jnp.broadcast_to(mine[None], (4, 2))
    return jnp.concatenate([slots, sorted_ids, own, seen], axis=1)


def small_sum(values):
    rows = values.shape[0] // 64
    got = lax.all_to_all(values.reshape(64, rows, -1), CTX, split_axis=0, concat_axis=0, tiled=True)
    mine = jnp.sum(got.astype(f32), axis=0).astype(values.dtype)
    wide = jnp.broadcast_to(mine[None], (64,) + mine.shape)
    out = lax.all_to_all(wide, CTX, split_axis=0, concat_axis=0, tiled=True)
    return out.reshape(values.shape)


def per_device(
    block_input,
    cotangent,
    pair_blocks,
    w_query,
    w_key,
    w_value,
    w_out,
    w_gate,
    w_up,
    w_down,
    attn_pre_gain,
    query_gain,
    key_gain,
    attn_post_gain,
    ffw_pre_gain,
    ffw_post_gain,
):
    rows = block_input.shape[1]
    rank = lax.axis_index(CTX)
    first = lax.axis_index("wsh") == 0

    def ordered(own, other, axis):
        return jnp.where(
            first,
            jnp.concatenate([own, other], axis=axis),
            jnp.concatenate([other, own], axis=axis),
        )

    resid_in = block_input[0].astype(f32)
    grad_top = cotangent[0]
    my_blocks = lax.dynamic_slice_in_dim(pair_blocks, rank, 1, 0)[0]
    query_pos = block_positions(my_blocks, rows // 2)
    tables = piece_tables(pair_blocks, my_blocks, jnp.where(first, 1, -1))
    cos_tab, sin_tab = rotary_tables(query_pos, HDIM)

    gains_own = jnp.concatenate(
        [attn_pre_gain, attn_post_gain, ffw_pre_gain, ffw_post_gain, query_gain, key_gain]
    )[None]
    gains_other = swap(gains_own)
    kv_own = jnp.concatenate([w_key, w_value], axis=1)
    kv_other = swap(kv_own)

    def gain(start, width):
        return ordered(
            gains_own[0, start : start + width], gains_other[0, start : start + width], 0
        ).astype(f32)[None]

    gain_one, gain_two, gain_three, gain_four = (gain(320 * i, 320) for i in range(4))
    gain_query, gain_key = gain(1280, 128), gain(1408, 128)
    key_w = ordered(kv_own[:, :128], kv_other[:, :128], 1)
    value_w = ordered(kv_own[:, 128:], kv_other[:, 128:], 1)

    normed_one, factor_one = rms_forward(resid_in, gain_one)
    attn_in = normed_one.astype(bf16)
    key_raw = dot_f32(attn_in, key_w)
    value_bf = dot_f32(attn_in, value_w).astype(bf16)
    key_normed, key_factor = rms_forward(key_raw, gain_key)
    key_rot = rotate(key_normed, cos_tab, sin_tab).astype(bf16)
    pieces = gather_ctx(jnp.concatenate([key_rot, value_bf], axis=1))

    query_w = (w_query, swap(w_query))
    out_w = (w_out, swap(w_out))
    gate_w = (w_gate, swap(w_gate))
    up_w = (w_up, swap(w_up))
    down_w = (w_down, swap(w_down))

    def heads_first(pair):
        return jnp.concatenate(
            [
                part[64 * i : 64 * i + 64, HDIM * h : HDIM * (h + 1)]
                for i in range(2)
                for part in pair
                for h in range(2)
            ],
            axis=0,
        )

    def heads_last(stacked):
        def block(i, p, h):
            start = 64 * (4 * i + 2 * p + h)
            return stacked[start : start + 64]

        return tuple(
            jnp.concatenate(
                [jnp.concatenate([block(i, p, 0), block(i, p, 1)], axis=1) for i in range(2)]
            )
            for p in range(2)
        )

    def tile_heads(table):
        return jnp.concatenate([table[:64]] * HEADS + [table[64:]] * HEADS)

    cos4, sin4 = tile_heads(cos_tab), tile_heads(sin_tab)
    query_raw = heads_first(tuple(dot_f32(attn_in, half) for half in query_w))
    query_normed, query_factor = rms_forward(query_raw, gain_query)
    query_rot = (rotate(query_normed, cos4, sin4)).astype(bf16) * bf16(HDIM**-0.5)
    state = None
    for d in range(4):
        state = forward_piece(tables[d], query_rot, *pieces[d], state)
    totals = jnp.sum(state[1], axis=1, keepdims=True)
    attn_heads = (state[0] / totals).astype(bf16)
    attn_out = heads_last(attn_heads)
    attn_proj = dot_f32(attn_out[0], out_w[0]) + dot_f32(attn_out[1], out_w[1])
    normed_two, factor_two = rms_forward(attn_proj, gain_two)
    mid = resid_in + normed_two
    normed_three, factor_three = rms_forward(mid, gain_three)
    ffw_in = normed_three.astype(bf16)

    gate = [dot_f32(ffw_in, half) for half in gate_w]
    up_val = [dot_f32(ffw_in, half) for half in up_w]
    acts = [jax.vjp(lambda inner: jax.nn.gelu(inner, approximate=True), g) for g in gate]
    hidden = [(act[0] * up).astype(bf16) for act, up in zip(acts, up_val)]
    ffw_proj = dot_f32(hidden[0], down_w[0]) + dot_f32(hidden[1], down_w[1])
    normed_four, factor_four = rms_forward(ffw_proj, gain_four)
    block_output = mid + normed_four

    grad_ffw, grad_gain_four = rms_backward(ffw_proj, factor_four, gain_four, grad_top)
    grad_ffw_bf = grad_ffw.astype(bf16)
    grad_hidden = [dot_nt(grad_ffw_bf, half) for half in down_w]
    grad_gate = [
        act[1](gh * up)[0].astype(bf16) for act, gh, up in zip(acts, grad_hidden, up_val)
    ]
    grad_up = [(gh * act[0]).astype(bf16) for act, gh in zip(acts, grad_hidden)]
    grad_ffw_in = (
        dot_nt(grad_gate[0], gate_w[0])
        + dot_nt(grad_gate[1], gate_w[1])
        + dot_nt(grad_up[0], up_w[0])
        + dot_nt(grad_up[1], up_w[1])
    )
    grad_mid_part, grad_gain_three = rms_backward(mid, factor_three, gain_three, grad_ffw_in)
    grad_mid = grad_top + grad_mid_part
    grad_proj, grad_gain_two = rms_backward(attn_proj, factor_two, gain_two, grad_mid)
    grad_proj_bf = grad_proj.astype(bf16)
    grad_attn = tuple(dot_nt(grad_proj_bf, half).astype(bf16) for half in out_w)
    grad_heads = heads_first(grad_attn)

    def both(own, other):
        return jnp.concatenate([own, swap(other)], axis=0)

    ffw_in2 = both(ffw_in, ffw_in)
    grad_w_down = dot_tn(both(hidden[0], hidden[1]), both(grad_ffw_bf, grad_ffw_bf))
    grad_w_gate = dot_tn(ffw_in2, both(grad_gate[0], grad_gate[1]))
    grad_w_up = dot_tn(ffw_in2, both(grad_up[0], grad_up[1]))
    grad_w_out = dot_tn(both(attn_out[0], attn_out[1]), both(grad_proj_bf, grad_proj_bf))
    attn_in2 = both(attn_in, attn_in)

    delta = jnp.sum(grad_heads.astype(f32) * attn_heads.astype(f32), axis=-1)
    stats = jnp.stack([jnp.log2(totals[:, 0]), delta])
    grad_query = None
    kv_terms = [None] * 4
    for d in (3, 2, 1, 0):
        grad_query, *kv_terms[d] = backward_piece(
            tables[d], query_rot, grad_heads, stats, *pieces[d], grad_query
        )
    grad_query = grad_query * HDIM**-0.5
    grad_query_raw, grad_gain_query = rms_backward(
        query_raw, query_factor, gain_query, rotate_back(grad_query, cos4, sin4)
    )
    grad_query_bf = heads_last(grad_query_raw.astype(bf16))
    grad_w_query = dot_tn(attn_in2, both(grad_query_bf[0], grad_query_bf[1]))
    big = tuple(g.astype(bf16) for g in (grad_w_out, grad_w_gate, grad_w_up, grad_w_down))
    sum_out, sum_gate, sum_up, sum_down = (g.astype(f32) for g in lax.psum(big, CTX))
    sum_query = small_sum(grad_w_query.astype(bf16)).astype(f32)

    kv_mine = scatter_sum(kv_terms)
    grad_key_raw, grad_gain_key = rms_backward(
        key_raw, key_factor, gain_key, rotate_back(kv_mine[:, :HDIM], cos_tab, sin_tab)
    )
    grad_key_bf = grad_key_raw.astype(bf16)
    grad_value_bf = kv_mine[:, HDIM:].astype(bf16)

    def mine_other(full):
        a, b = full[:, :128], full[:, 128:]
        return jnp.where(first, a, b), jnp.where(first, b, a)

    key_m, key_o = mine_other(grad_key_bf)
    val_m, val_o = mine_other(grad_value_bf)
    grad_kv2 = both(
        jnp.concatenate([key_m, val_m], axis=1), jnp.concatenate([key_o, val_o], axis=1)
    )
    grad_w_kv = dot_tn(grad_kv2, attn_in2)

    grad_attn_in = (
        dot_nt(grad_query_bf[0], query_w[0])
        + dot_nt(grad_query_bf[1], query_w[1])
        + dot_nt(grad_key_bf, key_w)
        + dot_nt(grad_value_bf, value_w)
    )
    grad_in_part, grad_gain_one = rms_backward(resid_in, factor_one, gain_one, grad_attn_in)
    input_grad = grad_mid + grad_in_part

    gain_grads = (
        grad_gain_one,
        grad_gain_two,
        grad_gain_three,
        grad_gain_four,
        grad_gain_query,
        grad_gain_key,
    )
    g_own = jnp.concatenate([jnp.where(first, g[: g.size // 2], g[g.size // 2 :]) for g in gain_grads])
    g_other = jnp.concatenate([jnp.where(first, g[g.size // 2 :], g[: g.size // 2]) for g in gain_grads])
    g_sum = g_own + swap(g_other[None])[0]
    g_block = jnp.concatenate([g_sum, jnp.zeros((1024,), f32)]).reshape(64, 40).astype(bf16)
    late = jnp.concatenate([grad_w_kv.astype(bf16).reshape(64, 2560), g_block], axis=1)
    late = small_sum(late).astype(f32)
    sum_kv = late[:, :2560].reshape(256, 640)
    sum_gains = late[:, 2560:].reshape(-1)
    return (
        block_output[None],
        input_grad[None],
        sum_query,
        sum_kv[:128].T,
        sum_kv[128:].T,
        sum_out,
        sum_gate,
        sum_up,
        sum_down,
        sum_gains[:320],
        sum_gains[1280:1408],
        sum_gains[1408:1536],
        sum_gains[320:640],
        sum_gains[640:960],
        sum_gains[960:1280],
    )


def solution(mesh):
    grid = Mesh(mesh.devices.reshape(4, 4, 4, 2), ("z", "x", "y", "wsh"))
    tokens = P("wsh", CTX, None)
    cols, rows, vec = P(None, "wsh"), P("wsh", None), P("wsh")
    return jax.shard_map(
        per_device,
        mesh=grid,
        in_specs=(tokens, tokens, P(), cols, cols, cols, rows, cols, cols, rows) + (vec,) * 6,
        out_specs=(tokens, tokens, cols, cols, cols, rows, cols, cols, rows) + (vec,) * 6,
        check_vma=False,
    )
```

```python
import functools

import jax
import jax.numpy as jnp
from jax import lax
from jax.experimental import pallas as pl
from jax.experimental.pallas import tpu as pltpu
from jax.sharding import Mesh
from jax.sharding import PartitionSpec as P

HEADS = 4
HDIM = 256
CTX = ("z", "x", "y")
LOG2E = 1.4426950408889634

epsilon = 1e-06
theta_base = 1000000.0
bf16 = jnp.bfloat16
f32 = jnp.float32


def rms_forward(values, gain_w):
    factor = lax.rsqrt(jnp.mean(values * values, axis=-1, keepdims=True) + epsilon)
    return (values * factor * (1.0 + gain_w), factor)


def rms_backward(values, factor, gain_w, grad_out):
    weighted = grad_out * (1.0 + gain_w)
    inner = jnp.mean(weighted * values, axis=-1, keepdims=True)
    grad_in = factor * (weighted - values * factor * factor * inner)
    grad_gain = jnp.sum((grad_out * values * factor).reshape(-1, values.shape[-1]), axis=0)
    return (grad_in, grad_gain)


def rotary_tables(positions, width):
    half_width = width // 2
    frequency = theta_base ** (-jnp.arange(half_width, dtype=f32) * 2.0 / width)
    angles = positions.astype(f32)[:, None] * frequency[None, :]
    return (jnp.cos(angles), jnp.sin(angles))


def rotate(values, cos_tab, sin_tab):
    half = values.shape[-1] // 2
    a, b = values[..., :half], values[..., half:]
    return jnp.concatenate([a * cos_tab - b * sin_tab, b * cos_tab + a * sin_tab], axis=-1)


def rotate_back(grads, cos_tab, sin_tab):
    half = grads.shape[-1] // 2
    a, b = grads[..., :half], grads[..., half:]
    return jnp.concatenate([a * cos_tab + b * sin_tab, b * cos_tab - a * sin_tab], axis=-1)


def block_positions(block_ids, half_rows):
    offsets = jnp.arange(half_rows, dtype=jnp.int32)
    return (block_ids[:, None] * half_rows + offsets[None, :]).reshape(-1)


def dot_f32(left, right):
    return jnp.dot(left, right, preferred_element_type=f32)


def dot_nt(left, right):
    return lax.dot_general(left, right, (((1,), (1,)), ((), ())), preferred_element_type=f32)


def dot_tn(left, right):
    return lax.dot_general(left, right, (((0,), (0,)), ((), ())), preferred_element_type=f32)


def swap(values):
    return lax.ppermute(values, "wsh", [(0, 1), (1, 0)])


def load_group(table, group, kv_all):
    slots = [table[8 * group + i] for i in range(8)]
    blocks = [kv_all[pl.ds(pl.multiple_of(slot * 64, 64), 64), :] for slot in slots]
    keys = jnp.concatenate([block[:, :HDIM] for block in blocks], axis=0)
    vals = jnp.concatenate([block[:, HDIM:] for block in blocks], axis=0)
    return slots, keys, vals


def key_places(table, group, shape, dim):
    place = lax.broadcasted_iota(jnp.int32, shape, dim)
    base = jnp.full(shape, table[32 + 8 * group + 7], jnp.int32)
    for i in range(6, -1, -1):
        base = jnp.where(place < 64 * (i + 1), table[32 + 8 * group + i], base)
    return base * 64 + place % 64


def forward_kernel(first, table, q_ref, a_ref, b_ref, *rest):
    if first:
        acc_ref, tot_ref, kv_all = rest
        acc_ref[...] = jnp.zeros_like(acc_ref)
        tot_ref[...] = jnp.zeros_like(tot_ref)
    else:
        acc_in, tot_in, acc_ref, tot_ref, kv_all = rest
        acc_ref[...] = acc_in[...]
        tot_ref[...] = tot_in[...]
    kv_all[:1024, :] = a_ref[...]
    kv_all[1024:, :] = b_ref[...]

    def step(group, carry):
        _, keys, vals = load_group(table, group, kv_all)
        places = key_places(table, group, (1, 512), 1)

        def half(i):
            rows = pl.ds(pl.multiple_of(table[64 + i] * 256, 256), 256)
            mine = lax.broadcasted_iota(jnp.int32, (256, 1), 0) % 64 + table[66 + i] * 64
            scores = dot_nt(q_ref[rows, :], keys)
            probs = jnp.where(places <= mine, jnp.exp2(scores * LOG2E), 0.0)
            tot_ref[rows, :] += (probs[:, :128] + probs[:, 128:256]) + (
                probs[:, 256:384] + probs[:, 384:]
            )
            acc_ref[rows, :] += dot_f32(probs.astype(bf16), vals)

        half(0)
        pl.when(8 * group < table[69])(lambda: half(1))
        return carry

    lax.fori_loop(0, (table[68] + 7) // 8, step, 0)


def backward_kernel(first, table, q_ref, g_ref, stat_ref, a_ref, b_ref, *rest):
    if first:
        dq_ref, da_ref, db_ref, kv_all, dkv, out_all = rest
        dq_ref[...] = jnp.zeros_like(dq_ref)
    else:
        dq_in, dq_ref, da_ref, db_ref, kv_all, dkv, out_all = rest
        dq_ref[...] = dq_in[...]
    kv_all[:1024, :] = a_ref[...]
    kv_all[1024:, :] = b_ref[...]
    out_all[...] = jnp.zeros_like(out_all)

    def step(group, carry):
        slots, keys, vals = load_group(table, group, kv_all)
        places = key_places(table, group, (512, 1), 0)

        def half(i):
            rows = pl.ds(pl.multiple_of(table[64 + i] * 256, 256), 256)
            mine = lax.broadcasted_iota(jnp.int32, (1, 256), 1) % 64 + table[66 + i] * 64
            query, grads = q_ref[rows, :], g_ref[rows, :]
            stat = stat_ref[table[64 + i]]
            scores = dot_nt(keys, query) * LOG2E - stat[0:1, :]
            probs = jnp.where(places <= mine, jnp.exp2(scores), 0.0)
            grad_scores = (probs * (dot_nt(vals, grads) - stat[1:2, :])).astype(bf16)
            dq_ref[rows, :] += dot_tn(grad_scores, keys)
            return dot_f32(grad_scores, query), dot_f32(probs.astype(bf16), grads)

        grad_k, grad_v = half(0)
        dkv[:, :HDIM] = grad_k
        dkv[:, HDIM:] = grad_v

        @pl.when(8 * group < table[69])
        def _():
            more_k, more_v = half(1)
            dkv[:, :HDIM] += more_k
            dkv[:, HDIM:] += more_v

        for i, slot in enumerate(slots):
            block = dkv[64 * i : 64 * i + 64, :].astype(bf16)
            out_all[pl.ds(pl.multiple_of(slot * 64, 64), 64), :] = block
        return carry

    lax.fori_loop(0, (table[68] + 7) // 8, step, 0)
    da_ref[...] = out_all[:1024, :]
    db_ref[...] = out_all[1024:, :]


def specs(count):
    return [pl.BlockSpec(memory_space=pltpu.SMEM)] + [
        pl.BlockSpec(memory_space=pltpu.VMEM) for _ in range(count)
    ]


def forward_piece(table, query, a, b, state):
    return pl.pallas_call(
        functools.partial(forward_kernel, state is None),
        out_shape=(
            jax.ShapeDtypeStruct((512, HDIM), f32),
            jax.ShapeDtypeStruct((512, 128), f32),
        ),
        in_specs=specs(3 if state is None else 5),
        out_specs=tuple(specs(2)[1:]),
        scratch_shapes=[pltpu.VMEM((2048, 512), bf16)],
        cost_estimate=pl.CostEstimate(flops=2 * 10**9, transcendentals=0, bytes_accessed=4 * 10**6),
        input_output_aliases={} if state is None else {4: 0, 5: 1},
        name="attn_fwd",
    )(table, query, a, b, *(state or ()))


def backward_piece(table, query, grads, stats, a, b, grad_query):
    return pl.pallas_call(
        functools.partial(backward_kernel, grad_query is None),
        out_shape=(
            jax.ShapeDtypeStruct((512, HDIM), f32),
            jax.ShapeDtypeStruct((1024, 512), bf16),
            jax.ShapeDtypeStruct((1024, 512), bf16),
        ),
        in_specs=specs(5 if grad_query is None else 6),
        out_specs=tuple(specs(3)[1:]),
        scratch_shapes=[
            pltpu.VMEM((2048, 512), bf16),
            pltpu.VMEM((512, 512), f32),
            pltpu.VMEM((2048, 512), bf16),
        ],
        cost_estimate=pl.CostEstimate(flops=5 * 10**9, transcendentals=0, bytes_accessed=8 * 10**6),
        input_output_aliases={} if grad_query is None else {6: 0},
        name="attn_bwd",
    )(table, query, grads, stats, a, b, *(() if grad_query is None else (grad_query,)))


def shift(values, axis, by):
    perm = [
        (2 * a + w, 2 * ((a + (by if w == 0 else -by)) % 4) + w) for a in range(4) for w in range(2)
    ]
    return lax.ppermute(values, (axis, "wsh"), perm)


def ring_gather(block, axis):
    out = [block]
    for _ in range(3):
        out.append(shift(out[-1], axis, 1))
    return out


def ring_sum(parts, axis):
    moving = parts[3]
    for d in (2, 1, 0):
        moving = (shift(moving, axis, -1).astype(f32) + parts[d].astype(f32)).astype(bf16)
    return moving


def direct_gather(block, axis):
    return [block] + [shift(block, axis, d) for d in (1, 2, 3)]


def direct_sum(parts, axis):
    got = [shift(parts[d], axis, -d) for d in (1, 2, 3)]
    return sum((g.astype(f32) for g in got), parts[0].astype(f32))


def gather_ctx(block):
    near = direct_gather(block, "z")
    a = direct_gather(jnp.concatenate([x[:64] for x in near]), "x")
    b = direct_gather(jnp.concatenate([x[64:] for x in near]), "y")
    a = ring_gather(jnp.concatenate(a), "y")
    b = ring_gather(jnp.concatenate(b), "x")
    return list(zip(a, b))


def scatter_sum(pieces):
    a = ring_sum([p[0] for p in pieces], "y")
    b = ring_sum([p[1] for p in pieces], "x")
    a = direct_sum([a[256 * d : 256 * d + 256] for d in range(4)], "x").astype(bf16)
    b = direct_sum([b[256 * d : 256 * d + 256] for d in range(4)], "y").astype(bf16)
    both = [
        jnp.concatenate([a[64 * d : 64 * d + 64], b[64 * d : 64 * d + 64]]) for d in range(4)
    ]
    return direct_sum(both, "z")


def piece_tables(pair_blocks, mine, sign):
    z, x, y = (lax.axis_index(name) for name in CTX)
    i = jnp.arange(128, dtype=jnp.int32)
    piece, inside = i // 32, i % 32
    color, outer, inner = inside // 16, (inside % 16) // 4, inside % 4
    at_z = (z - sign * inner) % 4
    at_x = (x - sign * jnp.where(color == 0, outer, piece)) % 4
    at_y = (y - sign * jnp.where(color == 0, piece, outer)) % 4
    source = 2 * (at_z * 16 + at_x * 4 + at_y) + color
    flat = pair_blocks.reshape(1, 128)
    hit = source[:, None] == jnp.arange(128, dtype=jnp.int32)[None]
    ids = jnp.sum(jnp.where(hit, flat, 0), axis=1).reshape(4, 32)
    rank = jnp.sum((ids[:, None, :] < ids[:, :, None]).astype(jnp.int32), axis=2)
    at = rank[:, None, :] == jnp.arange(32, dtype=jnp.int32)[None, :, None]
    slots = jnp.sum(jnp.where(at, jnp.arange(32, dtype=jnp.int32)[None, None], 0), axis=2)
    sorted_ids = jnp.sum(jnp.where(at, ids[:, None, :], 0), axis=2)
    seen = jnp.sum((ids[:, None, :] <= mine[None, :, None]).astype(jnp.int32), axis=2)
    upper = (mine[1] > mine[0]).astype(jnp.int32)
    which = jnp.stack([upper, 1 - upper])
    own = jnp.stack([jnp.max(mine), jnp.min(mine)])
    fixed = jnp.broadcast_to(jnp.concatenate([which, own])[None], (4, 4))
    seen = jnp.stack([jnp.max(seen, axis=1), jnp.min(seen, axis=1)], axis=1)
    return jnp.concatenate([slots, sorted_ids, fixed, seen], axis=1)


def small_sum(values):
    rows = values.shape[0] // 64
    got = lax.all_to_all(values.reshape(64, rows, -1), CTX, split_axis=0, concat_axis=0, tiled=True)
    mine = jnp.sum(got.astype(f32), axis=0).astype(values.dtype)
    wide = jnp.broadcast_to(mine[None], (64,) + mine.shape)
    out = lax.all_to_all(wide, CTX, split_axis=0, concat_axis=0, tiled=True)
    return out.reshape(values.shape)


def per_device(
    block_input,
    cotangent,
    pair_blocks,
    w_query,
    w_key,
    w_value,
    w_out,
    w_gate,
    w_up,
    w_down,
    attn_pre_gain,
    query_gain,
    key_gain,
    attn_post_gain,
    ffw_pre_gain,
    ffw_post_gain,
):
    rows = block_input.shape[1]
    rank = lax.axis_index(CTX)
    first = lax.axis_index("wsh") == 0

    def ordered(own, other, axis):
        return jnp.where(
            first,
            jnp.concatenate([own, other], axis=axis),
            jnp.concatenate([other, own], axis=axis),
        )

    resid_in = block_input[0].astype(f32)
    grad_top = cotangent[0]
    my_blocks = lax.dynamic_slice_in_dim(pair_blocks, rank, 1, 0)[0]
    query_pos = block_positions(my_blocks, rows // 2)
    tables = piece_tables(pair_blocks, my_blocks, jnp.where(first, 1, -1))
    cos_tab, sin_tab = rotary_tables(query_pos, HDIM)

    kv_own = jnp.concatenate([w_key, w_value], axis=1)
    kv_other = swap(kv_own)

    def gain(own):
        own = own[None]
        return ordered(own, swap(own), 1).astype(f32)

    gain_one, gain_key, gain_query = gain(attn_pre_gain), gain(key_gain), gain(query_gain)
    gain_two, gain_three, gain_four = gain(attn_post_gain), gain(ffw_pre_gain), gain(ffw_post_gain)
    key_w = ordered(kv_own[:, :128], kv_other[:, :128], 1)
    value_w = ordered(kv_own[:, 128:], kv_other[:, 128:], 1)

    normed_one, factor_one = rms_forward(resid_in, gain_one)
    attn_in = normed_one.astype(bf16)
    key_raw = dot_f32(attn_in, key_w)
    value_bf = dot_f32(attn_in, value_w).astype(bf16)
    key_normed, key_factor = rms_forward(key_raw, gain_key)
    key_rot = rotate(key_normed, cos_tab, sin_tab).astype(bf16)
    pieces = gather_ctx(jnp.concatenate([key_rot, value_bf], axis=1))

    query_w = (w_query, swap(w_query))
    out_w = (w_out, swap(w_out))
    gate_w = (w_gate, swap(w_gate))
    up_w = (w_up, swap(w_up))
    down_w = (w_down, swap(w_down))

    def heads_first(pair):
        return jnp.concatenate(
            [
                part[64 * i : 64 * i + 64, HDIM * h : HDIM * (h + 1)]
                for i in range(2)
                for part in pair
                for h in range(2)
            ],
            axis=0,
        )

    def heads_last(stacked):
        def block(i, p, h):
            start = 64 * (4 * i + 2 * p + h)
            return stacked[start : start + 64]

        return tuple(
            jnp.concatenate(
                [jnp.concatenate([block(i, p, 0), block(i, p, 1)], axis=1) for i in range(2)]
            )
            for p in range(2)
        )

    def tile_heads(table):
        return jnp.concatenate([table[:64]] * HEADS + [table[64:]] * HEADS)

    cos4, sin4 = tile_heads(cos_tab), tile_heads(sin_tab)
    query_raw = heads_first(tuple(dot_f32(attn_in, half) for half in query_w))
    query_normed, query_factor = rms_forward(query_raw, gain_query)
    query_rot = (rotate(query_normed, cos4, sin4)).astype(bf16) * bf16(HDIM**-0.5)
    state = None
    for d in range(4):
        state = forward_piece(tables[d], query_rot, *pieces[d], state)
    totals = jnp.sum(state[1], axis=1, keepdims=True)
    attn_heads = (state[0] / totals).astype(bf16)
    attn_out = heads_last(attn_heads)
    attn_proj = dot_f32(attn_out[0], out_w[0]) + dot_f32(attn_out[1], out_w[1])
    normed_two, factor_two = rms_forward(attn_proj, gain_two)
    mid = resid_in + normed_two
    normed_three, factor_three = rms_forward(mid, gain_three)
    ffw_in = normed_three.astype(bf16)

    gate = [dot_f32(ffw_in, half) for half in gate_w]
    up_val = [dot_f32(ffw_in, half) for half in up_w]
    acts = [jax.vjp(lambda inner: jax.nn.gelu(inner, approximate=True), g) for g in gate]
    hidden = [(act[0] * up).astype(bf16) for act, up in zip(acts, up_val)]
    ffw_proj = dot_f32(hidden[0], down_w[0]) + dot_f32(hidden[1], down_w[1])
    normed_four, factor_four = rms_forward(ffw_proj, gain_four)
    block_output = mid + normed_four

    grad_ffw, grad_gain_four = rms_backward(ffw_proj, factor_four, gain_four, grad_top)
    grad_ffw_bf = grad_ffw.astype(bf16)
    grad_hidden = [dot_nt(grad_ffw_bf, half) for half in down_w]
    grad_gate = [
        act[1](gh * up)[0].astype(bf16) for act, gh, up in zip(acts, grad_hidden, up_val)
    ]
    grad_up = [(gh * act[0]).astype(bf16) for act, gh in zip(acts, grad_hidden)]
    grad_ffw_in = (
        dot_nt(grad_gate[0], gate_w[0])
        + dot_nt(grad_gate[1], gate_w[1])
        + dot_nt(grad_up[0], up_w[0])
        + dot_nt(grad_up[1], up_w[1])
    )
    grad_mid_part, grad_gain_three = rms_backward(mid, factor_three, gain_three, grad_ffw_in)
    grad_mid = grad_top + grad_mid_part
    grad_proj, grad_gain_two = rms_backward(attn_proj, factor_two, gain_two, grad_mid)
    grad_proj_bf = grad_proj.astype(bf16)
    grad_attn = tuple(dot_nt(grad_proj_bf, half).astype(bf16) for half in out_w)
    grad_heads = heads_first(grad_attn)

    def both(own, other):
        return jnp.concatenate([own, swap(other)], axis=0)

    ffw_in2 = both(ffw_in, ffw_in)
    grad_w_down = dot_tn(both(hidden[0], hidden[1]), both(grad_ffw_bf, grad_ffw_bf))
    grad_w_gate = dot_tn(ffw_in2, both(grad_gate[0], grad_gate[1]))
    grad_w_up = dot_tn(ffw_in2, both(grad_up[0], grad_up[1]))
    grad_w_out = dot_tn(both(attn_out[0], attn_out[1]), both(grad_proj_bf, grad_proj_bf))
    attn_in2 = both(attn_in, attn_in)

    delta = jnp.sum(grad_heads.astype(f32) * attn_heads.astype(f32), axis=-1)
    stats = jnp.stack([jnp.log2(totals[:, 0]), delta]).reshape(2, 2, 256).transpose(1, 0, 2)
    big = tuple(g.astype(bf16) for g in (grad_w_out, grad_w_gate, grad_w_up, grad_w_down))
    stats, big = lax.optimization_barrier((stats, big))
    sum_out, sum_gate, sum_up, sum_down = (g.astype(f32) for g in lax.psum(big, CTX))
    grad_query = None
    kv_terms = [None] * 4
    for d in (3, 2, 1, 0):
        grad_query, *kv_terms[d] = backward_piece(
            tables[d], query_rot, grad_heads, stats, *pieces[d], grad_query
        )
    grad_query = grad_query * HDIM**-0.5
    grad_query_raw, grad_gain_query = rms_backward(
        query_raw, query_factor, gain_query, rotate_back(grad_query, cos4, sin4)
    )
    grad_query_bf = heads_last(grad_query_raw.astype(bf16))
    grad_w_query = dot_tn(attn_in2, both(grad_query_bf[0], grad_query_bf[1]))
    sum_query = small_sum(grad_w_query.astype(bf16)).astype(f32)

    kv_mine = scatter_sum(kv_terms)
    grad_key_raw, grad_gain_key = rms_backward(
        key_raw, key_factor, gain_key, rotate_back(kv_mine[:, :HDIM], cos_tab, sin_tab)
    )
    grad_key_bf = grad_key_raw.astype(bf16)
    grad_value_bf = kv_mine[:, HDIM:].astype(bf16)

    def mine_other(full):
        a, b = full[:, :128], full[:, 128:]
        return jnp.where(first, a, b), jnp.where(first, b, a)

    key_m, key_o = mine_other(grad_key_bf)
    val_m, val_o = mine_other(grad_value_bf)
    grad_kv2 = both(
        jnp.concatenate([key_m, val_m], axis=1), jnp.concatenate([key_o, val_o], axis=1)
    )
    grad_w_kv = dot_tn(grad_kv2, attn_in2)

    grad_attn_in = (
        dot_nt(grad_query_bf[0], query_w[0])
        + dot_nt(grad_query_bf[1], query_w[1])
        + dot_nt(grad_key_bf, key_w)
        + dot_nt(grad_value_bf, value_w)
    )
    grad_in_part, grad_gain_one = rms_backward(resid_in, factor_one, gain_one, grad_attn_in)
    input_grad = grad_mid + grad_in_part

    gain_grads = (
        grad_gain_one,
        grad_gain_two,
        grad_gain_three,
        grad_gain_four,
        grad_gain_query,
        grad_gain_key,
    )
    g_own = jnp.concatenate([jnp.where(first, g[: g.size // 2], g[g.size // 2 :]) for g in gain_grads])
    g_other = jnp.concatenate([jnp.where(first, g[g.size // 2 :], g[: g.size // 2]) for g in gain_grads])
    g_sum = g_own + swap(g_other[None])[0]
    g_block = jnp.concatenate([g_sum, jnp.zeros((1024,), f32)]).reshape(64, 40).astype(bf16)
    late = jnp.concatenate([grad_w_kv.astype(bf16).reshape(64, 2560), g_block], axis=1)
    late = small_sum(late).astype(f32)
    sum_kv = late[:, :2560].reshape(256, 640)
    sum_gains = late[:, 2560:].reshape(-1)
    return (
        block_output[None],
        input_grad[None],
        sum_query,
        sum_kv[:128].T,
        sum_kv[128:].T,
        sum_out,
        sum_gate,
        sum_up,
        sum_down,
        sum_gains[:320],
        sum_gains[1280:1408],
        sum_gains[1408:1536],
        sum_gains[320:640],
        sum_gains[640:960],
        sum_gains[960:1280],
    )


def solution(mesh):
    grid = Mesh(mesh.devices.reshape(4, 4, 4, 2), ("z", "x", "y", "wsh"))
    tokens = P("wsh", CTX, None)
    cols, rows, vec = P(None, "wsh"), P("wsh", None), P("wsh")
    return jax.shard_map(
        per_device,
        mesh=grid,
        in_specs=(tokens, tokens, P(), cols, cols, cols, rows, cols, cols, rows) + (vec,) * 6,
        out_specs=(tokens, tokens, cols, cols, cols, rows, cols, cols, rows) + (vec,) * 6,
        check_vma=False,
    )
```

```python
import functools

import jax
import jax.numpy as jnp
from jax import lax
from jax.experimental import pallas as pl
from jax.experimental.pallas import tpu as pltpu
from jax.sharding import Mesh
from jax.sharding import PartitionSpec as P

HEADS = 4
HDIM = 256
CTX = ("z", "x", "y")
LOG2E = 1.4426950408889634

epsilon = 1e-06
theta_base = 1000000.0
bf16 = jnp.bfloat16
f32 = jnp.float32


def rms_forward(values, gain_w):
    factor = lax.rsqrt(jnp.mean(values * values, axis=-1, keepdims=True) + epsilon)
    return (values * factor * (1.0 + gain_w), factor)


def rms_backward(values, factor, gain_w, grad_out):
    weighted = grad_out * (1.0 + gain_w)
    inner = jnp.mean(weighted * values, axis=-1, keepdims=True)
    grad_in = factor * (weighted - values * factor * factor * inner)
    grad_gain = jnp.sum((grad_out * values * factor).reshape(-1, values.shape[-1]), axis=0)
    return (grad_in, grad_gain)


def rotary_tables(positions, width):
    half_width = width // 2
    frequency = theta_base ** (-jnp.arange(half_width, dtype=f32) * 2.0 / width)
    angles = positions.astype(f32)[:, None] * frequency[None, :]
    return (jnp.cos(angles), jnp.sin(angles))


def rotate(values, cos_tab, sin_tab):
    half = values.shape[-1] // 2
    a, b = values[..., :half], values[..., half:]
    return jnp.concatenate([a * cos_tab - b * sin_tab, b * cos_tab + a * sin_tab], axis=-1)


def rotate_back(grads, cos_tab, sin_tab):
    half = grads.shape[-1] // 2
    a, b = grads[..., :half], grads[..., half:]
    return jnp.concatenate([a * cos_tab + b * sin_tab, b * cos_tab - a * sin_tab], axis=-1)


def block_positions(block_ids, half_rows):
    offsets = jnp.arange(half_rows, dtype=jnp.int32)
    return (block_ids[:, None] * half_rows + offsets[None, :]).reshape(-1)


def dot_f32(left, right):
    return jnp.dot(left, right, preferred_element_type=f32)


def dot_nt(left, right):
    return lax.dot_general(left, right, (((1,), (1,)), ((), ())), preferred_element_type=f32)


def dot_tn(left, right):
    return lax.dot_general(left, right, (((0,), (0,)), ((), ())), preferred_element_type=f32)


def swap(values):
    return lax.ppermute(values, "wsh", [(0, 1), (1, 0)])


def load_group(table, group, kv_all):
    slots = [table[8 * group + i] for i in range(8)]
    blocks = [kv_all[pl.ds(pl.multiple_of(slot * 64, 64), 64), :] for slot in slots]
    keys = jnp.concatenate([block[:, :HDIM] for block in blocks], axis=0)
    vals = jnp.concatenate([block[:, HDIM:] for block in blocks], axis=0)
    return slots, keys, vals


def key_places(table, group, shape, dim):
    place = lax.broadcasted_iota(jnp.int32, shape, dim)
    base = jnp.full(shape, table[32 + 8 * group + 7], jnp.int32)
    for i in range(6, -1, -1):
        base = jnp.where(place < 64 * (i + 1), table[32 + 8 * group + i], base)
    return base * 64 + place % 64


def forward_kernel(first, table, q_ref, a_ref, b_ref, *rest):
    if first:
        acc_ref, tot_ref, kv_all = rest
        acc_ref[...] = jnp.zeros_like(acc_ref)
        tot_ref[...] = jnp.zeros_like(tot_ref)
    else:
        acc_in, tot_in, acc_ref, tot_ref, kv_all = rest
        acc_ref[...] = acc_in[...]
        tot_ref[...] = tot_in[...]
    kv_all[:1024, :] = a_ref[...]
    kv_all[1024:, :] = b_ref[...]

    def step(group, carry):
        _, keys, vals = load_group(table, group, kv_all)
        places = key_places(table, group, (1, 512), 1)

        def half(i):
            rows = pl.ds(pl.multiple_of(table[64 + i] * 256, 256), 256)
            mine = lax.broadcasted_iota(jnp.int32, (256, 1), 0) % 64 + table[66 + i] * 64
            scores = dot_nt(q_ref[rows, :], keys)
            probs = jnp.where(places <= mine, jnp.exp2(scores * LOG2E), 0.0)
            tot_ref[rows, :] += (probs[:, :128] + probs[:, 128:256]) + (
                probs[:, 256:384] + probs[:, 384:]
            )
            acc_ref[rows, :] += dot_f32(probs.astype(bf16), vals)

        half(0)
        pl.when(8 * group < table[69])(lambda: half(1))
        return carry

    lax.fori_loop(0, (table[68] + 7) // 8, step, 0)


def backward_kernel(first, table, q_ref, g_ref, stat_ref, a_ref, b_ref, *rest):
    if first:
        dq_ref, da_ref, db_ref, kv_all, dkv, out_all = rest
        dq_ref[...] = jnp.zeros_like(dq_ref)
    else:
        dq_in, dq_ref, da_ref, db_ref, kv_all, dkv, out_all = rest
        dq_ref[...] = dq_in[...]
    kv_all[:1024, :] = a_ref[...]
    kv_all[1024:, :] = b_ref[...]
    out_all[...] = jnp.zeros_like(out_all)

    def step(group, carry):
        slots, keys, vals = load_group(table, group, kv_all)
        places = key_places(table, group, (512, 1), 0)

        def half(i):
            rows = pl.ds(pl.multiple_of(table[64 + i] * 256, 256), 256)
            mine = lax.broadcasted_iota(jnp.int32, (1, 256), 1) % 64 + table[66 + i] * 64
            query, grads = q_ref[rows, :], g_ref[rows, :]
            stat = stat_ref[table[64 + i]]
            scores = dot_nt(keys, query) * LOG2E - stat[0:1, :]
            probs = jnp.where(places <= mine, jnp.exp2(scores), 0.0)
            grad_scores = (probs * (dot_nt(vals, grads) - stat[1:2, :])).astype(bf16)
            dq_ref[rows, :] += dot_tn(grad_scores, keys)
            return dot_f32(grad_scores, query), dot_f32(probs.astype(bf16), grads)

        grad_k, grad_v = half(0)
        dkv[:, :HDIM] = grad_k
        dkv[:, HDIM:] = grad_v

        @pl.when(8 * group < table[69])
        def _():
            more_k, more_v = half(1)
            dkv[:, :HDIM] += more_k
            dkv[:, HDIM:] += more_v

        for i, slot in enumerate(slots):
            block = dkv[64 * i : 64 * i + 64, :].astype(bf16)
            out_all[pl.ds(pl.multiple_of(slot * 64, 64), 64), :] = block
        return carry

    lax.fori_loop(0, (table[68] + 7) // 8, step, 0)
    da_ref[...] = out_all[:1024, :]
    db_ref[...] = out_all[1024:, :]


def specs(count):
    return [pl.BlockSpec(memory_space=pltpu.SMEM)] + [
        pl.BlockSpec(memory_space=pltpu.VMEM) for _ in range(count)
    ]


def forward_piece(table, query, a, b, state):
    return pl.pallas_call(
        functools.partial(forward_kernel, state is None),
        out_shape=(
            jax.ShapeDtypeStruct((512, HDIM), f32),
            jax.ShapeDtypeStruct((512, 128), f32),
        ),
        in_specs=specs(3 if state is None else 5),
        out_specs=tuple(specs(2)[1:]),
        scratch_shapes=[pltpu.VMEM((2048, 512), bf16)],
        cost_estimate=pl.CostEstimate(flops=2 * 10**9, transcendentals=0, bytes_accessed=4 * 10**6),
        input_output_aliases={} if state is None else {4: 0, 5: 1},
        name="attn_fwd",
    )(table, query, a, b, *(state or ()))


def backward_piece(table, query, grads, stats, a, b, grad_query):
    return pl.pallas_call(
        functools.partial(backward_kernel, grad_query is None),
        out_shape=(
            jax.ShapeDtypeStruct((512, HDIM), f32),
            jax.ShapeDtypeStruct((1024, 512), bf16),
            jax.ShapeDtypeStruct((1024, 512), bf16),
        ),
        in_specs=specs(5 if grad_query is None else 6),
        out_specs=tuple(specs(3)[1:]),
        scratch_shapes=[
            pltpu.VMEM((2048, 512), bf16),
            pltpu.VMEM((512, 512), f32),
            pltpu.VMEM((2048, 512), bf16),
        ],
        input_output_aliases={} if grad_query is None else {6: 0},
        name="attn_bwd",
    )(table, query, grads, stats, a, b, *(() if grad_query is None else (grad_query,)))


def shift(values, axis, by):
    perm = [
        (2 * a + w, 2 * ((a + (by if w == 0 else -by)) % 4) + w) for a in range(4) for w in range(2)
    ]
    return lax.ppermute(values, (axis, "wsh"), perm)


def ring_gather(block, axis):
    out = [block]
    for _ in range(3):
        out.append(shift(out[-1], axis, 1))
    return out


def ring_sum(parts, axis):
    moving = parts[3]
    for d in (2, 1, 0):
        moving = (shift(moving, axis, -1).astype(f32) + parts[d].astype(f32)).astype(bf16)
    return moving


def direct_gather(block, axis):
    return [block] + [shift(block, axis, d) for d in (1, 2, 3)]


def direct_sum(parts, axis):
    got = [shift(parts[d], axis, -d) for d in (1, 2, 3)]
    return sum((g.astype(f32) for g in got), parts[0].astype(f32))


def gather_near(block):
    return direct_gather(block, "z")


def gather_middle(near):
    a = ring_gather(jnp.concatenate([x[:64] for x in near]), "x")
    b = ring_gather(jnp.concatenate([x[64:] for x in near]), "y")
    return jnp.concatenate(a), jnp.concatenate(b)


def weight_sum_scatter(big, sign):
    for axis, last in (("z", False), ("x", False), ("y", True)):
        count = big.shape[0] // 4
        at = lax.axis_index(axis)

        def part(d):
            start = ((at - sign * d) % 4) * count
            return lax.dynamic_slice_in_dim(big, start, count, 0)

        if last:
            big = direct_sum([part(d) for d in range(4)], axis).astype(bf16)
        else:
            big = ring_sum([part(d) for d in range(4)], axis)
    return big


def scatter_rest(a, b):
    a = ring_sum([a[256 * d : 256 * d + 256] for d in range(4)], "x")
    b = ring_sum([b[256 * d : 256 * d + 256] for d in range(4)], "y")
    both = [
        jnp.concatenate([a[64 * d : 64 * d + 64], b[64 * d : 64 * d + 64]]) for d in range(4)
    ]
    return direct_sum(both, "z")


def piece_tables(pair_blocks, mine, sign):
    z, x, y = (lax.axis_index(name) for name in CTX)
    i = jnp.arange(128, dtype=jnp.int32)
    piece, inside = i // 32, i % 32
    color, outer, inner = inside // 16, (inside % 16) // 4, inside % 4
    at_z = (z - sign * inner) % 4
    at_x = (x - sign * jnp.where(color == 0, outer, piece)) % 4
    at_y = (y - sign * jnp.where(color == 0, piece, outer)) % 4
    source = 2 * (at_z * 16 + at_x * 4 + at_y) + color
    flat = pair_blocks.reshape(1, 128)
    hit = source[:, None] == jnp.arange(128, dtype=jnp.int32)[None]
    ids = jnp.sum(jnp.where(hit, flat, 0), axis=1).reshape(4, 32)
    rank = jnp.sum((ids[:, None, :] < ids[:, :, None]).astype(jnp.int32), axis=2)
    at = rank[:, None, :] == jnp.arange(32, dtype=jnp.int32)[None, :, None]
    slots = jnp.sum(jnp.where(at, jnp.arange(32, dtype=jnp.int32)[None, None], 0), axis=2)
    sorted_ids = jnp.sum(jnp.where(at, ids[:, None, :], 0), axis=2)
    seen = jnp.sum((ids[:, None, :] <= mine[None, :, None]).astype(jnp.int32), axis=2)
    upper = (mine[1] > mine[0]).astype(jnp.int32)
    which = jnp.stack([upper, 1 - upper])
    own = jnp.stack([jnp.max(mine), jnp.min(mine)])
    fixed = jnp.broadcast_to(jnp.concatenate([which, own])[None], (4, 4))
    seen = jnp.stack([jnp.max(seen, axis=1), jnp.min(seen, axis=1)], axis=1)
    return jnp.concatenate([slots, sorted_ids, fixed, seen], axis=1)


def small_sum(values):
    rows = values.shape[0] // 64
    got = lax.all_to_all(values.reshape(64, rows, -1), CTX, split_axis=0, concat_axis=0, tiled=True)
    mine = jnp.sum(got.astype(f32), axis=0).astype(values.dtype)
    wide = jnp.broadcast_to(mine[None], (64,) + mine.shape)
    out = lax.all_to_all(wide, CTX, split_axis=0, concat_axis=0, tiled=True)
    return out.reshape(values.shape)


def per_device(
    block_input,
    cotangent,
    pair_blocks,
    w_query,
    w_key,
    w_value,
    w_out,
    w_gate,
    w_up,
    w_down,
    attn_pre_gain,
    query_gain,
    key_gain,
    attn_post_gain,
    ffw_pre_gain,
    ffw_post_gain,
):
    rows = block_input.shape[1]
    rank = lax.axis_index(CTX)
    first = lax.axis_index("wsh") == 0

    def ordered(own, other, axis):
        return jnp.where(
            first,
            jnp.concatenate([own, other], axis=axis),
            jnp.concatenate([other, own], axis=axis),
        )

    resid_in = block_input[0].astype(f32)
    grad_top = cotangent[0]
    my_blocks = lax.dynamic_slice_in_dim(pair_blocks, rank, 1, 0)[0]
    query_pos = block_positions(my_blocks, rows // 2)
    sign = jnp.where(first, 1, -1)
    cos_tab, sin_tab = rotary_tables(query_pos, HDIM)

    kv_own = jnp.concatenate([w_key, w_value], axis=1)
    kv_other = swap(kv_own)

    def gain(own):
        own = own[None]
        return ordered(own, swap(own), 1).astype(f32)

    gain_one, gain_key = gain(attn_pre_gain), gain(key_gain)
    key_w = ordered(kv_own[:, :128], kv_other[:, :128], 1)
    value_w = ordered(kv_own[:, 128:], kv_other[:, 128:], 1)

    normed_one, factor_one = rms_forward(resid_in, gain_one)
    attn_in = normed_one.astype(bf16)
    key_raw = dot_f32(attn_in, key_w)
    value_bf = dot_f32(attn_in, value_w).astype(bf16)
    key_normed, key_factor = rms_forward(key_raw, gain_key)
    key_rot = rotate(key_normed, cos_tab, sin_tab).astype(bf16)
    near = gather_near(jnp.concatenate([key_rot, value_bf], axis=1))
    near[1], late_blocks = lax.optimization_barrier((near[1], pair_blocks))
    mine_late = lax.dynamic_slice_in_dim(late_blocks, rank, 1, 0)[0]
    tables = piece_tables(late_blocks, mine_late, sign)
    own_a, own_b = gather_middle(near)
    own_a, own_b, w_query, w_out, w_gate, w_up, w_down, gains = lax.optimization_barrier(
        (
            own_a,
            own_b,
            w_query,
            w_out,
            w_gate,
            w_up,
            w_down,
            (query_gain, attn_post_gain, ffw_pre_gain, ffw_post_gain),
        )
    )
    gain_query, gain_two, gain_three, gain_four = (gain(g) for g in gains)
    query_w = (w_query, swap(w_query))
    out_w = (w_out, swap(w_out))
    gate_w = (w_gate, swap(w_gate))
    up_w = (w_up, swap(w_up))
    down_w = (w_down, swap(w_down))

    def heads_first(pair):
        return jnp.concatenate(
            [
                part[64 * i : 64 * i + 64, HDIM * h : HDIM * (h + 1)]
                for i in range(2)
                for part in pair
                for h in range(2)
            ],
            axis=0,
        )

    def heads_last(stacked):
        def block(i, p, h):
            start = 64 * (4 * i + 2 * p + h)
            return stacked[start : start + 64]

        return tuple(
            jnp.concatenate(
                [jnp.concatenate([block(i, p, 0), block(i, p, 1)], axis=1) for i in range(2)]
            )
            for p in range(2)
        )

    def tile_heads(table):
        return jnp.concatenate([table[:64]] * HEADS + [table[64:]] * HEADS)

    cos4, sin4 = tile_heads(cos_tab), tile_heads(sin_tab)
    query_raw = heads_first(tuple(dot_f32(attn_in, half) for half in query_w))
    query_normed, query_factor = rms_forward(query_raw, gain_query)
    query_rot = (rotate(query_normed, cos4, sin4)).astype(bf16) * bf16(HDIM**-0.5)
    state = None
    pieces = [(own_a, own_b)]
    for d in range(4):
        if d < 3:
            a, b = pieces[d]
            coming = (shift(a, "y", 1), shift(b, "x", 1))
        state = forward_piece(tables[d], query_rot, *pieces[d], state)
        if d < 3:
            *coming, state = lax.optimization_barrier((*coming, state))
            pieces.append(tuple(coming))
    totals = jnp.sum(state[1], axis=1, keepdims=True)
    attn_heads = (state[0] / totals).astype(bf16)
    attn_out = heads_last(attn_heads)
    attn_proj = dot_f32(attn_out[0], out_w[0]) + dot_f32(attn_out[1], out_w[1])
    normed_two, factor_two = rms_forward(attn_proj, gain_two)
    mid = resid_in + normed_two
    normed_three, factor_three = rms_forward(mid, gain_three)
    ffw_in = normed_three.astype(bf16)

    gate = [dot_f32(ffw_in, half) for half in gate_w]
    up_val = [dot_f32(ffw_in, half) for half in up_w]
    acts = [jax.vjp(lambda inner: jax.nn.gelu(inner, approximate=True), g) for g in gate]
    hidden = [(act[0] * up).astype(bf16) for act, up in zip(acts, up_val)]
    ffw_proj = dot_f32(hidden[0], down_w[0]) + dot_f32(hidden[1], down_w[1])
    normed_four, factor_four = rms_forward(ffw_proj, gain_four)
    block_output = mid + normed_four

    grad_ffw, grad_gain_four = rms_backward(ffw_proj, factor_four, gain_four, grad_top)
    grad_ffw_bf = grad_ffw.astype(bf16)
    grad_hidden = [dot_nt(grad_ffw_bf, half) for half in down_w]
    grad_gate = [
        act[1](gh * up)[0].astype(bf16) for act, gh, up in zip(acts, grad_hidden, up_val)
    ]
    grad_up = [(gh * act[0]).astype(bf16) for act, gh in zip(acts, grad_hidden)]
    grad_ffw_in = (
        dot_nt(grad_gate[0], gate_w[0])
        + dot_nt(grad_gate[1], gate_w[1])
        + dot_nt(grad_up[0], up_w[0])
        + dot_nt(grad_up[1], up_w[1])
    )
    grad_mid_part, grad_gain_three = rms_backward(mid, factor_three, gain_three, grad_ffw_in)
    grad_mid = grad_top + grad_mid_part
    grad_proj, grad_gain_two = rms_backward(attn_proj, factor_two, gain_two, grad_mid)
    grad_proj_bf = grad_proj.astype(bf16)
    grad_attn = tuple(dot_nt(grad_proj_bf, half).astype(bf16) for half in out_w)
    grad_heads = heads_first(grad_attn)

    def both(own, other):
        return jnp.concatenate([own, swap(other)], axis=0)

    ffw_in2 = both(ffw_in, ffw_in)
    grad_w_down = dot_tn(both(hidden[0], hidden[1]), both(grad_ffw_bf, grad_ffw_bf))
    grad_w_gate = dot_tn(both(grad_gate[0], grad_gate[1]), ffw_in2)
    grad_w_up = dot_tn(both(grad_up[0], grad_up[1]), ffw_in2)
    grad_w_out = dot_tn(both(attn_out[0], attn_out[1]), both(grad_proj_bf, grad_proj_bf))
    attn_in2 = both(attn_in, attn_in)

    delta = jnp.sum(grad_heads.astype(f32) * attn_heads.astype(f32), axis=-1)
    stats = jnp.stack([jnp.log2(totals[:, 0]), delta]).reshape(2, 2, 256).transpose(1, 0, 2)
    big = jnp.concatenate(
        [g.astype(bf16) for g in (grad_w_out, grad_w_gate, grad_w_up, grad_w_down)], axis=0
    )
    stats, big = lax.optimization_barrier((stats, big))
    grad_query = None
    moving = None
    for d in (3, 2, 1, 0):
        if d < 3:
            coming = (shift(moving[0], "y", -1), shift(moving[1], "x", -1))
        grad_query, *terms = backward_piece(
            tables[d], query_rot, grad_heads, stats, *pieces[d], grad_query
        )
        if d < 3:
            terms = [(c.astype(f32) + t.astype(f32)).astype(bf16) for c, t in zip(coming, terms)]
        if d:
            *terms, grad_query = lax.optimization_barrier((*terms, grad_query))
        moving = terms
    weights_mine = weight_sum_scatter(big, sign)
    moving[0], grad_query = lax.optimization_barrier((moving[0], grad_query))
    grad_query = grad_query * HDIM**-0.5
    grad_query_raw, grad_gain_query = rms_backward(
        query_raw, query_factor, gain_query, rotate_back(grad_query, cos4, sin4)
    )
    grad_query_bf = heads_last(grad_query_raw.astype(bf16))
    grad_w_query = dot_tn(attn_in2, both(grad_query_bf[0], grad_query_bf[1]))
    sum_query = small_sum(grad_w_query.astype(bf16)).astype(f32)

    kv_mine = scatter_rest(*moving)
    weights_mine, kv_mine = lax.optimization_barrier((weights_mine, kv_mine))
    weights_all = lax.all_gather(weights_mine, CTX, axis=0, tiled=True)
    sum_out = weights_all[:512].astype(f32)
    sum_gate = weights_all[512:1536].astype(f32).T
    sum_up = weights_all[1536:2560].astype(f32).T
    sum_down = weights_all[2560:].astype(f32)
    grad_key_raw, grad_gain_key = rms_backward(
        key_raw, key_factor, gain_key, rotate_back(kv_mine[:, :HDIM], cos_tab, sin_tab)
    )
    grad_key_bf = grad_key_raw.astype(bf16)
    grad_value_bf = kv_mine[:, HDIM:].astype(bf16)

    def mine_other(full):
        a, b = full[:, :128], full[:, 128:]
        return jnp.where(first, a, b), jnp.where(first, b, a)

    key_m, key_o = mine_other(grad_key_bf)
    val_m, val_o = mine_other(grad_value_bf)
    grad_kv2 = both(
        jnp.concatenate([key_m, val_m], axis=1), jnp.concatenate([key_o, val_o], axis=1)
    )
    grad_w_kv = dot_tn(grad_kv2, attn_in2)

    grad_attn_in = (
        dot_nt(grad_query_bf[0], query_w[0])
        + dot_nt(grad_query_bf[1], query_w[1])
        + dot_nt(grad_key_bf, key_w)
        + dot_nt(grad_value_bf, value_w)
    )
    grad_in_part, grad_gain_one = rms_backward(resid_in, factor_one, gain_one, grad_attn_in)
    input_grad = grad_mid + grad_in_part

    gain_grads = (
        grad_gain_one,
        grad_gain_two,
        grad_gain_three,
        grad_gain_four,
        grad_gain_query,
        grad_gain_key,
    )
    g_own = jnp.concatenate([jnp.where(first, g[: g.size // 2], g[g.size // 2 :]) for g in gain_grads])
    g_other = jnp.concatenate([jnp.where(first, g[g.size // 2 :], g[: g.size // 2]) for g in gain_grads])
    g_sum = g_own + swap(g_other[None])[0]
    g_block = jnp.concatenate([g_sum, jnp.zeros((1024,), f32)]).reshape(64, 40).astype(bf16)
    late = jnp.concatenate([grad_w_kv.astype(bf16).reshape(64, 2560), g_block], axis=1)
    late = small_sum(late).astype(f32)
    sum_kv = late[:, :2560].reshape(256, 640)
    sum_gains = late[:, 2560:].reshape(-1)
    return (
        block_output[None],
        input_grad[None],
        sum_query,
        sum_kv[:128].T,
        sum_kv[128:].T,
        sum_out,
        sum_gate,
        sum_up,
        sum_down,
        sum_gains[:320],
        sum_gains[1280:1408],
        sum_gains[1408:1536],
        sum_gains[320:640],
        sum_gains[640:960],
        sum_gains[960:1280],
    )


def solution(mesh):
    grid = Mesh(mesh.devices.reshape(4, 4, 4, 2), ("z", "x", "y", "wsh"))
    tokens = P("wsh", CTX, None)
    cols, rows, vec = P(None, "wsh"), P("wsh", None), P("wsh")
    return jax.shard_map(
        per_device,
        mesh=grid,
        in_specs=(tokens, tokens, P(), cols, cols, cols, rows, cols, cols, rows) + (vec,) * 6,
        out_specs=(tokens, tokens, cols, cols, cols, rows, cols, cols, rows) + (vec,) * 6,
        check_vma=False,
    )
```

```python
import functools

import jax
import jax.numpy as jnp
from jax import lax
from jax.experimental import pallas as pl
from jax.experimental.pallas import tpu as pltpu
from jax.sharding import Mesh
from jax.sharding import PartitionSpec as P

HEADS = 4
HDIM = 256
CTX = ("z", "x", "y")
LOG2E = 1.4426950408889634

epsilon = 1e-06
theta_base = 1000000.0
bf16 = jnp.bfloat16
f32 = jnp.float32


def rms_forward(values, gain_w):
    factor = lax.rsqrt(jnp.mean(values * values, axis=-1, keepdims=True) + epsilon)
    return (values * factor * (1.0 + gain_w), factor)


def rms_backward(values, factor, gain_w, grad_out):
    weighted = grad_out * (1.0 + gain_w)
    inner = jnp.mean(weighted * values, axis=-1, keepdims=True)
    grad_in = factor * (weighted - values * factor * factor * inner)
    grad_gain = jnp.sum((grad_out * values * factor).reshape(-1, values.shape[-1]), axis=0)
    return (grad_in, grad_gain)


def rotary_tables(positions, width):
    half_width = width // 2
    frequency = theta_base ** (-jnp.arange(half_width, dtype=f32) * 2.0 / width)
    angles = positions.astype(f32)[:, None] * frequency[None, :]
    return (jnp.cos(angles), jnp.sin(angles))


def rotate(values, cos_tab, sin_tab):
    half = values.shape[-1] // 2
    a, b = values[..., :half], values[..., half:]
    return jnp.concatenate([a * cos_tab - b * sin_tab, b * cos_tab + a * sin_tab], axis=-1)


def rotate_back(grads, cos_tab, sin_tab):
    half = grads.shape[-1] // 2
    a, b = grads[..., :half], grads[..., half:]
    return jnp.concatenate([a * cos_tab + b * sin_tab, b * cos_tab - a * sin_tab], axis=-1)


def block_positions(block_ids, half_rows):
    offsets = jnp.arange(half_rows, dtype=jnp.int32)
    return (block_ids[:, None] * half_rows + offsets[None, :]).reshape(-1)


def dot_f32(left, right):
    return jnp.dot(left, right, preferred_element_type=f32)


def dot_nt(left, right):
    return lax.dot_general(left, right, (((1,), (1,)), ((), ())), preferred_element_type=f32)


def dot_tn(left, right):
    return lax.dot_general(left, right, (((0,), (0,)), ((), ())), preferred_element_type=f32)


def swap(values):
    return lax.ppermute(values, "wsh", [(0, 1), (1, 0)])


def load_group(table, group, kv_all):
    slots = [table[8 * group + i] for i in range(8)]
    blocks = [kv_all[pl.ds(pl.multiple_of(slot * 64, 64), 64), :] for slot in slots]
    keys = jnp.concatenate([block[:, :HDIM] for block in blocks], axis=0)
    vals = jnp.concatenate([block[:, HDIM:] for block in blocks], axis=0)
    return slots, keys, vals


def key_places(table, group, shape, dim):
    place = lax.broadcasted_iota(jnp.int32, shape, dim)
    base = jnp.full(shape, table[32 + 8 * group + 7], jnp.int32)
    for i in range(6, -1, -1):
        base = jnp.where(place < 64 * (i + 1), table[32 + 8 * group + i], base)
    return base * 64 + place % 64


def load_piece(piece, kv_all):
    for i, ref in enumerate(piece):
        kv_all[512 * i : 512 * i + 512, :] = ref[...]


def forward_kernel(first, table, q_ref, *rest):
    piece, rest = rest[:4], rest[4:]
    if first:
        acc_ref, tot_ref, kv_all = rest
        acc_ref[...] = jnp.zeros_like(acc_ref)
        tot_ref[...] = jnp.zeros_like(tot_ref)
    else:
        acc_in, tot_in, acc_ref, tot_ref, kv_all = rest
        acc_ref[...] = acc_in[...]
        tot_ref[...] = tot_in[...]
    load_piece(piece, kv_all)

    def step(group, carry):
        _, keys, vals = load_group(table, group, kv_all)
        places = key_places(table, group, (1, 512), 1)

        def half(i):
            rows = pl.ds(pl.multiple_of(table[64 + i] * 256, 256), 256)
            mine = lax.broadcasted_iota(jnp.int32, (256, 1), 0) % 64 + table[66 + i] * 64
            scores = dot_nt(q_ref[rows, :], keys)
            probs = jnp.where(places <= mine, jnp.exp2(scores * LOG2E), 0.0)
            tot_ref[rows, :] += (probs[:, :128] + probs[:, 128:256]) + (
                probs[:, 256:384] + probs[:, 384:]
            )
            acc_ref[rows, :] += dot_f32(probs.astype(bf16), vals)

        half(0)
        pl.when(8 * group < table[69])(lambda: half(1))
        return carry

    lax.fori_loop(0, (table[68] + 7) // 8, step, 0)


def backward_kernel(first, table, q_ref, g_ref, stat_ref, *rest):
    piece, rest = rest[:4], rest[4:]
    if first:
        dq_ref, *out_refs, kv_all, dkv, out_all = rest
        dq_ref[...] = jnp.zeros_like(dq_ref)
    else:
        dq_in, dq_ref, *out_refs, kv_all, dkv, out_all = rest
        dq_ref[...] = dq_in[...]
    load_piece(piece, kv_all)
    out_all[...] = jnp.zeros_like(out_all)

    def step(group, carry):
        slots, keys, vals = load_group(table, group, kv_all)
        places = key_places(table, group, (512, 1), 0)

        def half(i):
            rows = pl.ds(pl.multiple_of(table[64 + i] * 256, 256), 256)
            mine = lax.broadcasted_iota(jnp.int32, (1, 256), 1) % 64 + table[66 + i] * 64
            query, grads = q_ref[rows, :], g_ref[rows, :]
            stat = stat_ref[table[64 + i]]
            scores = dot_nt(keys, query) * LOG2E - stat[0:1, :]
            probs = jnp.where(places <= mine, jnp.exp2(scores), 0.0)
            grad_scores = (probs * (dot_nt(vals, grads) - stat[1:2, :])).astype(bf16)
            dq_ref[rows, :] += dot_tn(grad_scores, keys)
            return dot_f32(grad_scores, query), dot_f32(probs.astype(bf16), grads)

        grad_k, grad_v = half(0)
        dkv[:, :HDIM] = grad_k
        dkv[:, HDIM:] = grad_v

        @pl.when(8 * group < table[69])
        def _():
            more_k, more_v = half(1)
            dkv[:, :HDIM] += more_k
            dkv[:, HDIM:] += more_v

        for i, slot in enumerate(slots):
            block = dkv[64 * i : 64 * i + 64, :].astype(bf16)
            out_all[pl.ds(pl.multiple_of(slot * 64, 64), 64), :] = block
        return carry

    lax.fori_loop(0, (table[68] + 7) // 8, step, 0)
    for i, ref in enumerate(out_refs):
        ref[...] = out_all[512 * i : 512 * i + 512, :]


def specs(count):
    return [pl.BlockSpec(memory_space=pltpu.SMEM)] + [
        pl.BlockSpec(memory_space=pltpu.VMEM) for _ in range(count)
    ]


def forward_piece(table, query, piece, state):
    return pl.pallas_call(
        functools.partial(forward_kernel, state is None),
        out_shape=(
            jax.ShapeDtypeStruct((512, HDIM), f32),
            jax.ShapeDtypeStruct((512, 128), f32),
        ),
        in_specs=specs(5 if state is None else 7),
        out_specs=tuple(specs(2)[1:]),
        scratch_shapes=[pltpu.VMEM((2048, 512), bf16)],
        cost_estimate=pl.CostEstimate(flops=2 * 10**9, transcendentals=0, bytes_accessed=4 * 10**6),
        input_output_aliases={} if state is None else {6: 0, 7: 1},
        name="attn_fwd",
    )(table, query, *piece, *(state or ()))


def backward_piece(table, query, grads, stats, piece, grad_query):
    return pl.pallas_call(
        functools.partial(backward_kernel, grad_query is None),
        out_shape=(jax.ShapeDtypeStruct((512, HDIM), f32),)
        + (jax.ShapeDtypeStruct((512, 512), bf16),) * 4,
        in_specs=specs(7 if grad_query is None else 8),
        out_specs=tuple(specs(5)[1:]),
        scratch_shapes=[
            pltpu.VMEM((2048, 512), bf16),
            pltpu.VMEM((512, 512), f32),
            pltpu.VMEM((2048, 512), bf16),
        ],
        input_output_aliases={} if grad_query is None else {8: 0},
        name="attn_bwd",
    )(table, query, grads, stats, *piece, *(() if grad_query is None else (grad_query,)))


def weight_kernel(*refs):
    lefts, rights, out = refs[:8], refs[8:14], refs[14]
    rights = (rights[0:2], rights[2:4], rights[2:4], rights[4:6])
    start = 0
    for quarter in range(4):
        for i in range(4):
            own, other = lefts[2 * i], lefts[2 * i + 1]
            count = own.shape[1] // 4
            cols = slice(quarter * count, quarter * count + count)
            left = jnp.concatenate([own[:, cols], other[:, cols]], axis=0)
            right = jnp.concatenate([rights[i][0][...], rights[i][1][...]], axis=0)
            out[start : start + count, :] = dot_tn(left, right).astype(bf16)
            start += count


def weight_grads(lefts, rights):
    return pl.pallas_call(
        weight_kernel,
        out_shape=jax.ShapeDtypeStruct((3584, 640), bf16),
        in_specs=specs(14)[1:],
        out_specs=specs(1)[1],
        name="weight_grads",
    )(*lefts, *rights)


def shift(values, axis, by):
    perm = [
        (2 * a + w, 2 * ((a + (by if w == 0 else -by)) % 4) + w) for a in range(4) for w in range(2)
    ]
    return lax.ppermute(values, (axis, "wsh"), perm)


def ring_gather(block, axis):
    out = [block]
    for _ in range(3):
        out.append(shift(out[-1], axis, 1))
    return out


def ring_sum(parts, axis):
    moving = parts[3]
    for d in (2, 1, 0):
        moving = (shift(moving, axis, -1).astype(f32) + parts[d].astype(f32)).astype(bf16)
    return moving


def direct_gather(block, axis):
    return [block] + [shift(block, axis, d) for d in (1, 2, 3)]


def direct_sum(parts, axis):
    got = [shift(parts[d], axis, -d) for d in (1, 2, 3)]
    return sum((g.astype(f32) for g in got), parts[0].astype(f32))


def to_pairs(values):
    perm = [
        (2 * z + w, 2 * z + w) if w == z % 2 else (2 * z + w, 2 * (z ^ 1) + 1 - w)
        for z in range(4)
        for w in range(2)
    ]
    return lax.ppermute(values, ("z", "wsh"), perm)


def across(values):
    perm = [(2 * z + w, 2 * ((z + 2) % 4) + w) for z in range(4) for w in range(2)]
    return lax.ppermute(values, ("z", "wsh"), perm)


def gather_middle(near):
    a = ring_gather(jnp.concatenate([x[:64] for x in near]), "x")
    b = ring_gather(jnp.concatenate([x[64:] for x in near]), "y")
    return jnp.concatenate(a), jnp.concatenate(b)


def weight_part(big, axis, sign):
    count = big.shape[0] // 4
    at = lax.axis_index(axis)
    return lambda d: lax.dynamic_slice_in_dim(big, ((at - sign * d) % 4) * count, count, 0)


def scatter_rest(a, b):
    a = ring_sum([a[128 * d : 128 * d + 128] for d in range(4)], "x")
    b = ring_sum([b[128 * d : 128 * d + 128] for d in range(4)], "y")
    both = [jnp.concatenate([a[64 * d : 64 * d + 64], b[64 * d : 64 * d + 64]]) for d in range(2)]
    return both[0].astype(f32) + across(both[1]).astype(f32)


def piece_tables(pair_blocks, mine, sign):
    z, x, y = (lax.axis_index(name) for name in CTX)
    i = jnp.arange(128, dtype=jnp.int32)
    piece, inside = i // 32, i % 32
    color, part = inside // 16, (inside % 16) // 8
    outer, inner = (inside % 8) // 2, inside % 2
    core = (1 - sign) // 2
    sign = jnp.where(part == 0, sign, -sign)
    at_z = 2 * ((z // 2 + inner) % 2) + jnp.where(part == 0, core, 1 - core)
    at_x = (x - sign * jnp.where(color == 0, outer, piece)) % 4
    at_y = (y - sign * jnp.where(color == 0, piece, outer)) % 4
    source = 2 * (at_z * 16 + at_x * 4 + at_y) + color
    flat = pair_blocks.reshape(1, 128)
    hit = source[:, None] == jnp.arange(128, dtype=jnp.int32)[None]
    ids = jnp.sum(jnp.where(hit, flat, 0), axis=1).reshape(4, 32)
    rank = jnp.sum((ids[:, None, :] < ids[:, :, None]).astype(jnp.int32), axis=2)
    at = rank[:, None, :] == jnp.arange(32, dtype=jnp.int32)[None, :, None]
    slots = jnp.sum(jnp.where(at, jnp.arange(32, dtype=jnp.int32)[None, None], 0), axis=2)
    sorted_ids = jnp.sum(jnp.where(at, ids[:, None, :], 0), axis=2)
    seen = jnp.sum((ids[:, None, :] <= mine[None, :, None]).astype(jnp.int32), axis=2)
    upper = (mine[1] > mine[0]).astype(jnp.int32)
    which = jnp.stack([upper, 1 - upper])
    own = jnp.stack([jnp.max(mine), jnp.min(mine)])
    fixed = jnp.broadcast_to(jnp.concatenate([which, own])[None], (4, 4))
    seen = jnp.stack([jnp.max(seen, axis=1), jnp.min(seen, axis=1)], axis=1)
    return jnp.concatenate([slots, sorted_ids, fixed, seen], axis=1)


def small_sum(values):
    rows = values.shape[0] // 64
    got = lax.all_to_all(values.reshape(64, rows, -1), CTX, split_axis=0, concat_axis=0, tiled=True)
    mine = jnp.sum(got.astype(f32), axis=0).astype(values.dtype)
    wide = jnp.broadcast_to(mine[None], (64,) + mine.shape)
    out = lax.all_to_all(wide, CTX, split_axis=0, concat_axis=0, tiled=True)
    return out.reshape(values.shape)


def per_device(
    block_input,
    cotangent,
    pair_blocks,
    w_query,
    w_key,
    w_value,
    w_out,
    w_gate,
    w_up,
    w_down,
    attn_pre_gain,
    query_gain,
    key_gain,
    attn_post_gain,
    ffw_pre_gain,
    ffw_post_gain,
):
    rows = block_input.shape[1]
    core = lax.axis_index("wsh")
    first = core == 0
    rank = 32 * (lax.axis_index("z") // 2) + 16 * core
    rank = rank + 4 * lax.axis_index("x") + lax.axis_index("y")

    def ordered(own, other, axis):
        return jnp.where(
            first,
            jnp.concatenate([own, other], axis=axis),
            jnp.concatenate([other, own], axis=axis),
        )

    resid_in = to_pairs(block_input[0]).astype(f32)
    my_blocks = lax.dynamic_slice_in_dim(pair_blocks, rank, 1, 0)[0]
    query_pos = block_positions(my_blocks, rows // 2)
    sign = jnp.where(first, 1, -1)
    cos_tab, sin_tab = rotary_tables(query_pos, HDIM)

    kv_own = jnp.concatenate([w_key, w_value], axis=1)
    kv_other = swap(kv_own)

    def gain(own):
        own = own[None]
        return ordered(own, swap(own), 1).astype(f32)

    gain_one, gain_key = gain(attn_pre_gain), gain(key_gain)
    key_w = ordered(kv_own[:, :128], kv_other[:, :128], 1)
    value_w = ordered(kv_own[:, 128:], kv_other[:, 128:], 1)

    normed_one, factor_one = rms_forward(resid_in, gain_one)
    attn_in = normed_one.astype(bf16)
    key_raw = dot_f32(attn_in, key_w)
    value_bf = dot_f32(attn_in, value_w).astype(bf16)
    key_normed, key_factor = rms_forward(key_raw, gain_key)
    key_rot = rotate(key_normed, cos_tab, sin_tab).astype(bf16)
    near = [jnp.concatenate([key_rot, value_bf], axis=1)]
    near.append(across(near[0]))
    near[1], late_blocks = lax.optimization_barrier((near[1], pair_blocks))
    mine_late = lax.dynamic_slice_in_dim(late_blocks, rank, 1, 0)[0]
    tables = piece_tables(late_blocks, mine_late, sign)
    own_a, own_b = gather_middle(near)
    own_a, own_b, cotangent, w_query, w_out, w_gate, w_up, w_down, gains = lax.optimization_barrier(
        (
            own_a,
            own_b,
            cotangent,
            w_query,
            w_out,
            w_gate,
            w_up,
            w_down,
            (query_gain, attn_post_gain, ffw_pre_gain, ffw_post_gain),
        )
    )
    grad_top = to_pairs(cotangent[0])
    gain_query, gain_two, gain_three, gain_four = (gain(g) for g in gains)
    query_w = (w_query, swap(w_query))
    out_w = (w_out, swap(w_out))
    gate_w = (w_gate, swap(w_gate))
    up_w = (w_up, swap(w_up))
    down_w = (w_down, swap(w_down))

    def heads_first(pair):
        return jnp.concatenate(
            [
                part[64 * i : 64 * i + 64, HDIM * h : HDIM * (h + 1)]
                for i in range(2)
                for part in pair
                for h in range(2)
            ],
            axis=0,
        )

    def heads_last(stacked):
        def block(i, p, h):
            start = 64 * (4 * i + 2 * p + h)
            return stacked[start : start + 64]

        return tuple(
            jnp.concatenate(
                [jnp.concatenate([block(i, p, 0), block(i, p, 1)], axis=1) for i in range(2)]
            )
            for p in range(2)
        )

    def tile_heads(table):
        return jnp.concatenate([table[:64]] * HEADS + [table[64:]] * HEADS)

    cos4, sin4 = tile_heads(cos_tab), tile_heads(sin_tab)
    query_raw = heads_first(tuple(dot_f32(attn_in, half) for half in query_w))
    query_normed, query_factor = rms_forward(query_raw, gain_query)
    query_rot = (rotate(query_normed, cos4, sin4)).astype(bf16) * bf16(HDIM**-0.5)
    state = None
    a, b = own_a, own_b
    pieces = []
    for d in range(4):
        pieces.append((a, swap(a), b, swap(b)))
        if d < 3:
            coming = (shift(a, "y", 1), shift(b, "x", 1))
        state = forward_piece(tables[d], query_rot, pieces[d], state)
        if d < 3:
            a, b, state = lax.optimization_barrier((*coming, state))
    totals = jnp.sum(state[1], axis=1, keepdims=True)
    attn_heads = (state[0] / totals).astype(bf16)
    attn_out = heads_last(attn_heads)
    attn_proj = dot_f32(attn_out[0], out_w[0]) + dot_f32(attn_out[1], out_w[1])
    normed_two, factor_two = rms_forward(attn_proj, gain_two)
    mid = resid_in + normed_two
    normed_three, factor_three = rms_forward(mid, gain_three)
    ffw_in = normed_three.astype(bf16)

    gate = [dot_f32(ffw_in, half) for half in gate_w]
    up_val = [dot_f32(ffw_in, half) for half in up_w]
    acts = [jax.vjp(lambda inner: jax.nn.gelu(inner, approximate=True), g) for g in gate]
    hidden = [(act[0] * up).astype(bf16) for act, up in zip(acts, up_val)]
    ffw_proj = dot_f32(hidden[0], down_w[0]) + dot_f32(hidden[1], down_w[1])
    normed_four, factor_four = rms_forward(ffw_proj, gain_four)
    block_output = mid + normed_four

    grad_ffw, grad_gain_four = rms_backward(ffw_proj, factor_four, gain_four, grad_top)
    grad_ffw_bf = grad_ffw.astype(bf16)
    grad_hidden = [dot_nt(grad_ffw_bf, half) for half in down_w]
    grad_gate = [
        act[1](gh * up)[0].astype(bf16) for act, gh, up in zip(acts, grad_hidden, up_val)
    ]
    grad_up = [(gh * act[0]).astype(bf16) for act, gh in zip(acts, grad_hidden)]
    grad_ffw_in = (
        dot_nt(grad_gate[0], gate_w[0])
        + dot_nt(grad_gate[1], gate_w[1])
        + dot_nt(grad_up[0], up_w[0])
        + dot_nt(grad_up[1], up_w[1])
    )
    grad_mid_part, grad_gain_three = rms_backward(mid, factor_three, gain_three, grad_ffw_in)
    grad_mid = grad_top + grad_mid_part
    grad_proj, grad_gain_two = rms_backward(attn_proj, factor_two, gain_two, grad_mid)
    grad_proj_bf = grad_proj.astype(bf16)
    grad_attn = tuple(dot_nt(grad_proj_bf, half).astype(bf16) for half in out_w)
    grad_heads = heads_first(grad_attn)

    def both(own, other):
        return jnp.concatenate([own, swap(other)], axis=0)

    ffw_in_p, grad_ffw_p, grad_proj_p = swap(ffw_in), swap(grad_ffw_bf), swap(grad_proj_bf)
    big = weight_grads(
        (
            attn_out[0],
            swap(attn_out[1]),
            grad_gate[0],
            swap(grad_gate[1]),
            grad_up[0],
            swap(grad_up[1]),
            hidden[0],
            swap(hidden[1]),
        ),
        (grad_proj_bf, grad_proj_p, ffw_in, ffw_in_p, grad_ffw_bf, grad_ffw_p),
    )
    attn_in2 = both(attn_in, attn_in)

    delta = jnp.sum(grad_heads.astype(f32) * attn_heads.astype(f32), axis=-1)
    stats = jnp.stack([jnp.log2(totals[:, 0]), delta]).reshape(2, 2, 256).transpose(1, 0, 2)
    stats, big = lax.optimization_barrier((stats, big))
    grad_query = None
    moving = None
    part = weight_part(big, "z", sign)
    weights = None
    for d in (3, 2, 1, 0):
        if d < 3:
            coming = (shift(moving[0], "y", -1), shift(moving[1], "x", -1))
            weights_in = shift(weights, "z", -1)
        grad_query, a, a_p, b, b_p = backward_piece(
            tables[d], query_rot, grad_heads, stats, pieces[d], grad_query
        )
        terms = [a.astype(f32) + swap(a_p).astype(f32), b.astype(f32) + swap(b_p).astype(f32)]
        if d < 3:
            terms = [c.astype(f32) + t for c, t in zip(coming, terms)]
            weights = (weights_in.astype(f32) + part(d).astype(f32)).astype(bf16)
        else:
            weights = part(3)
        moving = [t.astype(bf16) for t in terms]
        if d:
            *moving, grad_query = lax.optimization_barrier((*moving, grad_query))
    grad_query = grad_query * HDIM**-0.5
    grad_query_raw, grad_gain_query = rms_backward(
        query_raw, query_factor, gain_query, rotate_back(grad_query, cos4, sin4)
    )
    grad_query_bf = heads_last(grad_query_raw.astype(bf16))
    grad_w_query = dot_tn(both(grad_query_bf[0], grad_query_bf[1]), attn_in2).astype(bf16)
    part = weight_part(grad_w_query, "z", sign)
    mine_q = direct_sum([part(d) for d in range(4)], "z").astype(bf16)
    part = weight_part(jnp.concatenate([weights, mine_q], axis=0), "x", sign)
    weights = ring_sum([part(d) for d in range(4)], "x")
    part = weight_part(weights, "y", sign)
    weights_mine = direct_sum([part(d) for d in range(4)], "y").astype(bf16)

    kv_mine = scatter_rest(*moving)
    weights_mine, kv_mine = lax.optimization_barrier((weights_mine, kv_mine))
    weights_all = lax.all_gather(weights_mine, CTX, axis=0, tiled=True).reshape(4, 1024, 640)

    def summed(start, count):
        return weights_all[:, start : start + count].reshape(4 * count, 640).astype(f32)

    sum_out, sum_gate, sum_up = summed(0, 128), summed(128, 256).T, summed(384, 256).T
    sum_down, sum_query = summed(640, 256), summed(896, 128).T
    grad_key_raw, grad_gain_key = rms_backward(
        key_raw, key_factor, gain_key, rotate_back(kv_mine[:, :HDIM], cos_tab, sin_tab)
    )
    grad_key_bf = grad_key_raw.astype(bf16)
    grad_value_bf = kv_mine[:, HDIM:].astype(bf16)

    def mine_other(full):
        a, b = full[:, :128], full[:, 128:]
        return jnp.where(first, a, b), jnp.where(first, b, a)

    key_m, key_o = mine_other(grad_key_bf)
    val_m, val_o = mine_other(grad_value_bf)
    grad_kv2 = both(
        jnp.concatenate([key_m, val_m], axis=1), jnp.concatenate([key_o, val_o], axis=1)
    )
    grad_w_kv = dot_tn(grad_kv2, attn_in2)

    grad_attn_in = (
        dot_nt(grad_query_bf[0], query_w[0])
        + dot_nt(grad_query_bf[1], query_w[1])
        + dot_nt(grad_key_bf, key_w)
        + dot_nt(grad_value_bf, value_w)
    )
    grad_in_part, grad_gain_one = rms_backward(resid_in, factor_one, gain_one, grad_attn_in)
    input_grad = grad_mid + grad_in_part

    gain_grads = (
        grad_gain_one,
        grad_gain_two,
        grad_gain_three,
        grad_gain_four,
        grad_gain_query,
        grad_gain_key,
    )
    g_own = jnp.concatenate([jnp.where(first, g[: g.size // 2], g[g.size // 2 :]) for g in gain_grads])
    g_other = jnp.concatenate([jnp.where(first, g[g.size // 2 :], g[: g.size // 2]) for g in gain_grads])
    g_sum = g_own + swap(g_other[None])[0]
    g_block = jnp.concatenate([g_sum, jnp.zeros((1024,), f32)]).reshape(64, 40).astype(bf16)
    late = jnp.concatenate([grad_w_kv.astype(bf16).reshape(64, 2560), g_block], axis=1)
    late = small_sum(late).astype(f32)
    sum_kv = late[:, :2560].reshape(256, 640)
    sum_gains = late[:, 2560:].reshape(-1)
    return (
        to_pairs(block_output)[None],
        to_pairs(input_grad)[None],
        sum_query,
        sum_kv[:128].T,
        sum_kv[128:].T,
        sum_out,
        sum_gate,
        sum_up,
        sum_down,
        sum_gains[:320],
        sum_gains[1280:1408],
        sum_gains[1408:1536],
        sum_gains[320:640],
        sum_gains[640:960],
        sum_gains[960:1280],
    )


def solution(mesh):
    grid = Mesh(mesh.devices.reshape(4, 4, 4, 2), ("z", "x", "y", "wsh"))
    tokens = P("wsh", CTX, None)
    cols, rows, vec = P(None, "wsh"), P("wsh", None), P("wsh")
    return jax.shard_map(
        per_device,
        mesh=grid,
        in_specs=(tokens, tokens, P(), cols, cols, cols, rows, cols, cols, rows) + (vec,) * 6,
        out_specs=(tokens, tokens, cols, cols, cols, rows, cols, cols, rows) + (vec,) * 6,
        check_vma=False,
    )
```

```python
import functools

import jax
import jax.numpy as jnp
from jax import lax
from jax.experimental import pallas as pl
from jax.experimental.pallas import tpu as pltpu
from jax.sharding import Mesh
from jax.sharding import PartitionSpec as P

HEADS = 4
HDIM = 256
CTX = ("z", "x", "y")
LOG2E = 1.4426950408889634

epsilon = 1e-06
theta_base = 1000000.0
bf16 = jnp.bfloat16
f32 = jnp.float32


def rms_forward(values, gain_w):
    factor = lax.rsqrt(jnp.mean(values * values, axis=-1, keepdims=True) + epsilon)
    return (values * factor * (1.0 + gain_w), factor)


def rms_backward(values, factor, gain_w, grad_out):
    weighted = grad_out * (1.0 + gain_w)
    inner = jnp.mean(weighted * values, axis=-1, keepdims=True)
    grad_in = factor * (weighted - values * factor * factor * inner)
    grad_gain = jnp.sum((grad_out * values * factor).reshape(-1, values.shape[-1]), axis=0)
    return (grad_in, grad_gain)


def rotary_tables(positions, width):
    half_width = width // 2
    frequency = theta_base ** (-jnp.arange(half_width, dtype=f32) * 2.0 / width)
    angles = positions.astype(f32)[:, None] * frequency[None, :]
    return (jnp.cos(angles), jnp.sin(angles))


def rotate(values, cos_tab, sin_tab):
    half = values.shape[-1] // 2
    a, b = values[..., :half], values[..., half:]
    return jnp.concatenate([a * cos_tab - b * sin_tab, b * cos_tab + a * sin_tab], axis=-1)


def rotate_back(grads, cos_tab, sin_tab):
    half = grads.shape[-1] // 2
    a, b = grads[..., :half], grads[..., half:]
    return jnp.concatenate([a * cos_tab + b * sin_tab, b * cos_tab - a * sin_tab], axis=-1)


def block_positions(block_ids, half_rows):
    offsets = jnp.arange(half_rows, dtype=jnp.int32)
    return (block_ids[:, None] * half_rows + offsets[None, :]).reshape(-1)


def dot_f32(left, right):
    return jnp.dot(left, right, preferred_element_type=f32)


def dot_nt(left, right):
    return lax.dot_general(left, right, (((1,), (1,)), ((), ())), preferred_element_type=f32)


def dot_tn(left, right):
    return lax.dot_general(left, right, (((0,), (0,)), ((), ())), preferred_element_type=f32)


def swap(values):
    return lax.ppermute(values, "wsh", [(0, 1), (1, 0)])


def load_group(table, group, kv_all):
    slots = [table[8 * group + i] for i in range(8)]
    blocks = [kv_all[pl.ds(pl.multiple_of(slot * 64, 64), 64), :] for slot in slots]
    keys = jnp.concatenate([block[:, :HDIM] for block in blocks], axis=0)
    vals = jnp.concatenate([block[:, HDIM:] for block in blocks], axis=0)
    return slots, keys, vals


def key_places(table, group, shape, dim):
    place = lax.broadcasted_iota(jnp.int32, shape, dim)
    base = jnp.full(shape, table[32 + 8 * group + 7], jnp.int32)
    for i in range(6, -1, -1):
        base = jnp.where(place < 64 * (i + 1), table[32 + 8 * group + i], base)
    return base * 64 + place % 64


def load_piece(piece, kv_all):
    for i, ref in enumerate(piece):
        kv_all[512 * i : 512 * i + 512, :] = ref[...]


def forward_kernel(first, table, q_ref, *rest):
    piece, rest = rest[:4], rest[4:]
    if first:
        acc_ref, tot_ref, kv_all = rest
        acc_ref[...] = jnp.zeros_like(acc_ref)
        tot_ref[...] = jnp.zeros_like(tot_ref)
    else:
        acc_in, tot_in, acc_ref, tot_ref, kv_all = rest
        acc_ref[...] = acc_in[...]
        tot_ref[...] = tot_in[...]
    load_piece(piece, kv_all)

    def step(group, carry):
        _, keys, vals = load_group(table, group, kv_all)
        places = key_places(table, group, (1, 512), 1)

        def half(i):
            rows = pl.ds(pl.multiple_of(table[64 + i] * 256, 256), 256)
            mine = lax.broadcasted_iota(jnp.int32, (256, 1), 0) % 64 + table[66 + i] * 64
            scores = dot_nt(q_ref[rows, :], keys)
            probs = jnp.where(places <= mine, jnp.exp2(scores * LOG2E), 0.0)
            tot_ref[rows, :] += (probs[:, :128] + probs[:, 128:256]) + (
                probs[:, 256:384] + probs[:, 384:]
            )
            acc_ref[rows, :] += dot_f32(probs.astype(bf16), vals)

        half(0)
        pl.when(8 * group < table[69])(lambda: half(1))
        return carry

    lax.fori_loop(0, (table[68] + 7) // 8, step, 0)


def backward_kernel(first, table, q_ref, g_ref, stat_ref, *rest):
    piece, rest = rest[:4], rest[4:]
    if first:
        dq_ref, *out_refs, kv_all, dkv, out_all = rest
        dq_ref[...] = jnp.zeros_like(dq_ref)
    else:
        dq_in, dq_ref, *out_refs, kv_all, dkv, out_all = rest
        dq_ref[...] = dq_in[...]
    load_piece(piece, kv_all)
    out_all[...] = jnp.zeros_like(out_all)

    def step(group, carry):
        slots, keys, vals = load_group(table, group, kv_all)
        places = key_places(table, group, (512, 1), 0)

        def half(i):
            rows = pl.ds(pl.multiple_of(table[64 + i] * 256, 256), 256)
            mine = lax.broadcasted_iota(jnp.int32, (1, 256), 1) % 64 + table[66 + i] * 64
            query, grads = q_ref[rows, :], g_ref[rows, :]
            stat = stat_ref[table[64 + i]]
            scores = dot_nt(keys, query) * LOG2E - stat[0:1, :]
            probs = jnp.where(places <= mine, jnp.exp2(scores), 0.0)
            grad_scores = (probs * (dot_nt(vals, grads) - stat[1:2, :])).astype(bf16)
            dq_ref[rows, :] += dot_tn(grad_scores, keys)
            return dot_f32(grad_scores, query), dot_f32(probs.astype(bf16), grads)

        grad_k, grad_v = half(0)
        dkv[:, :HDIM] = grad_k
        dkv[:, HDIM:] = grad_v

        @pl.when(8 * group < table[69])
        def _():
            more_k, more_v = half(1)
            dkv[:, :HDIM] += more_k
            dkv[:, HDIM:] += more_v

        for i, slot in enumerate(slots):
            block = dkv[64 * i : 64 * i + 64, :].astype(bf16)
            out_all[pl.ds(pl.multiple_of(slot * 64, 64), 64), :] = block
        return carry

    lax.fori_loop(0, (table[68] + 7) // 8, step, 0)
    for i, ref in enumerate(out_refs):
        ref[...] = out_all[512 * i : 512 * i + 512, :]


def specs(count):
    return [pl.BlockSpec(memory_space=pltpu.SMEM)] + [
        pl.BlockSpec(memory_space=pltpu.VMEM) for _ in range(count)
    ]


def forward_piece(table, query, piece, state):
    return pl.pallas_call(
        functools.partial(forward_kernel, state is None),
        out_shape=(
            jax.ShapeDtypeStruct((512, HDIM), f32),
            jax.ShapeDtypeStruct((512, 128), f32),
        ),
        in_specs=specs(5 if state is None else 7),
        out_specs=tuple(specs(2)[1:]),
        scratch_shapes=[pltpu.VMEM((2048, 512), bf16)],
        cost_estimate=pl.CostEstimate(flops=2 * 10**9, transcendentals=0, bytes_accessed=4 * 10**6),
        input_output_aliases={} if state is None else {6: 0, 7: 1},
        name="attn_fwd",
    )(table, query, *piece, *(state or ()))


def backward_piece(table, query, grads, stats, piece, grad_query):
    return pl.pallas_call(
        functools.partial(backward_kernel, grad_query is None),
        out_shape=(jax.ShapeDtypeStruct((512, HDIM), f32),)
        + (jax.ShapeDtypeStruct((512, 512), bf16),) * 4,
        in_specs=specs(7 if grad_query is None else 8),
        out_specs=tuple(specs(5)[1:]),
        scratch_shapes=[
            pltpu.VMEM((2048, 512), bf16),
            pltpu.VMEM((512, 512), f32),
            pltpu.VMEM((2048, 512), bf16),
        ],
        input_output_aliases={} if grad_query is None else {8: 0},
        name="attn_bwd",
    )(table, query, grads, stats, *piece, *(() if grad_query is None else (grad_query,)))


def weight_kernel(*refs):
    lefts, rights, out = refs[:8], refs[8:14], refs[14]
    rights = (rights[0:2], rights[2:4], rights[2:4], rights[4:6])
    start = 0
    for quarter in range(4):
        for i in range(4):
            own, other = lefts[2 * i], lefts[2 * i + 1]
            count = own.shape[1] // 4
            cols = slice(quarter * count, quarter * count + count)
            left = jnp.concatenate([own[:, cols], other[:, cols]], axis=0)
            right = jnp.concatenate([rights[i][0][...], rights[i][1][...]], axis=0)
            out[start : start + count, :] = dot_tn(left, right).astype(bf16)
            start += count


def weight_grads(lefts, rights):
    return pl.pallas_call(
        weight_kernel,
        out_shape=jax.ShapeDtypeStruct((3584, 640), bf16),
        in_specs=specs(14)[1:],
        out_specs=specs(1)[1],
        name="weight_grads",
    )(*lefts, *rights)


def shift(values, axis, by):
    perm = [
        (2 * a + w, 2 * ((a + (by if w == 0 else -by)) % 4) + w) for a in range(4) for w in range(2)
    ]
    return lax.ppermute(values, (axis, "wsh"), perm)


def ring_gather(block, axis):
    out = [block]
    for _ in range(3):
        out.append(shift(out[-1], axis, 1))
    return out


def ring_sum(parts, axis):
    moving = parts[3]
    for d in (2, 1, 0):
        moving = (shift(moving, axis, -1).astype(f32) + parts[d].astype(f32)).astype(bf16)
    return moving


def direct_gather(block, axis):
    return [block] + [shift(block, axis, d) for d in (1, 2, 3)]


def direct_sum(parts, axis):
    got = [shift(parts[d], axis, -d) for d in (1, 2, 3)]
    return sum((g.astype(f32) for g in got), parts[0].astype(f32))


def to_pairs(values):
    perm = [
        (2 * z + w, 2 * z + w) if w == z % 2 else (2 * z + w, 2 * (z ^ 1) + 1 - w)
        for z in range(4)
        for w in range(2)
    ]
    return lax.ppermute(values, ("z", "wsh"), perm)


def across(values):
    perm = [(2 * z + w, 2 * ((z + 2) % 4) + w) for z in range(4) for w in range(2)]
    return lax.ppermute(values, ("z", "wsh"), perm)


def gather_middle(near):
    a = ring_gather(jnp.concatenate([x[:64] for x in near]), "x")
    b = ring_gather(jnp.concatenate([x[64:] for x in near]), "y")
    return jnp.concatenate(a), jnp.concatenate(b)


def weight_part(big, axis, sign):
    count = big.shape[0] // 4
    at = lax.axis_index(axis)
    return lambda d: lax.dynamic_slice_in_dim(big, ((at - sign * d) % 4) * count, count, 0)


def tie(*values):
    return lax.optimization_barrier(values)


def plus(left, right):
    return (left.astype(f32) + right.astype(f32)).astype(bf16)


def piece_tables(pair_blocks, mine, sign):
    z, x, y = (lax.axis_index(name) for name in CTX)
    i = jnp.arange(128, dtype=jnp.int32)
    piece, inside = i // 32, i % 32
    color, part = inside // 16, (inside % 16) // 8
    outer, inner = (inside % 8) // 2, inside % 2
    core = (1 - sign) // 2
    sign = jnp.where(part == 0, sign, -sign)
    at_z = 2 * ((z // 2 + inner) % 2) + jnp.where(part == 0, core, 1 - core)
    at_x = (x - sign * jnp.where(color == 0, outer, piece)) % 4
    at_y = (y - sign * jnp.where(color == 0, piece, outer)) % 4
    source = 2 * (at_z * 16 + at_x * 4 + at_y) + color
    flat = pair_blocks.reshape(1, 128)
    hit = source[:, None] == jnp.arange(128, dtype=jnp.int32)[None]
    ids = jnp.sum(jnp.where(hit, flat, 0), axis=1).reshape(4, 32)
    rank = jnp.sum((ids[:, None, :] < ids[:, :, None]).astype(jnp.int32), axis=2)
    at = rank[:, None, :] == jnp.arange(32, dtype=jnp.int32)[None, :, None]
    slots = jnp.sum(jnp.where(at, jnp.arange(32, dtype=jnp.int32)[None, None], 0), axis=2)
    sorted_ids = jnp.sum(jnp.where(at, ids[:, None, :], 0), axis=2)
    seen = jnp.sum((ids[:, None, :] <= mine[None, :, None]).astype(jnp.int32), axis=2)
    upper = (mine[1] > mine[0]).astype(jnp.int32)
    which = jnp.stack([upper, 1 - upper])
    own = jnp.stack([jnp.max(mine), jnp.min(mine)])
    fixed = jnp.broadcast_to(jnp.concatenate([which, own])[None], (4, 4))
    seen = jnp.stack([jnp.max(seen, axis=1), jnp.min(seen, axis=1)], axis=1)
    return jnp.concatenate([slots, sorted_ids, fixed, seen], axis=1)


def chunk_sum(values):
    got = lax.all_to_all(values, CTX, split_axis=0, concat_axis=0, tiled=True)
    return jnp.sum(got.astype(f32), axis=0)


def chunk_gather(values):
    wide = jnp.broadcast_to(values[None], (64,) + values.shape)
    return lax.all_to_all(wide, CTX, split_axis=0, concat_axis=0, tiled=True)


def per_device(
    block_input,
    cotangent,
    pair_blocks,
    w_query,
    w_key,
    w_value,
    w_out,
    w_gate,
    w_up,
    w_down,
    attn_pre_gain,
    query_gain,
    key_gain,
    attn_post_gain,
    ffw_pre_gain,
    ffw_post_gain,
):
    rows = block_input.shape[1]
    core = lax.axis_index("wsh")
    first = core == 0
    rank = 32 * (lax.axis_index("z") // 2) + 16 * core
    rank = rank + 4 * lax.axis_index("x") + lax.axis_index("y")

    def ordered(own, other, axis):
        return jnp.where(
            first,
            jnp.concatenate([own, other], axis=axis),
            jnp.concatenate([other, own], axis=axis),
        )

    resid_in = to_pairs(block_input[0]).astype(f32)
    my_blocks = lax.dynamic_slice_in_dim(pair_blocks, rank, 1, 0)[0]
    query_pos = block_positions(my_blocks, rows // 2)
    sign = jnp.where(first, 1, -1)
    cos_tab, sin_tab = rotary_tables(query_pos, HDIM)

    kv_own = jnp.concatenate([w_key, w_value], axis=1)
    kv_other = swap(kv_own)

    def gain(own):
        own = own[None]
        return ordered(own, swap(own), 1).astype(f32)

    gain_one, gain_key = gain(attn_pre_gain), gain(key_gain)
    key_w = ordered(kv_own[:, :128], kv_other[:, :128], 1)
    value_w = ordered(kv_own[:, 128:], kv_other[:, 128:], 1)

    normed_one, factor_one = rms_forward(resid_in, gain_one)
    attn_in = normed_one.astype(bf16)
    key_raw = dot_f32(attn_in, key_w)
    value_bf = dot_f32(attn_in, value_w).astype(bf16)
    key_normed, key_factor = rms_forward(key_raw, gain_key)
    key_rot = rotate(key_normed, cos_tab, sin_tab).astype(bf16)
    near = [jnp.concatenate([key_rot, value_bf], axis=1)]
    near.append(across(near[0]))
    near[1], late_blocks = lax.optimization_barrier((near[1], pair_blocks))
    mine_late = lax.dynamic_slice_in_dim(late_blocks, rank, 1, 0)[0]
    tables = piece_tables(late_blocks, mine_late, sign)
    own_a, own_b = gather_middle(near)
    own_a, own_b, cotangent, w_query, w_out, w_gate, w_up, w_down, gains = lax.optimization_barrier(
        (
            own_a,
            own_b,
            cotangent,
            w_query,
            w_out,
            w_gate,
            w_up,
            w_down,
            (query_gain, attn_post_gain, ffw_pre_gain, ffw_post_gain),
        )
    )
    grad_top = to_pairs(cotangent[0])
    gain_query, gain_two, gain_three, gain_four = (gain(g) for g in gains)
    query_w = (w_query, swap(w_query))
    out_w = (w_out, swap(w_out))
    gate_w = (w_gate, swap(w_gate))
    up_w = (w_up, swap(w_up))
    down_w = (w_down, swap(w_down))

    def heads_first(pair):
        return jnp.concatenate(
            [
                part[64 * i : 64 * i + 64, HDIM * h : HDIM * (h + 1)]
                for i in range(2)
                for part in pair
                for h in range(2)
            ],
            axis=0,
        )

    def heads_last(stacked):
        def block(i, p, h):
            start = 64 * (4 * i + 2 * p + h)
            return stacked[start : start + 64]

        return tuple(
            jnp.concatenate(
                [jnp.concatenate([block(i, p, 0), block(i, p, 1)], axis=1) for i in range(2)]
            )
            for p in range(2)
        )

    def tile_heads(table):
        return jnp.concatenate([table[:64]] * HEADS + [table[64:]] * HEADS)

    cos4, sin4 = tile_heads(cos_tab), tile_heads(sin_tab)
    query_raw = heads_first(tuple(dot_f32(attn_in, half) for half in query_w))
    query_normed, query_factor = rms_forward(query_raw, gain_query)
    query_rot = (rotate(query_normed, cos4, sin4)).astype(bf16) * bf16(HDIM**-0.5)
    state = None
    a, b = own_a, own_b
    pieces = []
    for d in range(4):
        pieces.append((a, swap(a), b, swap(b)))
        if d < 3:
            coming = (shift(a, "y", 1), shift(b, "x", 1))
        state = forward_piece(tables[d], query_rot, pieces[d], state)
        if d < 3:
            a, b, state = lax.optimization_barrier((*coming, state))
    totals = jnp.sum(state[1], axis=1, keepdims=True)
    attn_heads = (state[0] / totals).astype(bf16)
    attn_out = heads_last(attn_heads)
    attn_proj = dot_f32(attn_out[0], out_w[0]) + dot_f32(attn_out[1], out_w[1])
    normed_two, factor_two = rms_forward(attn_proj, gain_two)
    mid = resid_in + normed_two
    normed_three, factor_three = rms_forward(mid, gain_three)
    ffw_in = normed_three.astype(bf16)

    gate = [dot_f32(ffw_in, half) for half in gate_w]
    up_val = [dot_f32(ffw_in, half) for half in up_w]
    acts = [jax.vjp(lambda inner: jax.nn.gelu(inner, approximate=True), g) for g in gate]
    hidden = [(act[0] * up).astype(bf16) for act, up in zip(acts, up_val)]
    ffw_proj = dot_f32(hidden[0], down_w[0]) + dot_f32(hidden[1], down_w[1])
    normed_four, factor_four = rms_forward(ffw_proj, gain_four)
    block_output = mid + normed_four

    grad_ffw, grad_gain_four = rms_backward(ffw_proj, factor_four, gain_four, grad_top)
    grad_ffw_bf = grad_ffw.astype(bf16)
    grad_hidden = [dot_nt(grad_ffw_bf, half) for half in down_w]
    grad_gate = [
        act[1](gh * up)[0].astype(bf16) for act, gh, up in zip(acts, grad_hidden, up_val)
    ]
    grad_up = [(gh * act[0]).astype(bf16) for act, gh in zip(acts, grad_hidden)]
    grad_ffw_in = (
        dot_nt(grad_gate[0], gate_w[0])
        + dot_nt(grad_gate[1], gate_w[1])
        + dot_nt(grad_up[0], up_w[0])
        + dot_nt(grad_up[1], up_w[1])
    )
    grad_mid_part, grad_gain_three = rms_backward(mid, factor_three, gain_three, grad_ffw_in)
    grad_mid = grad_top + grad_mid_part
    grad_proj, grad_gain_two = rms_backward(attn_proj, factor_two, gain_two, grad_mid)
    grad_proj_bf = grad_proj.astype(bf16)
    grad_attn = tuple(dot_nt(grad_proj_bf, half).astype(bf16) for half in out_w)
    grad_heads = heads_first(grad_attn)

    def both(own, other):
        return jnp.concatenate([own, swap(other)], axis=0)

    ffw_in_p, grad_ffw_p, grad_proj_p = swap(ffw_in), swap(grad_ffw_bf), swap(grad_proj_bf)
    big = weight_grads(
        (
            attn_out[0],
            swap(attn_out[1]),
            grad_gate[0],
            swap(grad_gate[1]),
            grad_up[0],
            swap(grad_up[1]),
            hidden[0],
            swap(hidden[1]),
        ),
        (grad_proj_bf, grad_proj_p, ffw_in, ffw_in_p, grad_ffw_bf, grad_ffw_p),
    )
    attn_in2 = both(attn_in, attn_in)

    delta = jnp.sum(grad_heads.astype(f32) * attn_heads.astype(f32), axis=-1)
    stats = jnp.stack([jnp.log2(totals[:, 0]), delta]).reshape(2, 2, 256).transpose(1, 0, 2)
    stats, big = lax.optimization_barrier((stats, big))
    grad_query = None
    moving = None
    weights = big
    rounds = [("z", 2), ("z", 1), ("z", 0), ("x", 2), ("x", 1), ("x", 0)]
    part = weight_part(big, "z", sign)
    weights = part(3)

    def weight_round(weights, part, step):
        axis, d = rounds[step]
        weights = plus(shift(weights, axis, -1), part(d))
        if d == 0 and axis == "z":
            part = weight_part(weights, "x", sign)
            weights = part(3)
        return weights, part

    for step, d in enumerate((3, 2, 1, 0)):
        if d < 3:
            coming = (shift(moving[0], "y", -1), shift(moving[1], "x", -1))
        weights, part = weight_round(weights, part, step)
        grad_query, a, a_p, b, b_p = backward_piece(
            tables[d], query_rot, grad_heads, stats, pieces[d], grad_query
        )
        terms = [a.astype(f32) + swap(a_p).astype(f32), b.astype(f32) + swap(b_p).astype(f32)]
        if d < 3:
            terms = [c.astype(f32) + t for c, t in zip(coming, terms)]
        moving = [t.astype(bf16) for t in terms]
        if d:
            *moving, grad_query, weights = tie(*moving, grad_query, weights)
    all_a, all_b = moving
    a, b, weights = tie(all_a[384:], all_b[384:], weights)
    for d in (2, 1, 0):
        rows_d = slice(128 * d, 128 * d + 128)
        a = plus(shift(a, "x", -1), all_a[rows_d])
        b = plus(shift(b, "y", -1), all_b[rows_d])
        if d:
            weights, part = weight_round(weights, part, 6 - d)
        else:
            part = weight_part(weights, "y", sign)
            weights_mine = direct_sum([part(i) for i in range(4)], "y").astype(bf16)
        if d:
            a, b, weights = tie(a, b, weights)
    weights_all = lax.all_gather(weights_mine, CTX, axis=0, tiled=True)
    kv_far = jnp.concatenate([a[64:], b[64:]])
    kv_mine = jnp.concatenate([a[:64], b[:64]]).astype(f32) + across(kv_far).astype(f32)
    grad_query = grad_query * HDIM**-0.5
    grad_query_raw, grad_gain_query = rms_backward(
        query_raw, query_factor, gain_query, rotate_back(grad_query, cos4, sin4)
    )
    grad_query_bf = heads_last(grad_query_raw.astype(bf16))
    grad_w_query = dot_tn(both(grad_query_bf[0], grad_query_bf[1]), attn_in2).astype(bf16)
    mine_query = chunk_sum(grad_w_query.reshape(64, 8, 640)).astype(bf16)
    weights_all = weights_all.reshape(4, 896, 640)

    def summed(start, count):
        return weights_all[:, start : start + count].reshape(4 * count, 640).astype(f32)

    sum_out, sum_gate, sum_up = summed(0, 128), summed(128, 256).T, summed(384, 256).T
    sum_down = summed(640, 256)
    grad_key_raw, grad_gain_key = rms_backward(
        key_raw, key_factor, gain_key, rotate_back(kv_mine[:, :HDIM], cos_tab, sin_tab)
    )
    grad_key_bf = grad_key_raw.astype(bf16)
    grad_value_bf = kv_mine[:, HDIM:].astype(bf16)

    def mine_other(full):
        a, b = full[:, :128], full[:, 128:]
        return jnp.where(first, a, b), jnp.where(first, b, a)

    key_m, key_o = mine_other(grad_key_bf)
    val_m, val_o = mine_other(grad_value_bf)
    grad_kv2 = both(
        jnp.concatenate([key_m, val_m], axis=1), jnp.concatenate([key_o, val_o], axis=1)
    )
    grad_w_kv = dot_tn(grad_kv2, attn_in2)

    grad_attn_in = (
        dot_nt(grad_query_bf[0], query_w[0])
        + dot_nt(grad_query_bf[1], query_w[1])
        + dot_nt(grad_key_bf, key_w)
        + dot_nt(grad_value_bf, value_w)
    )
    grad_in_part, grad_gain_one = rms_backward(resid_in, factor_one, gain_one, grad_attn_in)
    input_grad = grad_mid + grad_in_part

    gain_grads = (
        grad_gain_one,
        grad_gain_two,
        grad_gain_three,
        grad_gain_four,
        grad_gain_query,
        grad_gain_key,
    )
    g_own = jnp.concatenate([jnp.where(first, g[: g.size // 2], g[g.size // 2 :]) for g in gain_grads])
    g_other = jnp.concatenate([jnp.where(first, g[g.size // 2 :], g[: g.size // 2]) for g in gain_grads])
    g_sum = g_own + swap(g_other[None])[0]
    g_block = jnp.concatenate([g_sum, jnp.zeros((1024,), f32)]).reshape(4, 640).astype(bf16)
    g_block = jnp.concatenate([g_block, jnp.zeros((60, 640), bf16)])
    late = jnp.concatenate([grad_w_kv.astype(bf16).reshape(64, 4, 640), g_block[:, None]], axis=1)
    mine_late = chunk_sum(jnp.pad(late, ((0, 0), (0, 3), (0, 0)))).astype(bf16)
    late = chunk_gather(jnp.concatenate([mine_query, mine_late])).astype(f32)
    sum_query = late[:, :8].reshape(512, 640).T
    sum_kv = late[:, 8:12].reshape(256, 640)
    sum_gains = late[:4, 12].reshape(-1)
    return (
        to_pairs(block_output)[None],
        to_pairs(input_grad)[None],
        sum_query,
        sum_kv[:128].T,
        sum_kv[128:].T,
        sum_out,
        sum_gate,
        sum_up,
        sum_down,
        sum_gains[:320],
        sum_gains[1280:1408],
        sum_gains[1408:1536],
        sum_gains[320:640],
        sum_gains[640:960],
        sum_gains[960:1280],
    )


def solution(mesh):
    grid = Mesh(mesh.devices.reshape(4, 4, 4, 2), ("z", "x", "y", "wsh"))
    tokens = P("wsh", CTX, None)
    cols, rows, vec = P(None, "wsh"), P("wsh", None), P("wsh")
    return jax.shard_map(
        per_device,
        mesh=grid,
        in_specs=(tokens, tokens, P(), cols, cols, cols, rows, cols, cols, rows) + (vec,) * 6,
        out_specs=(tokens, tokens, cols, cols, cols, rows, cols, cols, rows) + (vec,) * 6,
        check_vma=False,
    )
```

```python
import functools

import jax
import jax.numpy as jnp
from jax import lax
from jax.experimental import pallas as pl
from jax.experimental.pallas import tpu as pltpu
from jax.sharding import Mesh
from jax.sharding import PartitionSpec as P

HEADS = 4
HDIM = 256
CTX = ("z", "x", "y")
LOG2E = 1.4426950408889634

epsilon = 1e-06
theta_base = 1000000.0
bf16 = jnp.bfloat16
f32 = jnp.float32


def rms_forward(values, gain_w):
    factor = lax.rsqrt(jnp.mean(values * values, axis=-1, keepdims=True) + epsilon)
    return (values * factor * (1.0 + gain_w), factor)


def rms_backward(values, factor, gain_w, grad_out):
    weighted = grad_out * (1.0 + gain_w)
    inner = jnp.mean(weighted * values, axis=-1, keepdims=True)
    grad_in = factor * (weighted - values * factor * factor * inner)
    grad_gain = jnp.sum((grad_out * values * factor).reshape(-1, values.shape[-1]), axis=0)
    return (grad_in, grad_gain)


def rotary_tables(positions, width):
    half_width = width // 2
    frequency = theta_base ** (-jnp.arange(half_width, dtype=f32) * 2.0 / width)
    angles = positions.astype(f32)[:, None] * frequency[None, :]
    return (jnp.cos(angles), jnp.sin(angles))


def rotate(values, cos_tab, sin_tab):
    half = values.shape[-1] // 2
    a, b = values[..., :half], values[..., half:]
    return jnp.concatenate([a * cos_tab - b * sin_tab, b * cos_tab + a * sin_tab], axis=-1)


def rotate_back(grads, cos_tab, sin_tab):
    half = grads.shape[-1] // 2
    a, b = grads[..., :half], grads[..., half:]
    return jnp.concatenate([a * cos_tab + b * sin_tab, b * cos_tab - a * sin_tab], axis=-1)


def block_positions(block_ids, half_rows):
    offsets = jnp.arange(half_rows, dtype=jnp.int32)
    return (block_ids[:, None] * half_rows + offsets[None, :]).reshape(-1)


def dot_f32(left, right):
    return jnp.dot(left, right, preferred_element_type=f32)


def dot_nt(left, right):
    return lax.dot_general(left, right, (((1,), (1,)), ((), ())), preferred_element_type=f32)


def dot_tn(left, right):
    return lax.dot_general(left, right, (((0,), (0,)), ((), ())), preferred_element_type=f32)


def swap(values):
    return lax.ppermute(values, "wsh", [(0, 1), (1, 0)])


def load_group(table, group, kv_all):
    slots = [table[8 * group + i] for i in range(8)]
    blocks = [kv_all[pl.ds(pl.multiple_of(slot * 64, 64), 64), :] for slot in slots]
    keys = jnp.concatenate([block[:, :HDIM] for block in blocks], axis=0)
    vals = jnp.concatenate([block[:, HDIM:] for block in blocks], axis=0)
    return slots, keys, vals


def key_places(table, group, shape, dim):
    place = lax.broadcasted_iota(jnp.int32, shape, dim)
    base = jnp.full(shape, table[32 + 8 * group + 7], jnp.int32)
    for i in range(6, -1, -1):
        base = jnp.where(place < 64 * (i + 1), table[32 + 8 * group + i], base)
    return base * 64 + place % 64


def load_piece(piece, kv_all):
    for i, ref in enumerate(piece):
        kv_all[512 * i : 512 * i + 512, :] = ref[...]


def forward_kernel(first, table, q_ref, *rest):
    piece, rest = rest[:4], rest[4:]
    if first:
        acc_ref, tot_ref, kv_all = rest
        acc_ref[...] = jnp.zeros_like(acc_ref)
        tot_ref[...] = jnp.zeros_like(tot_ref)
    else:
        acc_in, tot_in, acc_ref, tot_ref, kv_all = rest
        acc_ref[...] = acc_in[...]
        tot_ref[...] = tot_in[...]
    load_piece(piece, kv_all)

    def step(group, carry):
        _, keys, vals = load_group(table, group, kv_all)
        places = key_places(table, group, (1, 512), 1)

        def half(i):
            rows = pl.ds(pl.multiple_of(table[64 + i] * 256, 256), 256)
            mine = lax.broadcasted_iota(jnp.int32, (256, 1), 0) % 64 + table[66 + i] * 64
            scores = dot_nt(q_ref[rows, :], keys)
            probs = jnp.where(places <= mine, jnp.exp2(scores * LOG2E), 0.0)
            tot_ref[rows, :] += (probs[:, :128] + probs[:, 128:256]) + (
                probs[:, 256:384] + probs[:, 384:]
            )
            acc_ref[rows, :] += dot_f32(probs.astype(bf16), vals)

        half(0)
        pl.when(8 * group < table[69])(lambda: half(1))
        return carry

    lax.fori_loop(0, (table[68] + 7) // 8, step, 0)


def backward_kernel(first, table, q_ref, g_ref, stat_ref, *rest):
    piece, rest = rest[:4], rest[4:]
    if first:
        dq_ref, *out_refs, kv_all, dkv, out_all = rest
        dq_ref[...] = jnp.zeros_like(dq_ref)
    else:
        dq_in, dq_ref, *out_refs, kv_all, dkv, out_all = rest
        dq_ref[...] = dq_in[...]
    load_piece(piece, kv_all)
    out_all[...] = jnp.zeros_like(out_all)

    def step(group, carry):
        slots, keys, vals = load_group(table, group, kv_all)
        places = key_places(table, group, (512, 1), 0)

        def half(i):
            rows = pl.ds(pl.multiple_of(table[64 + i] * 256, 256), 256)
            mine = lax.broadcasted_iota(jnp.int32, (1, 256), 1) % 64 + table[66 + i] * 64
            query, grads = q_ref[rows, :], g_ref[rows, :]
            stat = stat_ref[table[64 + i]]
            scores = dot_nt(keys, query) * LOG2E - stat[0:1, :]
            probs = jnp.where(places <= mine, jnp.exp2(scores), 0.0)
            grad_scores = (probs * (dot_nt(vals, grads) - stat[1:2, :])).astype(bf16)
            dq_ref[rows, :] += dot_tn(grad_scores, keys)
            return dot_f32(grad_scores, query), dot_f32(probs.astype(bf16), grads)

        grad_k, grad_v = half(0)
        dkv[:, :HDIM] = grad_k
        dkv[:, HDIM:] = grad_v

        @pl.when(8 * group < table[69])
        def _():
            more_k, more_v = half(1)
            dkv[:, :HDIM] += more_k
            dkv[:, HDIM:] += more_v

        for i, slot in enumerate(slots):
            block = dkv[64 * i : 64 * i + 64, :].astype(bf16)
            out_all[pl.ds(pl.multiple_of(slot * 64, 64), 64), :] = block
        return carry

    lax.fori_loop(0, (table[68] + 7) // 8, step, 0)
    for i, ref in enumerate(out_refs):
        ref[...] = out_all[512 * i : 512 * i + 512, :]


def specs(count):
    return [pl.BlockSpec(memory_space=pltpu.SMEM)] + [
        pl.BlockSpec(memory_space=pltpu.VMEM) for _ in range(count)
    ]


def forward_piece(table, query, piece, state):
    return pl.pallas_call(
        functools.partial(forward_kernel, state is None),
        out_shape=(
            jax.ShapeDtypeStruct((512, HDIM), f32),
            jax.ShapeDtypeStruct((512, 128), f32),
        ),
        in_specs=specs(5 if state is None else 7),
        out_specs=tuple(specs(2)[1:]),
        scratch_shapes=[pltpu.VMEM((2048, 512), bf16)],
        cost_estimate=pl.CostEstimate(flops=2 * 10**9, transcendentals=0, bytes_accessed=4 * 10**6),
        input_output_aliases={} if state is None else {6: 0, 7: 1},
        name="attn_fwd",
    )(table, query, *piece, *(state or ()))


def backward_piece(table, query, grads, stats, piece, grad_query):
    return pl.pallas_call(
        functools.partial(backward_kernel, grad_query is None),
        out_shape=(jax.ShapeDtypeStruct((512, HDIM), f32),)
        + (jax.ShapeDtypeStruct((512, 512), bf16),) * 4,
        in_specs=specs(7 if grad_query is None else 8),
        out_specs=tuple(specs(5)[1:]),
        scratch_shapes=[
            pltpu.VMEM((2048, 512), bf16),
            pltpu.VMEM((512, 512), f32),
            pltpu.VMEM((2048, 512), bf16),
        ],
        input_output_aliases={} if grad_query is None else {8: 0},
        name="attn_bwd",
    )(table, query, grads, stats, *piece, *(() if grad_query is None else (grad_query,)))


def weight_kernel(*refs):
    pairs = [(refs[2 * i][...], refs[2 * i + 1][...]) for i in range(7)]
    act, gate, up, hidden, proj, ffw_in, ffw = (jnp.concatenate(p, axis=0) for p in pairs)
    out_ref, gate_ref, up_ref, down_ref = refs[14:]
    out_ref[...] = dot_tn(act, proj).astype(bf16)
    gate_ref[...] = dot_tn(ffw_in, gate).astype(bf16)
    up_ref[...] = dot_tn(ffw_in, up).astype(bf16)
    down_ref[...] = dot_tn(hidden, ffw).astype(bf16)


def weight_grads(*pairs):
    return pl.pallas_call(
        weight_kernel,
        out_shape=(
            jax.ShapeDtypeStruct((512, 640), bf16),
            jax.ShapeDtypeStruct((640, 1024), bf16),
            jax.ShapeDtypeStruct((640, 1024), bf16),
            jax.ShapeDtypeStruct((1024, 640), bf16),
        ),
        in_specs=specs(14)[1:],
        out_specs=tuple(specs(4)[1:]),
        name="weight_grads",
    )(*pairs)


def shift(values, axis, by):
    perm = [
        (2 * a + w, 2 * ((a + (by if w == 0 else -by)) % 4) + w) for a in range(4) for w in range(2)
    ]
    return lax.ppermute(values, (axis, "wsh"), perm)


def ring_gather(block, axis):
    out = [block]
    for _ in range(3):
        out.append(shift(out[-1], axis, 1))
    return out


def ring_sum(parts, axis):
    moving = parts[3]
    for d in (2, 1, 0):
        moving = (shift(moving, axis, -1).astype(f32) + parts[d].astype(f32)).astype(bf16)
    return moving


def direct_gather(block, axis):
    return [block] + [shift(block, axis, d) for d in (1, 2, 3)]


def direct_sum(parts, axis):
    got = [shift(parts[d], axis, -d) for d in (1, 2, 3)]
    return sum((g.astype(f32) for g in got), parts[0].astype(f32))


def to_pairs(values):
    perm = [
        (2 * z + w, 2 * z + w) if w == z % 2 else (2 * z + w, 2 * (z ^ 1) + 1 - w)
        for z in range(4)
        for w in range(2)
    ]
    return lax.ppermute(values, ("z", "wsh"), perm)


def across(values):
    perm = [(2 * z + w, 2 * ((z + 2) % 4) + w) for z in range(4) for w in range(2)]
    return lax.ppermute(values, ("z", "wsh"), perm)


def gather_middle(near):
    a = ring_gather(jnp.concatenate([x[:64] for x in near]), "x")
    b = ring_gather(jnp.concatenate([x[64:] for x in near]), "y")
    return jnp.concatenate(a), jnp.concatenate(b)


def tie(*values):
    return lax.optimization_barrier(values)


def plus(left, right):
    return (left.astype(f32) + right.astype(f32)).astype(bf16)


def piece_tables(pair_blocks, mine, sign):
    z, x, y = (lax.axis_index(name) for name in CTX)
    i = jnp.arange(128, dtype=jnp.int32)
    piece, inside = i // 32, i % 32
    color, part = inside // 16, (inside % 16) // 8
    outer, inner = (inside % 8) // 2, inside % 2
    core = (1 - sign) // 2
    sign = jnp.where(part == 0, sign, -sign)
    at_z = 2 * ((z // 2 + inner) % 2) + jnp.where(part == 0, core, 1 - core)
    at_x = (x - sign * jnp.where(color == 0, outer, piece)) % 4
    at_y = (y - sign * jnp.where(color == 0, piece, outer)) % 4
    source = 2 * (at_z * 16 + at_x * 4 + at_y) + color
    flat = pair_blocks.reshape(1, 128)
    hit = source[:, None] == jnp.arange(128, dtype=jnp.int32)[None]
    ids = jnp.sum(jnp.where(hit, flat, 0), axis=1).reshape(4, 32)
    rank = jnp.sum((ids[:, None, :] < ids[:, :, None]).astype(jnp.int32), axis=2)
    at = rank[:, None, :] == jnp.arange(32, dtype=jnp.int32)[None, :, None]
    slots = jnp.sum(jnp.where(at, jnp.arange(32, dtype=jnp.int32)[None, None], 0), axis=2)
    sorted_ids = jnp.sum(jnp.where(at, ids[:, None, :], 0), axis=2)
    seen = jnp.sum((ids[:, None, :] <= mine[None, :, None]).astype(jnp.int32), axis=2)
    upper = (mine[1] > mine[0]).astype(jnp.int32)
    which = jnp.stack([upper, 1 - upper])
    own = jnp.stack([jnp.max(mine), jnp.min(mine)])
    fixed = jnp.broadcast_to(jnp.concatenate([which, own])[None], (4, 4))
    seen = jnp.stack([jnp.max(seen, axis=1), jnp.min(seen, axis=1)], axis=1)
    return jnp.concatenate([slots, sorted_ids, fixed, seen], axis=1)


def chunk_sum(values):
    got = lax.all_to_all(values, CTX, split_axis=0, concat_axis=0, tiled=True)
    return jnp.sum(got.astype(f32), axis=0)


def chunk_gather(values):
    wide = jnp.broadcast_to(values[None], (64,) + values.shape)
    return lax.all_to_all(wide, CTX, split_axis=0, concat_axis=0, tiled=True)


def per_device(
    block_input,
    cotangent,
    pair_blocks,
    w_query,
    w_key,
    w_value,
    w_out,
    w_gate,
    w_up,
    w_down,
    attn_pre_gain,
    query_gain,
    key_gain,
    attn_post_gain,
    ffw_pre_gain,
    ffw_post_gain,
):
    rows = block_input.shape[1]
    core = lax.axis_index("wsh")
    first = core == 0
    rank = 32 * (lax.axis_index("z") // 2) + 16 * core
    rank = rank + 4 * lax.axis_index("x") + lax.axis_index("y")

    def ordered(own, other, axis):
        return jnp.where(
            first,
            jnp.concatenate([own, other], axis=axis),
            jnp.concatenate([other, own], axis=axis),
        )

    resid_in = to_pairs(block_input[0]).astype(f32)
    my_blocks = lax.dynamic_slice_in_dim(pair_blocks, rank, 1, 0)[0]
    query_pos = block_positions(my_blocks, rows // 2)
    sign = jnp.where(first, 1, -1)
    cos_tab, sin_tab = rotary_tables(query_pos, HDIM)

    kv_own = jnp.concatenate([w_key, w_value], axis=1)
    kv_other = swap(kv_own)

    def gain(own):
        own = own[None]
        return ordered(own, swap(own), 1).astype(f32)

    gain_one, gain_key = gain(attn_pre_gain), gain(key_gain)
    key_w = ordered(kv_own[:, :128], kv_other[:, :128], 1)
    value_w = ordered(kv_own[:, 128:], kv_other[:, 128:], 1)

    normed_one, factor_one = rms_forward(resid_in, gain_one)
    attn_in = normed_one.astype(bf16)
    key_raw = dot_f32(attn_in, key_w)
    value_bf = dot_f32(attn_in, value_w).astype(bf16)
    key_normed, key_factor = rms_forward(key_raw, gain_key)
    key_rot = rotate(key_normed, cos_tab, sin_tab).astype(bf16)
    near = [jnp.concatenate([key_rot, value_bf], axis=1)]
    near.append(across(near[0]))
    near[1], late_blocks = lax.optimization_barrier((near[1], pair_blocks))
    mine_late = lax.dynamic_slice_in_dim(late_blocks, rank, 1, 0)[0]
    tables = piece_tables(late_blocks, mine_late, sign)
    own_a, own_b = gather_middle(near)
    own_a, own_b, cotangent, w_query, w_out, w_gate, w_up, w_down, gains = lax.optimization_barrier(
        (
            own_a,
            own_b,
            cotangent,
            w_query,
            w_out,
            w_gate,
            w_up,
            w_down,
            (query_gain, attn_post_gain, ffw_pre_gain, ffw_post_gain),
        )
    )
    grad_top = to_pairs(cotangent[0])
    gain_query, gain_two, gain_three, gain_four = (gain(g) for g in gains)
    query_w = (w_query, swap(w_query))
    out_w = (w_out, swap(w_out))
    gate_w = (w_gate, swap(w_gate))
    up_w = (w_up, swap(w_up))
    down_w = (w_down, swap(w_down))

    def heads_first(pair):
        return jnp.concatenate(
            [
                part[64 * i : 64 * i + 64, HDIM * h : HDIM * (h + 1)]
                for i in range(2)
                for part in pair
                for h in range(2)
            ],
            axis=0,
        )

    def heads_last(stacked):
        def block(i, p, h):
            start = 64 * (4 * i + 2 * p + h)
            return stacked[start : start + 64]

        return tuple(
            jnp.concatenate(
                [jnp.concatenate([block(i, p, 0), block(i, p, 1)], axis=1) for i in range(2)]
            )
            for p in range(2)
        )

    def tile_heads(table):
        return jnp.concatenate([table[:64]] * HEADS + [table[64:]] * HEADS)

    cos4, sin4 = tile_heads(cos_tab), tile_heads(sin_tab)
    query_raw = heads_first(tuple(dot_f32(attn_in, half) for half in query_w))
    query_normed, query_factor = rms_forward(query_raw, gain_query)
    query_rot = (rotate(query_normed, cos4, sin4)).astype(bf16) * bf16(HDIM**-0.5)
    state = None
    a, b = own_a, own_b
    pieces = []
    for d in range(4):
        pieces.append((a, swap(a), b, swap(b)))
        if d < 3:
            coming = (shift(a, "y", 1), shift(b, "x", 1))
        state = forward_piece(tables[d], query_rot, pieces[d], state)
        if d < 3:
            a, b, state = lax.optimization_barrier((*coming, state))
    totals = jnp.sum(state[1], axis=1, keepdims=True)
    attn_heads = (state[0] / totals).astype(bf16)
    attn_out = heads_last(attn_heads)
    attn_proj = dot_f32(attn_out[0], out_w[0]) + dot_f32(attn_out[1], out_w[1])
    normed_two, factor_two = rms_forward(attn_proj, gain_two)
    mid = resid_in + normed_two
    normed_three, factor_three = rms_forward(mid, gain_three)
    ffw_in = normed_three.astype(bf16)

    gate = [dot_f32(ffw_in, half) for half in gate_w]
    up_val = [dot_f32(ffw_in, half) for half in up_w]
    acts = [jax.vjp(lambda inner: jax.nn.gelu(inner, approximate=True), g) for g in gate]
    hidden = [(act[0] * up).astype(bf16) for act, up in zip(acts, up_val)]
    ffw_proj = dot_f32(hidden[0], down_w[0]) + dot_f32(hidden[1], down_w[1])
    normed_four, factor_four = rms_forward(ffw_proj, gain_four)
    block_output = mid + normed_four

    grad_ffw, grad_gain_four = rms_backward(ffw_proj, factor_four, gain_four, grad_top)
    grad_ffw_bf = grad_ffw.astype(bf16)
    grad_hidden = [dot_nt(grad_ffw_bf, half) for half in down_w]
    grad_gate = [
        act[1](gh * up)[0].astype(bf16) for act, gh, up in zip(acts, grad_hidden, up_val)
    ]
    grad_up = [(gh * act[0]).astype(bf16) for act, gh in zip(acts, grad_hidden)]
    grad_ffw_in = (
        dot_nt(grad_gate[0], gate_w[0])
        + dot_nt(grad_gate[1], gate_w[1])
        + dot_nt(grad_up[0], up_w[0])
        + dot_nt(grad_up[1], up_w[1])
    )
    grad_mid_part, grad_gain_three = rms_backward(mid, factor_three, gain_three, grad_ffw_in)
    grad_mid = grad_top + grad_mid_part
    grad_proj, grad_gain_two = rms_backward(attn_proj, factor_two, gain_two, grad_mid)
    grad_proj_bf = grad_proj.astype(bf16)
    grad_attn = tuple(dot_nt(grad_proj_bf, half).astype(bf16) for half in out_w)
    grad_heads = heads_first(grad_attn)

    def both(own, other):
        return jnp.concatenate([own, swap(other)], axis=0)

    ffw_in_p, grad_ffw_p, grad_proj_p = swap(ffw_in), swap(grad_ffw_bf), swap(grad_proj_bf)
    big = weight_grads(
        attn_out[0],
        swap(attn_out[1]),
        grad_gate[0],
        swap(grad_gate[1]),
        grad_up[0],
        swap(grad_up[1]),
        hidden[0],
        swap(hidden[1]),
        grad_proj_bf,
        grad_proj_p,
        ffw_in,
        ffw_in_p,
        grad_ffw_bf,
        grad_ffw_p,
    )
    attn_in2 = both(attn_in, attn_in)

    delta = jnp.sum(grad_heads.astype(f32) * attn_heads.astype(f32), axis=-1)
    stats = jnp.stack([jnp.log2(totals[:, 0]), delta]).reshape(2, 2, 256).transpose(1, 0, 2)
    stats, big = lax.optimization_barrier((stats, big))
    sum_out, sum_gate, sum_up, sum_down = (g.astype(f32) for g in lax.psum(big, CTX))
    grad_query = None
    moving = None
    for d in (3, 2, 1, 0):
        if d < 3:
            coming = (shift(moving[0], "y", -1), shift(moving[1], "x", -1))
        grad_query, a, a_p, b, b_p = backward_piece(
            tables[d], query_rot, grad_heads, stats, pieces[d], grad_query
        )
        terms = [a.astype(f32) + swap(a_p).astype(f32), b.astype(f32) + swap(b_p).astype(f32)]
        if d < 3:
            terms = [c.astype(f32) + t for c, t in zip(coming, terms)]
        moving = [t.astype(bf16) for t in terms]
        if d:
            *moving, grad_query = tie(*moving, grad_query)
    all_a, all_b = moving
    a, b = all_a[384:], all_b[384:]
    for d in (2, 1, 0):
        rows_d = slice(128 * d, 128 * d + 128)
        a = plus(shift(a, "x", -1), all_a[rows_d])
        b = plus(shift(b, "y", -1), all_b[rows_d])
    grad_query = grad_query * HDIM**-0.5
    grad_query_raw, grad_gain_query = rms_backward(
        query_raw, query_factor, gain_query, rotate_back(grad_query, cos4, sin4)
    )
    grad_query_bf = heads_last(grad_query_raw.astype(bf16))
    grad_w_query = dot_tn(both(grad_query_bf[0], grad_query_bf[1]), attn_in2).astype(bf16)
    mine_query = chunk_sum(grad_w_query.reshape(64, 8, 640)).astype(bf16)
    a, b, mine_query = tie(a, b, mine_query)
    kv_far = jnp.concatenate([a[64:], b[64:]])
    kv_mine = jnp.concatenate([a[:64], b[:64]]).astype(f32) + across(kv_far).astype(f32)
    grad_key_raw, grad_gain_key = rms_backward(
        key_raw, key_factor, gain_key, rotate_back(kv_mine[:, :HDIM], cos_tab, sin_tab)
    )
    grad_key_bf = grad_key_raw.astype(bf16)
    grad_value_bf = kv_mine[:, HDIM:].astype(bf16)

    def mine_other(full):
        a, b = full[:, :128], full[:, 128:]
        return jnp.where(first, a, b), jnp.where(first, b, a)

    key_m, key_o = mine_other(grad_key_bf)
    val_m, val_o = mine_other(grad_value_bf)
    grad_kv2 = both(
        jnp.concatenate([key_m, val_m], axis=1), jnp.concatenate([key_o, val_o], axis=1)
    )
    grad_w_kv = dot_tn(grad_kv2, attn_in2)

    grad_attn_in = (
        dot_nt(grad_query_bf[0], query_w[0])
        + dot_nt(grad_query_bf[1], query_w[1])
        + dot_nt(grad_key_bf, key_w)
        + dot_nt(grad_value_bf, value_w)
    )
    grad_in_part, grad_gain_one = rms_backward(resid_in, factor_one, gain_one, grad_attn_in)
    input_grad = grad_mid + grad_in_part

    gain_grads = (
        grad_gain_one,
        grad_gain_two,
        grad_gain_three,
        grad_gain_four,
        grad_gain_query,
        grad_gain_key,
    )
    g_own = jnp.concatenate([jnp.where(first, g[: g.size // 2], g[g.size // 2 :]) for g in gain_grads])
    g_other = jnp.concatenate([jnp.where(first, g[g.size // 2 :], g[: g.size // 2]) for g in gain_grads])
    g_sum = g_own + swap(g_other[None])[0]
    g_block = jnp.concatenate([g_sum, jnp.zeros((1024,), f32)]).reshape(4, 640).astype(bf16)
    g_block = jnp.concatenate([g_block, jnp.zeros((60, 640), bf16)])
    late = jnp.concatenate([grad_w_kv.astype(bf16).reshape(64, 4, 640), g_block[:, None]], axis=1)
    mine_late = chunk_sum(jnp.pad(late, ((0, 0), (0, 3), (0, 0)))).astype(bf16)
    late = chunk_gather(jnp.concatenate([mine_query, mine_late])).astype(f32)
    sum_query = late[:, :8].reshape(512, 640).T
    sum_kv = late[:, 8:12].reshape(256, 640)
    sum_gains = late[:4, 12].reshape(-1)
    return (
        to_pairs(block_output)[None],
        to_pairs(input_grad)[None],
        sum_query,
        sum_kv[:128].T,
        sum_kv[128:].T,
        sum_out,
        sum_gate,
        sum_up,
        sum_down,
        sum_gains[:320],
        sum_gains[1280:1408],
        sum_gains[1408:1536],
        sum_gains[320:640],
        sum_gains[640:960],
        sum_gains[960:1280],
    )


def solution(mesh):
    grid = Mesh(mesh.devices.reshape(4, 4, 4, 2), ("z", "x", "y", "wsh"))
    tokens = P("wsh", CTX, None)
    cols, rows, vec = P(None, "wsh"), P("wsh", None), P("wsh")
    return jax.shard_map(
        per_device,
        mesh=grid,
        in_specs=(tokens, tokens, P(), cols, cols, cols, rows, cols, cols, rows) + (vec,) * 6,
        out_specs=(tokens, tokens, cols, cols, cols, rows, cols, cols, rows) + (vec,) * 6,
        check_vma=False,
    )
```

```python
import functools

import jax
import jax.numpy as jnp
from jax import lax
from jax.experimental import pallas as pl
from jax.experimental.pallas import tpu as pltpu
from jax.sharding import Mesh
from jax.sharding import PartitionSpec as P

HEADS = 4
HDIM = 256
CTX = ("z", "x", "y")
LOG2E = 1.4426950408889634
GELU_C = 0.7978845608028654

epsilon = 1e-06
theta_base = 1000000.0
bf16 = jnp.bfloat16
f32 = jnp.float32


def rms_forward(values, gain_w):
    factor = lax.rsqrt(jnp.mean(values * values, axis=-1, keepdims=True) + epsilon)
    return (values * factor * (1.0 + gain_w), factor)


def rms_backward(values, factor, gain_w, grad_out):
    weighted = grad_out * (1.0 + gain_w)
    inner = jnp.mean(weighted * values, axis=-1, keepdims=True)
    grad_in = factor * (weighted - values * factor * factor * inner)
    grad_gain = jnp.sum((grad_out * values * factor).reshape(-1, values.shape[-1]), axis=0)
    return (grad_in, grad_gain)


def rotary_tables(positions, width):
    half_width = width // 2
    frequency = theta_base ** (-jnp.arange(half_width, dtype=f32) * 2.0 / width)
    angles = positions.astype(f32)[:, None] * frequency[None, :]
    return (jnp.cos(angles), jnp.sin(angles))


def rotate(values, cos_tab, sin_tab):
    half = values.shape[-1] // 2
    a, b = values[..., :half], values[..., half:]
    return jnp.concatenate([a * cos_tab - b * sin_tab, b * cos_tab + a * sin_tab], axis=-1)


def rotate_back(grads, cos_tab, sin_tab):
    half = grads.shape[-1] // 2
    a, b = grads[..., :half], grads[..., half:]
    return jnp.concatenate([a * cos_tab + b * sin_tab, b * cos_tab - a * sin_tab], axis=-1)


def block_positions(block_ids, half_rows):
    offsets = jnp.arange(half_rows, dtype=jnp.int32)
    return (block_ids[:, None] * half_rows + offsets[None, :]).reshape(-1)


def dot_f32(left, right):
    return jnp.dot(left, right, preferred_element_type=f32)


def dot_nt(left, right):
    return lax.dot_general(left, right, (((1,), (1,)), ((), ())), preferred_element_type=f32)


def dot_tn(left, right):
    return lax.dot_general(left, right, (((0,), (0,)), ((), ())), preferred_element_type=f32)


def swap(values):
    return lax.ppermute(values, "wsh", [(0, 1), (1, 0)])


def load_group(table, group, kv_all):
    slots = [table[8 * group + i] for i in range(8)]
    blocks = [kv_all[pl.ds(pl.multiple_of(slot * 64, 64), 64), :] for slot in slots]
    keys = jnp.concatenate([block[:, :HDIM] for block in blocks], axis=0)
    vals = jnp.concatenate([block[:, HDIM:] for block in blocks], axis=0)
    return slots, keys, vals


def key_places(table, group, shape, dim):
    place = lax.broadcasted_iota(jnp.int32, shape, dim)
    base = jnp.full(shape, table[32 + 8 * group + 7], jnp.int32)
    for i in range(6, -1, -1):
        base = jnp.where(place < 64 * (i + 1), table[32 + 8 * group + i], base)
    return base * 64 + place % 64


def load_piece(piece, kv_all):
    for i, ref in enumerate(piece):
        kv_all[512 * i : 512 * i + 512, :] = ref[...]


def forward_kernel(first, table, q_ref, *rest):
    piece, rest = rest[:4], rest[4:]
    if first:
        acc_ref, tot_ref, kv_all = rest
        acc_ref[...] = jnp.zeros_like(acc_ref)
        tot_ref[...] = jnp.zeros_like(tot_ref)
    else:
        acc_in, tot_in, acc_ref, tot_ref, kv_all = rest
        acc_ref[...] = acc_in[...]
        tot_ref[...] = tot_in[...]
    load_piece(piece, kv_all)

    def step(group, carry):
        _, keys, vals = load_group(table, group, kv_all)
        places = key_places(table, group, (1, 512), 1)

        def half(i):
            rows = pl.ds(pl.multiple_of(table[64 + i] * 256, 256), 256)
            mine = lax.broadcasted_iota(jnp.int32, (256, 1), 0) % 64 + table[66 + i] * 64
            scores = dot_nt(q_ref[rows, :], keys)
            probs = jnp.where(places <= mine, jnp.exp2(scores * LOG2E), 0.0)
            tot_ref[rows, :] += (probs[:, :128] + probs[:, 128:256]) + (
                probs[:, 256:384] + probs[:, 384:]
            )
            acc_ref[rows, :] += dot_f32(probs.astype(bf16), vals)

        half(0)
        pl.when(8 * group < table[69])(lambda: half(1))
        return carry

    lax.fori_loop(0, (table[68] + 7) // 8, step, 0)


def backward_kernel(first, table, q_ref, g_ref, stat_ref, *rest):
    piece, rest = rest[:4], rest[4:]
    if first:
        dq_ref, *out_refs, kv_all, dkv, out_all = rest
        dq_ref[...] = jnp.zeros_like(dq_ref)
    else:
        dq_in, dq_ref, *out_refs, kv_all, dkv, out_all = rest
        dq_ref[...] = dq_in[...]
    load_piece(piece, kv_all)
    out_all[...] = jnp.zeros_like(out_all)

    def step(group, carry):
        slots, keys, vals = load_group(table, group, kv_all)
        places = key_places(table, group, (512, 1), 0)

        def half(i):
            rows = pl.ds(pl.multiple_of(table[64 + i] * 256, 256), 256)
            mine = lax.broadcasted_iota(jnp.int32, (1, 256), 1) % 64 + table[66 + i] * 64
            query, grads = q_ref[rows, :], g_ref[rows, :]
            stat = stat_ref[table[64 + i]]
            scores = dot_nt(keys, query) * LOG2E - stat[0:1, :]
            probs = jnp.where(places <= mine, jnp.exp2(scores), 0.0)
            grad_scores = (probs * (dot_nt(vals, grads) - stat[1:2, :])).astype(bf16)
            dq_ref[rows, :] += dot_tn(grad_scores, keys)
            return dot_f32(grad_scores, query), dot_f32(probs.astype(bf16), grads)

        grad_k, grad_v = half(0)
        dkv[:, :HDIM] = grad_k
        dkv[:, HDIM:] = grad_v

        @pl.when(8 * group < table[69])
        def _():
            more_k, more_v = half(1)
            dkv[:, :HDIM] += more_k
            dkv[:, HDIM:] += more_v

        for i, slot in enumerate(slots):
            block = dkv[64 * i : 64 * i + 64, :].astype(bf16)
            out_all[pl.ds(pl.multiple_of(slot * 64, 64), 64), :] = block
        return carry

    lax.fori_loop(0, (table[68] + 7) // 8, step, 0)
    for i, ref in enumerate(out_refs):
        ref[...] = out_all[512 * i : 512 * i + 512, :]


def specs(count):
    return [pl.BlockSpec(memory_space=pltpu.SMEM)] + [
        pl.BlockSpec(memory_space=pltpu.VMEM) for _ in range(count)
    ]


def forward_piece(table, query, piece, state):
    return pl.pallas_call(
        functools.partial(forward_kernel, state is None),
        out_shape=(
            jax.ShapeDtypeStruct((512, HDIM), f32),
            jax.ShapeDtypeStruct((512, 128), f32),
        ),
        in_specs=specs(5 if state is None else 7),
        out_specs=tuple(specs(2)[1:]),
        scratch_shapes=[pltpu.VMEM((2048, 512), bf16)],
        cost_estimate=pl.CostEstimate(flops=2 * 10**9, transcendentals=0, bytes_accessed=4 * 10**6),
        input_output_aliases={} if state is None else {6: 0, 7: 1},
        name="attn_fwd",
    )(table, query, *piece, *(state or ()))


def backward_piece(table, query, grads, stats, piece, grad_query):
    return pl.pallas_call(
        functools.partial(backward_kernel, grad_query is None),
        out_shape=(jax.ShapeDtypeStruct((512, HDIM), f32),)
        + (jax.ShapeDtypeStruct((512, 512), bf16),) * 4,
        in_specs=specs(7 if grad_query is None else 8),
        out_specs=tuple(specs(5)[1:]),
        scratch_shapes=[
            pltpu.VMEM((2048, 512), bf16),
            pltpu.VMEM((512, 512), f32),
            pltpu.VMEM((2048, 512), bf16),
        ],
        input_output_aliases={} if grad_query is None else {8: 0},
        name="attn_bwd",
    )(table, query, grads, stats, *piece, *(() if grad_query is None else (grad_query,)))


def gelu_pair(v):
    inner = GELU_C * (v + 0.044715 * v * v * v)
    t = jnp.tanh(inner)
    slope = 0.5 * (1.0 + t) + 0.5 * v * (1.0 - t * t) * (GELU_C * (1.0 + 0.134145 * v * v))
    return 0.5 * v * (1.0 + t), slope


def norm_backward(values, factor, gain_w, grad_out):
    weighted = grad_out * (1.0 + gain_w)
    inner = jnp.mean(weighted * values, axis=-1, keepdims=True)
    grad_in = factor * (weighted - values * factor * factor * inner)
    return grad_in, jnp.sum(grad_out * values * factor, axis=0, keepdims=True)


def middle_kernel(*refs):
    acc, tot, resid, grad_top, gain_two, gain_three, gain_four = (r[...] for r in refs[:7])
    out_w, gate_w, up_w, down_w = refs[7:9], refs[9:11], refs[11:13], refs[13:15]
    attn_o, hidden_o, ggate_o, gup_o = refs[15:17], refs[17:19], refs[19:21], refs[21:23]
    block_o, grad_mid_o, ffw_in_o, grad_ffw_o, grad_proj_o, heads_o, stat_o = refs[23:30]
    two_o, three_o, four_o = refs[30:]
    totals = jnp.sum(tot, axis=1, keepdims=True)
    heads = (acc / totals).astype(bf16)

    def block(i, p, h):
        start = 64 * (4 * i + 2 * p + h)
        return heads[start : start + 64]

    attn_proj = jnp.zeros((128, 640), f32)
    for p in range(2):
        part = jnp.concatenate(
            [jnp.concatenate([block(i, p, 0), block(i, p, 1)], axis=1) for i in range(2)], axis=0
        )
        attn_o[p][...] = part
        attn_proj += dot_f32(part, out_w[p][...])
    normed_two, factor_two = rms_forward(attn_proj, gain_two)
    mid = resid + normed_two
    normed_three, factor_three = rms_forward(mid, gain_three)
    ffw_in = normed_three.astype(bf16)
    ffw_in_o[...] = ffw_in
    ffw_proj = jnp.zeros((128, 640), f32)
    for p in range(2):
        act, _ = gelu_pair(dot_f32(ffw_in, gate_w[p][...]))
        hidden = (act * dot_f32(ffw_in, up_w[p][...])).astype(bf16)
        hidden_o[p][...] = hidden
        ffw_proj += dot_f32(hidden, down_w[p][...])
    normed_four, factor_four = rms_forward(ffw_proj, gain_four)
    block_o[...] = mid + normed_four
    grad_ffw, four_o[...] = norm_backward(ffw_proj, factor_four, gain_four, grad_top)
    grad_ffw_bf = grad_ffw.astype(bf16)
    grad_ffw_o[...] = grad_ffw_bf
    grad_ffw_in = jnp.zeros((128, 640), f32)
    for p in range(2):
        act, slope = gelu_pair(dot_f32(ffw_in, gate_w[p][...]))
        up = dot_f32(ffw_in, up_w[p][...])
        grad_hidden = dot_nt(grad_ffw_bf, down_w[p][...])
        grad_gate = (grad_hidden * up * slope).astype(bf16)
        grad_up = (grad_hidden * act).astype(bf16)
        ggate_o[p][...] = grad_gate
        gup_o[p][...] = grad_up
        grad_ffw_in += dot_nt(grad_gate, gate_w[p][...]) + dot_nt(grad_up, up_w[p][...])
    grad_mid_part, three_o[...] = norm_backward(mid, factor_three, gain_three, grad_ffw_in)
    grad_mid = grad_top + grad_mid_part
    grad_mid_o[...] = grad_mid
    grad_proj, two_o[...] = norm_backward(attn_proj, factor_two, gain_two, grad_mid)
    grad_proj_bf = grad_proj.astype(bf16)
    grad_proj_o[...] = grad_proj_bf
    grad_attn = [dot_nt(grad_proj_bf, out_w[p][...]).astype(bf16) for p in range(2)]
    grad_heads = jnp.concatenate(
        [
            grad_attn[p][64 * i : 64 * i + 64, HDIM * h : HDIM * (h + 1)]
            for i in range(2)
            for p in range(2)
            for h in range(2)
        ],
        axis=0,
    )
    heads_o[...] = grad_heads
    delta = jnp.sum(grad_heads.astype(f32) * heads.astype(f32), axis=1, keepdims=True)
    for i, col in enumerate((jnp.log(totals) * LOG2E, delta)):
        row = jnp.broadcast_to(col, (512, 128)).T[0:1]
        stat_o[0, i : i + 1, :] = row[:, :256]
        stat_o[1, i : i + 1, :] = row[:, 256:]


def middle(*values):
    shapes = [((128, 512), bf16)] * 2 + [((128, 1024), bf16)] * 6 + [((128, 640), f32)] * 2
    shapes += [((128, 640), bf16)] * 3 + [((512, HDIM), bf16), ((2, 2, 256), f32)]
    shapes += [((1, 640), f32)] * 3
    return pl.pallas_call(
        middle_kernel,
        out_shape=tuple(jax.ShapeDtypeStruct(*s) for s in shapes),
        in_specs=specs(15)[1:],
        out_specs=tuple(specs(18)[1:]),
        name="middle",
    )(*values)


def weight_kernel(*refs):
    pairs = [(refs[2 * i][...], refs[2 * i + 1][...]) for i in range(7)]
    act, gate, up, hidden, proj, ffw_in, ffw = (jnp.concatenate(p, axis=0) for p in pairs)
    out_ref, gate_ref, up_ref, down_ref = refs[14:]
    out_ref[...] = dot_tn(act, proj).astype(bf16)
    gate_ref[...] = dot_tn(ffw_in, gate).astype(bf16)
    up_ref[...] = dot_tn(ffw_in, up).astype(bf16)
    down_ref[...] = dot_tn(hidden, ffw).astype(bf16)


def weight_grads(*pairs):
    return pl.pallas_call(
        weight_kernel,
        out_shape=(
            jax.ShapeDtypeStruct((512, 640), bf16),
            jax.ShapeDtypeStruct((640, 1024), bf16),
            jax.ShapeDtypeStruct((640, 1024), bf16),
            jax.ShapeDtypeStruct((1024, 640), bf16),
        ),
        in_specs=specs(14)[1:],
        out_specs=tuple(specs(4)[1:]),
        name="weight_grads",
    )(*pairs)


def shift(values, axis, by):
    perm = [
        (2 * a + w, 2 * ((a + (by if w == 0 else -by)) % 4) + w) for a in range(4) for w in range(2)
    ]
    return lax.ppermute(values, (axis, "wsh"), perm)


def ring_gather(block, axis):
    out = [block]
    for _ in range(3):
        out.append(shift(out[-1], axis, 1))
    return out


def ring_sum(parts, axis):
    moving = parts[3]
    for d in (2, 1, 0):
        moving = (shift(moving, axis, -1).astype(f32) + parts[d].astype(f32)).astype(bf16)
    return moving


def direct_gather(block, axis):
    return [block] + [shift(block, axis, d) for d in (1, 2, 3)]


def direct_sum(parts, axis):
    got = [shift(parts[d], axis, -d) for d in (1, 2, 3)]
    return sum((g.astype(f32) for g in got), parts[0].astype(f32))


def to_pairs(values):
    perm = [
        (2 * z + w, 2 * z + w) if w == z % 2 else (2 * z + w, 2 * (z ^ 1) + 1 - w)
        for z in range(4)
        for w in range(2)
    ]
    return lax.ppermute(values, ("z", "wsh"), perm)


def across(values):
    perm = [(2 * z + w, 2 * ((z + 2) % 4) + w) for z in range(4) for w in range(2)]
    return lax.ppermute(values, ("z", "wsh"), perm)


def gather_middle(near):
    a = ring_gather(jnp.concatenate([x[:64] for x in near]), "x")
    b = ring_gather(jnp.concatenate([x[64:] for x in near]), "y")
    return jnp.concatenate(a), jnp.concatenate(b)


def tie(*values):
    return lax.optimization_barrier(values)


def plus(left, right):
    return (left.astype(f32) + right.astype(f32)).astype(bf16)


def piece_tables(pair_blocks, mine, sign):
    z, x, y = (lax.axis_index(name) for name in CTX)
    i = jnp.arange(128, dtype=jnp.int32)
    piece, inside = i // 32, i % 32
    color, part = inside // 16, (inside % 16) // 8
    outer, inner = (inside % 8) // 2, inside % 2
    core = (1 - sign) // 2
    sign = jnp.where(part == 0, sign, -sign)
    at_z = 2 * ((z // 2 + inner) % 2) + jnp.where(part == 0, core, 1 - core)
    at_x = (x - sign * jnp.where(color == 0, outer, piece)) % 4
    at_y = (y - sign * jnp.where(color == 0, piece, outer)) % 4
    source = 2 * (at_z * 16 + at_x * 4 + at_y) + color
    flat = pair_blocks.reshape(1, 128)
    hit = source[:, None] == jnp.arange(128, dtype=jnp.int32)[None]
    ids = jnp.sum(jnp.where(hit, flat, 0), axis=1).reshape(4, 32)
    rank = jnp.sum((ids[:, None, :] < ids[:, :, None]).astype(jnp.int32), axis=2)
    at = rank[:, None, :] == jnp.arange(32, dtype=jnp.int32)[None, :, None]
    slots = jnp.sum(jnp.where(at, jnp.arange(32, dtype=jnp.int32)[None, None], 0), axis=2)
    sorted_ids = jnp.sum(jnp.where(at, ids[:, None, :], 0), axis=2)
    seen = jnp.sum((ids[:, None, :] <= mine[None, :, None]).astype(jnp.int32), axis=2)
    upper = (mine[1] > mine[0]).astype(jnp.int32)
    which = jnp.stack([upper, 1 - upper])
    own = jnp.stack([jnp.max(mine), jnp.min(mine)])
    fixed = jnp.broadcast_to(jnp.concatenate([which, own])[None], (4, 4))
    seen = jnp.stack([jnp.max(seen, axis=1), jnp.min(seen, axis=1)], axis=1)
    return jnp.concatenate([slots, sorted_ids, fixed, seen], axis=1)


def chunk_sum(values):
    got = lax.all_to_all(values, CTX, split_axis=0, concat_axis=0, tiled=True)
    return jnp.sum(got.astype(f32), axis=0)


def chunk_gather(values):
    wide = jnp.broadcast_to(values[None], (64,) + values.shape)
    return lax.all_to_all(wide, CTX, split_axis=0, concat_axis=0, tiled=True)


def per_device(
    block_input,
    cotangent,
    pair_blocks,
    w_query,
    w_key,
    w_value,
    w_out,
    w_gate,
    w_up,
    w_down,
    attn_pre_gain,
    query_gain,
    key_gain,
    attn_post_gain,
    ffw_pre_gain,
    ffw_post_gain,
):
    rows = block_input.shape[1]
    core = lax.axis_index("wsh")
    first = core == 0
    rank = 32 * (lax.axis_index("z") // 2) + 16 * core
    rank = rank + 4 * lax.axis_index("x") + lax.axis_index("y")

    def ordered(own, other, axis):
        return jnp.where(
            first,
            jnp.concatenate([own, other], axis=axis),
            jnp.concatenate([other, own], axis=axis),
        )

    resid_in = to_pairs(block_input[0]).astype(f32)
    my_blocks = lax.dynamic_slice_in_dim(pair_blocks, rank, 1, 0)[0]
    query_pos = block_positions(my_blocks, rows // 2)
    sign = jnp.where(first, 1, -1)
    cos_tab, sin_tab = rotary_tables(query_pos, HDIM)

    kv_own = jnp.concatenate([w_key, w_value], axis=1)
    kv_other = swap(kv_own)

    def gain(own):
        own = own[None]
        return ordered(own, swap(own), 1).astype(f32)

    gain_one, gain_key = gain(attn_pre_gain), gain(key_gain)
    key_w = ordered(kv_own[:, :128], kv_other[:, :128], 1)
    value_w = ordered(kv_own[:, 128:], kv_other[:, 128:], 1)

    normed_one, factor_one = rms_forward(resid_in, gain_one)
    attn_in = normed_one.astype(bf16)
    key_raw = dot_f32(attn_in, key_w)
    value_bf = dot_f32(attn_in, value_w).astype(bf16)
    key_normed, key_factor = rms_forward(key_raw, gain_key)
    key_rot = rotate(key_normed, cos_tab, sin_tab).astype(bf16)
    near = [jnp.concatenate([key_rot, value_bf], axis=1)]
    near.append(across(near[0]))
    near[1], late_blocks = lax.optimization_barrier((near[1], pair_blocks))
    mine_late = lax.dynamic_slice_in_dim(late_blocks, rank, 1, 0)[0]
    tables = piece_tables(late_blocks, mine_late, sign)
    own_a, own_b = gather_middle(near)
    own_a, own_b, cotangent, w_query, w_out, w_gate, w_up, w_down, gains = lax.optimization_barrier(
        (
            own_a,
            own_b,
            cotangent,
            w_query,
            w_out,
            w_gate,
            w_up,
            w_down,
            (query_gain, attn_post_gain, ffw_pre_gain, ffw_post_gain),
        )
    )
    grad_top = to_pairs(cotangent[0])
    gain_query, gain_two, gain_three, gain_four = (gain(g) for g in gains)
    query_w = (w_query, swap(w_query))
    out_w = (w_out, swap(w_out))
    gate_w = (w_gate, swap(w_gate))
    up_w = (w_up, swap(w_up))
    down_w = (w_down, swap(w_down))

    def heads_first(pair):
        return jnp.concatenate(
            [
                part[64 * i : 64 * i + 64, HDIM * h : HDIM * (h + 1)]
                for i in range(2)
                for part in pair
                for h in range(2)
            ],
            axis=0,
        )

    def heads_last(stacked):
        def block(i, p, h):
            start = 64 * (4 * i + 2 * p + h)
            return stacked[start : start + 64]

        return tuple(
            jnp.concatenate(
                [jnp.concatenate([block(i, p, 0), block(i, p, 1)], axis=1) for i in range(2)]
            )
            for p in range(2)
        )

    def tile_heads(table):
        return jnp.concatenate([table[:64]] * HEADS + [table[64:]] * HEADS)

    cos4, sin4 = tile_heads(cos_tab), tile_heads(sin_tab)
    query_raw = heads_first(tuple(dot_f32(attn_in, half) for half in query_w))
    query_normed, query_factor = rms_forward(query_raw, gain_query)
    query_rot = (rotate(query_normed, cos4, sin4)).astype(bf16) * bf16(HDIM**-0.5)
    state = None
    a, b = own_a, own_b
    pieces = []
    for d in range(4):
        pieces.append((a, swap(a), b, swap(b)))
        if d < 3:
            coming = (shift(a, "y", 1), shift(b, "x", 1))
        state = forward_piece(tables[d], query_rot, pieces[d], state)
        if d < 3:
            a, b, state = lax.optimization_barrier((*coming, state))
    attn_a, attn_b, hidden_a, hidden_b, ggate_a, ggate_b, gup_a, gup_b, *rest = middle(
        *state, resid_in, grad_top, gain_two, gain_three, gain_four, *out_w, *gate_w, *up_w, *down_w
    )
    block_output, grad_mid, ffw_in, grad_ffw_bf, grad_proj_bf, grad_heads, stats, *rest = rest
    grad_gain_two, grad_gain_three, grad_gain_four = (g[0] for g in rest)
    attn_out, hidden = (attn_a, attn_b), (hidden_a, hidden_b)
    grad_gate, grad_up = (ggate_a, ggate_b), (gup_a, gup_b)

    def both(own, other):
        return jnp.concatenate([own, swap(other)], axis=0)

    ffw_in_p, grad_ffw_p, grad_proj_p = swap(ffw_in), swap(grad_ffw_bf), swap(grad_proj_bf)
    big = weight_grads(
        attn_out[0],
        swap(attn_out[1]),
        grad_gate[0],
        swap(grad_gate[1]),
        grad_up[0],
        swap(grad_up[1]),
        hidden[0],
        swap(hidden[1]),
        grad_proj_bf,
        grad_proj_p,
        ffw_in,
        ffw_in_p,
        grad_ffw_bf,
        grad_ffw_p,
    )
    attn_in2 = both(attn_in, attn_in)

    stats, big = lax.optimization_barrier((stats, big))
    sum_out, sum_gate, sum_up, sum_down = (g.astype(f32) for g in lax.psum(big, CTX))
    grad_query = None
    moving = None
    for d in (3, 2, 1, 0):
        if d < 3:
            coming = (shift(moving[0], "y", -1), shift(moving[1], "x", -1))
        grad_query, a, a_p, b, b_p = backward_piece(
            tables[d], query_rot, grad_heads, stats, pieces[d], grad_query
        )
        terms = [a.astype(f32) + swap(a_p).astype(f32), b.astype(f32) + swap(b_p).astype(f32)]
        if d < 3:
            terms = [c.astype(f32) + t for c, t in zip(coming, terms)]
        moving = [t.astype(bf16) for t in terms]
        if d:
            *moving, grad_query = tie(*moving, grad_query)
    all_a, all_b = moving
    a, b = all_a[384:], all_b[384:]
    for d in (2, 1, 0):
        rows_d = slice(128 * d, 128 * d + 128)
        a = plus(shift(a, "x", -1), all_a[rows_d])
        b = plus(shift(b, "y", -1), all_b[rows_d])
    grad_query = grad_query * HDIM**-0.5
    grad_query_raw, grad_gain_query = rms_backward(
        query_raw, query_factor, gain_query, rotate_back(grad_query, cos4, sin4)
    )
    grad_query_bf = heads_last(grad_query_raw.astype(bf16))
    grad_w_query = dot_tn(both(grad_query_bf[0], grad_query_bf[1]), attn_in2).astype(bf16)
    mine_query = chunk_sum(grad_w_query.reshape(64, 8, 640)).astype(bf16)
    a, b, mine_query = tie(a, b, mine_query)
    kv_far = jnp.concatenate([a[64:], b[64:]])
    kv_mine = jnp.concatenate([a[:64], b[:64]]).astype(f32) + across(kv_far).astype(f32)
    grad_key_raw, grad_gain_key = rms_backward(
        key_raw, key_factor, gain_key, rotate_back(kv_mine[:, :HDIM], cos_tab, sin_tab)
    )
    grad_key_bf = grad_key_raw.astype(bf16)
    grad_value_bf = kv_mine[:, HDIM:].astype(bf16)

    def mine_other(full):
        a, b = full[:, :128], full[:, 128:]
        return jnp.where(first, a, b), jnp.where(first, b, a)

    key_m, key_o = mine_other(grad_key_bf)
    val_m, val_o = mine_other(grad_value_bf)
    grad_kv2 = both(
        jnp.concatenate([key_m, val_m], axis=1), jnp.concatenate([key_o, val_o], axis=1)
    )
    grad_w_kv = dot_tn(grad_kv2, attn_in2)

    grad_attn_in = (
        dot_nt(grad_query_bf[0], query_w[0])
        + dot_nt(grad_query_bf[1], query_w[1])
        + dot_nt(grad_key_bf, key_w)
        + dot_nt(grad_value_bf, value_w)
    )
    grad_in_part, grad_gain_one = rms_backward(resid_in, factor_one, gain_one, grad_attn_in)
    input_grad = grad_mid + grad_in_part

    gain_grads = (
        grad_gain_one,
        grad_gain_two,
        grad_gain_three,
        grad_gain_four,
        grad_gain_query,
        grad_gain_key,
    )
    g_own = jnp.concatenate([jnp.where(first, g[: g.size // 2], g[g.size // 2 :]) for g in gain_grads])
    g_other = jnp.concatenate([jnp.where(first, g[g.size // 2 :], g[: g.size // 2]) for g in gain_grads])
    g_sum = g_own + swap(g_other[None])[0]
    g_block = jnp.concatenate([g_sum, jnp.zeros((1024,), f32)]).reshape(4, 640).astype(bf16)
    g_block = jnp.concatenate([g_block, jnp.zeros((60, 640), bf16)])
    late = jnp.concatenate([grad_w_kv.astype(bf16).reshape(64, 4, 640), g_block[:, None]], axis=1)
    mine_late = chunk_sum(jnp.pad(late, ((0, 0), (0, 3), (0, 0)))).astype(bf16)
    late = chunk_gather(jnp.concatenate([mine_query, mine_late])).astype(f32)
    sum_query = late[:, :8].reshape(512, 640).T
    sum_kv = late[:, 8:12].reshape(256, 640)
    sum_gains = late[:4, 12].reshape(-1)
    return (
        to_pairs(block_output)[None],
        to_pairs(input_grad)[None],
        sum_query,
        sum_kv[:128].T,
        sum_kv[128:].T,
        sum_out,
        sum_gate,
        sum_up,
        sum_down,
        sum_gains[:320],
        sum_gains[1280:1408],
        sum_gains[1408:1536],
        sum_gains[320:640],
        sum_gains[640:960],
        sum_gains[960:1280],
    )


def solution(mesh):
    grid = Mesh(mesh.devices.reshape(4, 4, 4, 2), ("z", "x", "y", "wsh"))
    tokens = P("wsh", CTX, None)
    cols, rows, vec = P(None, "wsh"), P("wsh", None), P("wsh")
    return jax.shard_map(
        per_device,
        mesh=grid,
        in_specs=(tokens, tokens, P(), cols, cols, cols, rows, cols, cols, rows) + (vec,) * 6,
        out_specs=(tokens, tokens, cols, cols, cols, rows, cols, cols, rows) + (vec,) * 6,
        check_vma=False,
    )
```

```python
import functools

import jax
import jax.numpy as jnp
from jax import lax
from jax.experimental import pallas as pl
from jax.experimental.pallas import tpu as pltpu
from jax.sharding import Mesh
from jax.sharding import PartitionSpec as P

HEADS = 4
HDIM = 256
CTX = ("z", "x", "y")
LOG2E = 1.4426950408889634
GELU_C = 0.7978845608028654

epsilon = 1e-06
theta_base = 1000000.0
bf16 = jnp.bfloat16
f32 = jnp.float32


def rms_forward(values, gain_w):
    factor = lax.rsqrt(jnp.mean(values * values, axis=-1, keepdims=True) + epsilon)
    return (values * factor * (1.0 + gain_w), factor)


def rms_backward(values, factor, gain_w, grad_out):
    weighted = grad_out * (1.0 + gain_w)
    inner = jnp.mean(weighted * values, axis=-1, keepdims=True)
    grad_in = factor * (weighted - values * factor * factor * inner)
    grad_gain = jnp.sum((grad_out * values * factor).reshape(-1, values.shape[-1]), axis=0)
    return (grad_in, grad_gain)


def rotary_tables(positions, width):
    half_width = width // 2
    frequency = theta_base ** (-jnp.arange(half_width, dtype=f32) * 2.0 / width)
    angles = positions.astype(f32)[:, None] * frequency[None, :]
    return (jnp.cos(angles), jnp.sin(angles))


def rotate(values, cos_tab, sin_tab):
    half = values.shape[-1] // 2
    a, b = values[..., :half], values[..., half:]
    return jnp.concatenate([a * cos_tab - b * sin_tab, b * cos_tab + a * sin_tab], axis=-1)


def rotate_back(grads, cos_tab, sin_tab):
    half = grads.shape[-1] // 2
    a, b = grads[..., :half], grads[..., half:]
    return jnp.concatenate([a * cos_tab + b * sin_tab, b * cos_tab - a * sin_tab], axis=-1)


def block_positions(block_ids, half_rows):
    offsets = jnp.arange(half_rows, dtype=jnp.int32)
    return (block_ids[:, None] * half_rows + offsets[None, :]).reshape(-1)


def dot_f32(left, right):
    return jnp.dot(left, right, preferred_element_type=f32)


def dot_nt(left, right):
    return lax.dot_general(left, right, (((1,), (1,)), ((), ())), preferred_element_type=f32)


def dot_tn(left, right):
    return lax.dot_general(left, right, (((0,), (0,)), ((), ())), preferred_element_type=f32)


def swap(values):
    return lax.ppermute(values, "wsh", [(0, 1), (1, 0)])


def load_group(table, group, kv_all):
    slots = [table[8 * group + i] for i in range(8)]
    blocks = [kv_all[pl.ds(pl.multiple_of(slot * 64, 64), 64), :] for slot in slots]
    keys = jnp.concatenate([block[:, :HDIM] for block in blocks], axis=0)
    vals = jnp.concatenate([block[:, HDIM:] for block in blocks], axis=0)
    return slots, keys, vals


def key_places(table, group, shape, dim):
    place = lax.broadcasted_iota(jnp.int32, shape, dim)
    base = jnp.full(shape, table[32 + 8 * group + 7], jnp.int32)
    for i in range(6, -1, -1):
        base = jnp.where(place < 64 * (i + 1), table[32 + 8 * group + i], base)
    return base * 64 + place % 64


def load_piece(piece, kv_all):
    for i, ref in enumerate(piece):
        kv_all[512 * i : 512 * i + 512, :] = ref[...]


def forward_kernel(first, table, q_ref, *rest):
    piece, rest = rest[:4], rest[4:]
    if first:
        acc_ref, tot_ref, kv_all = rest
        acc_ref[...] = jnp.zeros_like(acc_ref)
        tot_ref[...] = jnp.zeros_like(tot_ref)
    else:
        acc_in, tot_in, acc_ref, tot_ref, kv_all = rest
        acc_ref[...] = acc_in[...]
        tot_ref[...] = tot_in[...]
    load_piece(piece, kv_all)

    def step(group, carry):
        _, keys, vals = load_group(table, group, kv_all)
        places = key_places(table, group, (1, 512), 1)

        def half(i):
            rows = pl.ds(pl.multiple_of(table[64 + i] * 256, 256), 256)
            mine = lax.broadcasted_iota(jnp.int32, (256, 1), 0) % 64 + table[66 + i] * 64
            scores = dot_nt(q_ref[rows, :], keys)
            probs = jnp.where(places <= mine, jnp.exp2(scores * LOG2E), 0.0)
            tot_ref[rows, :] += (probs[:, :128] + probs[:, 128:256]) + (
                probs[:, 256:384] + probs[:, 384:]
            )
            acc_ref[rows, :] += dot_f32(probs.astype(bf16), vals)

        half(0)
        pl.when(8 * group < table[69])(lambda: half(1))
        return carry

    lax.fori_loop(0, (table[68] + 7) // 8, step, 0)


def backward_kernel(first, table, q_ref, g_ref, stat_ref, *rest):
    piece, rest = rest[:4], rest[4:]
    if first:
        dq_ref, *out_refs, kv_all, dkv, out_all = rest
        dq_ref[...] = jnp.zeros_like(dq_ref)
    else:
        dq_in, dq_ref, *out_refs, kv_all, dkv, out_all = rest
        dq_ref[...] = dq_in[...]
    load_piece(piece, kv_all)
    out_all[...] = jnp.zeros_like(out_all)

    def step(group, carry):
        slots, keys, vals = load_group(table, group, kv_all)
        places = key_places(table, group, (512, 1), 0)

        def half(i):
            rows = pl.ds(pl.multiple_of(table[64 + i] * 256, 256), 256)
            mine = lax.broadcasted_iota(jnp.int32, (1, 256), 1) % 64 + table[66 + i] * 64
            query, grads = q_ref[rows, :], g_ref[rows, :]
            stat = stat_ref[table[64 + i]]
            scores = dot_nt(keys, query) * LOG2E - stat[0:1, :]
            probs = jnp.where(places <= mine, jnp.exp2(scores), 0.0)
            grad_scores = (probs * (dot_nt(vals, grads) - stat[1:2, :])).astype(bf16)
            dq_ref[rows, :] += dot_tn(grad_scores, keys)
            return dot_f32(grad_scores, query), dot_f32(probs.astype(bf16), grads)

        grad_k, grad_v = half(0)
        dkv[:, :HDIM] = grad_k
        dkv[:, HDIM:] = grad_v

        @pl.when(8 * group < table[69])
        def _():
            more_k, more_v = half(1)
            dkv[:, :HDIM] += more_k
            dkv[:, HDIM:] += more_v

        for i, slot in enumerate(slots):
            block = dkv[64 * i : 64 * i + 64, :].astype(bf16)
            out_all[pl.ds(pl.multiple_of(slot * 64, 64), 64), :] = block
        return carry

    lax.fori_loop(0, (table[68] + 7) // 8, step, 0)
    for i, ref in enumerate(out_refs):
        ref[...] = out_all[512 * i : 512 * i + 512, :]


def specs(count):
    return [pl.BlockSpec(memory_space=pltpu.SMEM)] + [
        pl.BlockSpec(memory_space=pltpu.VMEM) for _ in range(count)
    ]


def forward_piece(table, query, piece, state):
    return pl.pallas_call(
        functools.partial(forward_kernel, state is None),
        out_shape=(
            jax.ShapeDtypeStruct((512, HDIM), f32),
            jax.ShapeDtypeStruct((512, 128), f32),
        ),
        in_specs=specs(5 if state is None else 7),
        out_specs=tuple(specs(2)[1:]),
        scratch_shapes=[pltpu.VMEM((2048, 512), bf16)],
        cost_estimate=pl.CostEstimate(flops=2 * 10**9, transcendentals=0, bytes_accessed=4 * 10**6),
        input_output_aliases={} if state is None else {6: 0, 7: 1},
        name="attn_fwd",
    )(table, query, *piece, *(state or ()))


def backward_piece(table, query, grads, stats, piece, grad_query):
    return pl.pallas_call(
        functools.partial(backward_kernel, grad_query is None),
        out_shape=(jax.ShapeDtypeStruct((512, HDIM), f32),)
        + (jax.ShapeDtypeStruct((512, 512), bf16),) * 4,
        in_specs=specs(7 if grad_query is None else 8),
        out_specs=tuple(specs(5)[1:]),
        scratch_shapes=[
            pltpu.VMEM((2048, 512), bf16),
            pltpu.VMEM((512, 512), f32),
            pltpu.VMEM((2048, 512), bf16),
        ],
        input_output_aliases={} if grad_query is None else {8: 0},
        name="attn_bwd",
    )(table, query, grads, stats, *piece, *(() if grad_query is None else (grad_query,)))


def gelu_pair(v):
    inner = GELU_C * (v + 0.044715 * v * v * v)
    t = jnp.tanh(inner)
    slope = 0.5 * (1.0 + t) + 0.5 * v * (1.0 - t * t) * (GELU_C * (1.0 + 0.134145 * v * v))
    return 0.5 * v * (1.0 + t), slope


def norm_backward(values, factor, gain_w, grad_out):
    weighted = grad_out * (1.0 + gain_w)
    inner = jnp.mean(weighted * values, axis=-1, keepdims=True)
    grad_in = factor * (weighted - values * factor * factor * inner)
    return grad_in, jnp.sum(grad_out * values * factor, axis=0, keepdims=True)


def middle_kernel(*refs):
    acc, tot, resid, grad_top, gain_two, gain_three, gain_four = (r[...] for r in refs[:7])
    out_w, gate_w, up_w, down_w = refs[7:9], refs[9:11], refs[11:13], refs[13:15]
    attn_o, hidden_o, ggate_o, gup_o = refs[15:17], refs[17:19], refs[19:21], refs[21:23]
    block_o, grad_mid_o, ffw_in_o, grad_ffw_o, grad_proj_o, heads_o, stat_o = refs[23:30]
    two_o, three_o, four_o = refs[30:]
    totals = jnp.sum(tot, axis=1, keepdims=True)
    heads = (acc / totals).astype(bf16)

    def block(i, p, h):
        start = 64 * (4 * i + 2 * p + h)
        return heads[start : start + 64]

    attn_proj = jnp.zeros((128, 640), f32)
    for p in range(2):
        part = jnp.concatenate(
            [jnp.concatenate([block(i, p, 0), block(i, p, 1)], axis=1) for i in range(2)], axis=0
        )
        attn_o[p][...] = part
        attn_proj += dot_f32(part, out_w[p][...])
    normed_two, factor_two = rms_forward(attn_proj, gain_two)
    mid = resid + normed_two
    normed_three, factor_three = rms_forward(mid, gain_three)
    ffw_in = normed_three.astype(bf16)
    ffw_in_o[...] = ffw_in
    ffw_proj = jnp.zeros((128, 640), f32)
    for p in range(2):
        act, _ = gelu_pair(dot_f32(ffw_in, gate_w[p][...]))
        hidden = (act * dot_f32(ffw_in, up_w[p][...])).astype(bf16)
        hidden_o[p][...] = hidden
        ffw_proj += dot_f32(hidden, down_w[p][...])
    normed_four, factor_four = rms_forward(ffw_proj, gain_four)
    block_o[...] = mid + normed_four
    grad_ffw, four_o[...] = norm_backward(ffw_proj, factor_four, gain_four, grad_top)
    grad_ffw_bf = grad_ffw.astype(bf16)
    grad_ffw_o[...] = grad_ffw_bf
    grad_ffw_in = jnp.zeros((128, 640), f32)
    for p in range(2):
        act, slope = gelu_pair(dot_f32(ffw_in, gate_w[p][...]))
        up = dot_f32(ffw_in, up_w[p][...])
        grad_hidden = dot_nt(grad_ffw_bf, down_w[p][...])
        grad_gate = (grad_hidden * up * slope).astype(bf16)
        grad_up = (grad_hidden * act).astype(bf16)
        ggate_o[p][...] = grad_gate
        gup_o[p][...] = grad_up
        grad_ffw_in += dot_nt(grad_gate, gate_w[p][...]) + dot_nt(grad_up, up_w[p][...])
    grad_mid_part, three_o[...] = norm_backward(mid, factor_three, gain_three, grad_ffw_in)
    grad_mid = grad_top + grad_mid_part
    grad_mid_o[...] = grad_mid
    grad_proj, two_o[...] = norm_backward(attn_proj, factor_two, gain_two, grad_mid)
    grad_proj_bf = grad_proj.astype(bf16)
    grad_proj_o[...] = grad_proj_bf
    grad_attn = [dot_nt(grad_proj_bf, out_w[p][...]).astype(bf16) for p in range(2)]
    grad_heads = jnp.concatenate(
        [
            grad_attn[p][64 * i : 64 * i + 64, HDIM * h : HDIM * (h + 1)]
            for i in range(2)
            for p in range(2)
            for h in range(2)
        ],
        axis=0,
    )
    heads_o[...] = grad_heads
    delta = jnp.sum(grad_heads.astype(f32) * heads.astype(f32), axis=1, keepdims=True)
    for i, col in enumerate((jnp.log(totals) * LOG2E, delta)):
        row = jnp.broadcast_to(col, (512, 128)).T[0:1]
        stat_o[0, i : i + 1, :] = row[:, :256]
        stat_o[1, i : i + 1, :] = row[:, 256:]


def middle(*values):
    shapes = [((128, 512), bf16)] * 2 + [((128, 1024), bf16)] * 6 + [((128, 640), f32)] * 2
    shapes += [((128, 640), bf16)] * 3 + [((512, HDIM), bf16), ((2, 2, 256), f32)]
    shapes += [((1, 640), f32)] * 3
    return pl.pallas_call(
        middle_kernel,
        out_shape=tuple(jax.ShapeDtypeStruct(*s) for s in shapes),
        in_specs=specs(15)[1:],
        out_specs=tuple(specs(18)[1:]),
        name="middle",
    )(*values)


def weight_kernel(*refs):
    pairs = [(refs[2 * i][...], refs[2 * i + 1][...]) for i in range(7)]
    act, gate, up, hidden, proj, ffw_in, ffw = (jnp.concatenate(p, axis=0) for p in pairs)
    out_ref, gate_ref, up_ref, down_ref = refs[14:]
    out_ref[...] = dot_tn(act, proj).astype(bf16)
    gate_ref[...] = dot_tn(ffw_in, gate).astype(bf16)
    up_ref[...] = dot_tn(ffw_in, up).astype(bf16)
    down_ref[...] = dot_tn(hidden, ffw).astype(bf16)


def weight_grads(*pairs):
    return pl.pallas_call(
        weight_kernel,
        out_shape=(
            jax.ShapeDtypeStruct((512, 640), bf16),
            jax.ShapeDtypeStruct((640, 1024), bf16),
            jax.ShapeDtypeStruct((640, 1024), bf16),
            jax.ShapeDtypeStruct((1024, 640), bf16),
        ),
        in_specs=specs(14)[1:],
        out_specs=tuple(specs(4)[1:]),
        name="weight_grads",
    )(*pairs)


def shift(values, axis, by):
    perm = [
        (2 * a + w, 2 * ((a + (by if w == 0 else -by)) % 4) + w) for a in range(4) for w in range(2)
    ]
    return lax.ppermute(values, (axis, "wsh"), perm)


def ring_gather(block, axis):
    out = [block]
    for _ in range(3):
        out.append(shift(out[-1], axis, 1))
    return out


def ring_sum(parts, axis):
    moving = parts[3]
    for d in (2, 1, 0):
        moving = (shift(moving, axis, -1).astype(f32) + parts[d].astype(f32)).astype(bf16)
    return moving


def direct_gather(block, axis):
    return [block] + [shift(block, axis, d) for d in (1, 2, 3)]


def direct_sum(parts, axis):
    got = [shift(parts[d], axis, -d) for d in (1, 2, 3)]
    return sum((g.astype(f32) for g in got), parts[0].astype(f32))


def to_pairs(values):
    perm = [
        (2 * z + w, 2 * z + w) if w == z % 2 else (2 * z + w, 2 * (z ^ 1) + 1 - w)
        for z in range(4)
        for w in range(2)
    ]
    return lax.ppermute(values, ("z", "wsh"), perm)


def across(values):
    perm = [(2 * z + w, 2 * ((z + 2) % 4) + w) for z in range(4) for w in range(2)]
    return lax.ppermute(values, ("z", "wsh"), perm)


def gather_middle(near):
    a = ring_gather(jnp.concatenate([x[:64] for x in near]), "x")
    b = ring_gather(jnp.concatenate([x[64:] for x in near]), "y")
    return jnp.concatenate(a), jnp.concatenate(b)


def tie(*values):
    return lax.optimization_barrier(values)


def plus(left, right):
    return (left.astype(f32) + right.astype(f32)).astype(bf16)


def piece_tables(pair_blocks, mine, sign):
    z, x, y = (lax.axis_index(name) for name in CTX)
    i = jnp.arange(128, dtype=jnp.int32)
    piece, inside = i // 32, i % 32
    color, part = inside // 16, (inside % 16) // 8
    outer, inner = (inside % 8) // 2, inside % 2
    core = (1 - sign) // 2
    sign = jnp.where(part == 0, sign, -sign)
    at_z = 2 * ((z // 2 + inner) % 2) + jnp.where(part == 0, core, 1 - core)
    at_x = (x - sign * jnp.where(color == 0, outer, piece)) % 4
    at_y = (y - sign * jnp.where(color == 0, piece, outer)) % 4
    source = 2 * (at_z * 16 + at_x * 4 + at_y) + color
    flat = pair_blocks.reshape(1, 128)
    hit = source[:, None] == jnp.arange(128, dtype=jnp.int32)[None]
    ids = jnp.sum(jnp.where(hit, flat, 0), axis=1).reshape(4, 32)
    rank = jnp.sum((ids[:, None, :] < ids[:, :, None]).astype(jnp.int32), axis=2)
    at = rank[:, None, :] == jnp.arange(32, dtype=jnp.int32)[None, :, None]
    slots = jnp.sum(jnp.where(at, jnp.arange(32, dtype=jnp.int32)[None, None], 0), axis=2)
    sorted_ids = jnp.sum(jnp.where(at, ids[:, None, :], 0), axis=2)
    seen = jnp.sum((ids[:, None, :] <= mine[None, :, None]).astype(jnp.int32), axis=2)
    upper = (mine[1] > mine[0]).astype(jnp.int32)
    which = jnp.stack([upper, 1 - upper])
    own = jnp.stack([jnp.max(mine), jnp.min(mine)])
    fixed = jnp.broadcast_to(jnp.concatenate([which, own])[None], (4, 4))
    seen = jnp.stack([jnp.max(seen, axis=1), jnp.min(seen, axis=1)], axis=1)
    return jnp.concatenate([slots, sorted_ids, fixed, seen], axis=1)


def chunk_sum(values):
    got = lax.all_to_all(values, CTX, split_axis=0, concat_axis=0, tiled=True)
    return jnp.sum(got.astype(f32), axis=0)


def chunk_gather(values):
    wide = jnp.broadcast_to(values[None], (64,) + values.shape)
    return lax.all_to_all(wide, CTX, split_axis=0, concat_axis=0, tiled=True)


def per_device(
    block_input,
    cotangent,
    pair_blocks,
    w_query,
    w_key,
    w_value,
    w_out,
    w_gate,
    w_up,
    w_down,
    attn_pre_gain,
    query_gain,
    key_gain,
    attn_post_gain,
    ffw_pre_gain,
    ffw_post_gain,
):
    rows = block_input.shape[1]
    core = lax.axis_index("wsh")
    first = core == 0
    rank = 32 * (lax.axis_index("z") // 2) + 16 * core
    rank = rank + 4 * lax.axis_index("x") + lax.axis_index("y")

    def ordered(own, other, axis):
        return jnp.where(
            first,
            jnp.concatenate([own, other], axis=axis),
            jnp.concatenate([other, own], axis=axis),
        )

    resid_in = to_pairs(block_input[0]).astype(f32)
    my_blocks = lax.dynamic_slice_in_dim(pair_blocks, rank, 1, 0)[0]
    query_pos = block_positions(my_blocks, rows // 2)
    sign = jnp.where(first, 1, -1)
    cos_tab, sin_tab = rotary_tables(query_pos, HDIM)

    kv_own = jnp.concatenate([w_key, w_value], axis=1)
    kv_other = swap(kv_own)

    def gain(own):
        own = own[None]
        return ordered(own, swap(own), 1).astype(f32)

    gain_one, gain_key = gain(attn_pre_gain), gain(key_gain)
    key_w = ordered(kv_own[:, :128], kv_other[:, :128], 1)
    value_w = ordered(kv_own[:, 128:], kv_other[:, 128:], 1)

    normed_one, factor_one = rms_forward(resid_in, gain_one)
    attn_in = normed_one.astype(bf16)
    key_raw = dot_f32(attn_in, key_w)
    value_bf = dot_f32(attn_in, value_w).astype(bf16)
    key_normed, key_factor = rms_forward(key_raw, gain_key)
    key_rot = rotate(key_normed, cos_tab, sin_tab).astype(bf16)
    near = [jnp.concatenate([key_rot, value_bf], axis=1)]
    near.append(across(near[0]))
    near[1], late_blocks = lax.optimization_barrier((near[1], pair_blocks))
    mine_late = lax.dynamic_slice_in_dim(late_blocks, rank, 1, 0)[0]
    tables = piece_tables(late_blocks, mine_late, sign)
    own_a, own_b = gather_middle(near)
    own_a, own_b, cotangent, w_query, w_out, w_gate, w_up, w_down, gains = lax.optimization_barrier(
        (
            own_a,
            own_b,
            cotangent,
            w_query,
            w_out,
            w_gate,
            w_up,
            w_down,
            (query_gain, attn_post_gain, ffw_pre_gain, ffw_post_gain),
        )
    )
    grad_top = to_pairs(cotangent[0])
    gain_query, gain_two, gain_three, gain_four = (gain(g) for g in gains)
    query_w = (w_query, swap(w_query))
    out_w = (w_out, swap(w_out))
    gate_w = (w_gate, swap(w_gate))
    up_w = (w_up, swap(w_up))
    down_w = (w_down, swap(w_down))

    def heads_first(pair):
        return jnp.concatenate(
            [
                part[64 * i : 64 * i + 64, HDIM * h : HDIM * (h + 1)]
                for i in range(2)
                for part in pair
                for h in range(2)
            ],
            axis=0,
        )

    def heads_last(stacked):
        def block(i, p, h):
            start = 64 * (4 * i + 2 * p + h)
            return stacked[start : start + 64]

        return tuple(
            jnp.concatenate(
                [jnp.concatenate([block(i, p, 0), block(i, p, 1)], axis=1) for i in range(2)]
            )
            for p in range(2)
        )

    def tile_heads(table):
        return jnp.concatenate([table[:64]] * HEADS + [table[64:]] * HEADS)

    cos4, sin4 = tile_heads(cos_tab), tile_heads(sin_tab)
    query_raw = heads_first(tuple(dot_f32(attn_in, half) for half in query_w))
    query_normed, query_factor = rms_forward(query_raw, gain_query)
    query_rot = (rotate(query_normed, cos4, sin4)).astype(bf16) * bf16(HDIM**-0.5)
    state = None
    a, b = own_a, own_b
    pieces = []
    for d in range(4):
        pieces.append((a, swap(a), b, swap(b)))
        if d < 3:
            coming = (shift(a, "y", 1), shift(b, "x", 1))
        state = forward_piece(tables[d], query_rot, pieces[d], state)
        if d < 3:
            a, b, state = lax.optimization_barrier((*coming, state))
        if d == 1:
            a, b, grad_top, gain_two, gain_three, gain_four = tie(
                a, b, grad_top, gain_two, gain_three, gain_four
            )
    attn_a, attn_b, hidden_a, hidden_b, ggate_a, ggate_b, gup_a, gup_b, *rest = middle(
        *state, resid_in, grad_top, gain_two, gain_three, gain_four, *out_w, *gate_w, *up_w, *down_w
    )
    block_output, grad_mid, ffw_in, grad_ffw_bf, grad_proj_bf, grad_heads, stats, *rest = rest
    grad_gain_two, grad_gain_three, grad_gain_four = (g[0] for g in rest)
    attn_out, hidden = (attn_a, attn_b), (hidden_a, hidden_b)
    grad_gate, grad_up = (ggate_a, ggate_b), (gup_a, gup_b)

    def both(own, other):
        return jnp.concatenate([own, swap(other)], axis=0)

    ffw_in_p, grad_ffw_p, grad_proj_p = swap(ffw_in), swap(grad_ffw_bf), swap(grad_proj_bf)
    big = weight_grads(
        attn_out[0],
        swap(attn_out[1]),
        grad_gate[0],
        swap(grad_gate[1]),
        grad_up[0],
        swap(grad_up[1]),
        hidden[0],
        swap(hidden[1]),
        grad_proj_bf,
        grad_proj_p,
        ffw_in,
        ffw_in_p,
        grad_ffw_bf,
        grad_ffw_p,
    )
    attn_in2 = both(attn_in, attn_in)

    stats, big = lax.optimization_barrier((stats, big))
    sum_out, sum_gate, sum_up, sum_down = (g.astype(f32) for g in lax.psum(big, CTX))
    grad_query = None
    moving = None
    for d in (3, 2, 1, 0):
        if d < 3:
            coming = (shift(moving[0], "y", -1), shift(moving[1], "x", -1))
        grad_query, a, a_p, b, b_p = backward_piece(
            tables[d], query_rot, grad_heads, stats, pieces[d], grad_query
        )
        terms = [a.astype(f32) + swap(a_p).astype(f32), b.astype(f32) + swap(b_p).astype(f32)]
        if d < 3:
            terms = [c.astype(f32) + t for c, t in zip(coming, terms)]
        moving = [t.astype(bf16) for t in terms]
        if d:
            *moving, grad_query = tie(*moving, grad_query)
    all_a, all_b = moving
    a, b = all_a[384:], all_b[384:]
    for d in (2, 1, 0):
        rows_d = slice(128 * d, 128 * d + 128)
        a = plus(shift(a, "x", -1), all_a[rows_d])
        b = plus(shift(b, "y", -1), all_b[rows_d])
    grad_query = grad_query * HDIM**-0.5
    grad_query_raw, grad_gain_query = rms_backward(
        query_raw, query_factor, gain_query, rotate_back(grad_query, cos4, sin4)
    )
    grad_query_bf = heads_last(grad_query_raw.astype(bf16))
    grad_w_query = dot_tn(both(grad_query_bf[0], grad_query_bf[1]), attn_in2).astype(bf16)
    mine_query = chunk_sum(grad_w_query.reshape(64, 8, 640)).astype(bf16)
    a, b, mine_query = tie(a, b, mine_query)
    kv_far = jnp.concatenate([a[64:], b[64:]])
    kv_mine = jnp.concatenate([a[:64], b[:64]]).astype(f32) + across(kv_far).astype(f32)
    grad_key_raw, grad_gain_key = rms_backward(
        key_raw, key_factor, gain_key, rotate_back(kv_mine[:, :HDIM], cos_tab, sin_tab)
    )
    grad_key_bf = grad_key_raw.astype(bf16)
    grad_value_bf = kv_mine[:, HDIM:].astype(bf16)

    def mine_other(full):
        a, b = full[:, :128], full[:, 128:]
        return jnp.where(first, a, b), jnp.where(first, b, a)

    key_m, key_o = mine_other(grad_key_bf)
    val_m, val_o = mine_other(grad_value_bf)
    grad_kv2 = both(
        jnp.concatenate([key_m, val_m], axis=1), jnp.concatenate([key_o, val_o], axis=1)
    )
    grad_w_kv = dot_tn(grad_kv2, attn_in2)

    grad_attn_in = (
        dot_nt(grad_query_bf[0], query_w[0])
        + dot_nt(grad_query_bf[1], query_w[1])
        + dot_nt(grad_key_bf, key_w)
        + dot_nt(grad_value_bf, value_w)
    )
    grad_in_part, grad_gain_one = rms_backward(resid_in, factor_one, gain_one, grad_attn_in)
    input_grad = grad_mid + grad_in_part

    gain_grads = (
        grad_gain_one,
        grad_gain_two,
        grad_gain_three,
        grad_gain_four,
        grad_gain_query,
        grad_gain_key,
    )
    g_own = jnp.concatenate([jnp.where(first, g[: g.size // 2], g[g.size // 2 :]) for g in gain_grads])
    g_other = jnp.concatenate([jnp.where(first, g[g.size // 2 :], g[: g.size // 2]) for g in gain_grads])
    g_sum = g_own + swap(g_other[None])[0]
    g_block = jnp.concatenate([g_sum, jnp.zeros((1024,), f32)]).reshape(4, 640).astype(bf16)
    g_block = jnp.concatenate([g_block, jnp.zeros((60, 640), bf16)])
    late = jnp.concatenate([grad_w_kv.astype(bf16).reshape(64, 4, 640), g_block[:, None]], axis=1)
    mine_late = chunk_sum(jnp.pad(late, ((0, 0), (0, 3), (0, 0)))).astype(bf16)
    late = chunk_gather(jnp.concatenate([mine_query, mine_late])).astype(f32)
    sum_query = late[:, :8].reshape(512, 640).T
    sum_kv = late[:, 8:12].reshape(256, 640)
    sum_gains = late[:4, 12].reshape(-1)
    return (
        to_pairs(block_output)[None],
        to_pairs(input_grad)[None],
        sum_query,
        sum_kv[:128].T,
        sum_kv[128:].T,
        sum_out,
        sum_gate,
        sum_up,
        sum_down,
        sum_gains[:320],
        sum_gains[1280:1408],
        sum_gains[1408:1536],
        sum_gains[320:640],
        sum_gains[640:960],
        sum_gains[960:1280],
    )


def solution(mesh):
    grid = Mesh(mesh.devices.reshape(4, 4, 4, 2), ("z", "x", "y", "wsh"))
    tokens = P("wsh", CTX, None)
    cols, rows, vec = P(None, "wsh"), P("wsh", None), P("wsh")
    return jax.shard_map(
        per_device,
        mesh=grid,
        in_specs=(tokens, tokens, P(), cols, cols, cols, rows, cols, cols, rows) + (vec,) * 6,
        out_specs=(tokens, tokens, cols, cols, cols, rows, cols, cols, rows) + (vec,) * 6,
        check_vma=False,
    )
```
